32 devices in a mesh: dp: 8 (over z, x), mp: 4 (over y, core).
Axes of the slice: x: 2, y: 2, z: 4, core: 2. Of those that a mesh axis runs over, the one named last changes fastest.
Arguments:
- patches: bfloat16 [32000, 768], P(('dp', 'mp')), may hold values from -6 to 6
- dataset_id: int32 [160], P('dp'), may hold values from 0 to 7
- patch_masks: int32 [8, 200], replicated, may hold values 0 or 1
- mask_tokens: bfloat16 [8, 768], replicated, may hold values from -6 to 6
- key_mask: int32 [160, 200], P('dp'), may hold values from 0 to 1, as said below
- bias_index: int32 [200, 200], replicated, may hold values from 0 to 731
- norm1_gain: float32 [768], replicated, may hold values from 0.5 to 1.5
- norm1_shift: float32 [768], replicated, may hold values from -1.8 to 1.8
- qkv_weight: bfloat16 [768, 3, 768], P(None, None, 'mp'), may hold values from -0.21875 to 0.21875
- query_bias: bfloat16 [768], P('mp'), may hold values from -3 to 3
- value_bias: bfloat16 [768], P('mp'), may hold values from -3 to 3
- bias_table: bfloat16 [732, 12], P(None, 'mp'), may hold values from -5 to 5
- out_weight: bfloat16 [768, 768], P('mp'), may hold values from -1.75 to 1.75
- out_bias: float32 [768], replicated, may hold values from -1.8 to 1.8
- gamma_attn: float32 [768], replicated, may hold values from 0.5 to 2
- norm2_gain: float32 [768], replicated, may hold values from 0.5 to 1.5
- norm2_shift: float32 [768], replicated, may hold values from -1.8 to 1.8
- up_weight: bfloat16 [768, 3072], P(None, 'mp'), may hold values from -0.21875 to 0.21875
- up_bias: bfloat16 [3072], P('mp'), may hold values from -3 to 3
- down_weight: bfloat16 [3072, 768], P('mp'), may hold values from -0.109375 to 0.109375
- down_bias: float32 [768], replicated, may hold values from -1.8 to 1.8
- gamma_mlp: float32 [768], replicated, may hold values from 0.5 to 2
- cotangent: bfloat16 [32000, 768], P(('dp', 'mp')), may hold values from -6 to 6
Outputs:
- output: bfloat16 [32000, 768], P(('dp', 'mp'))
- patch_grad: float32 [32000, 768], P(('dp', 'mp'))
- token_grad: float32 [8, 768], replicated
- norm1_gain_grad: float32 [768], replicated
- norm1_shift_grad: float32 [768], replicated
- qkv_grad: float32 [768, 3, 768], P(None, None, 'mp')
- query_bias_grad: float32 [768], P('mp')
- value_bias_grad: float32 [768], P('mp')
- table_grad: float32 [732, 12], P(None, 'mp')
- out_weight_grad: float32 [768, 768], P('mp')
- out_bias_grad: float32 [768], replicated
- gamma_attn_grad: float32 [768], replicated
- norm2_gain_grad: float32 [768], replicated
- norm2_shift_grad: float32 [768], replicated
- up_weight_grad: float32 [768, 3072], P(None, 'mp')
- up_bias_grad: float32 [3072], P('mp')
- down_weight_grad: float32 [3072, 768], P('mp')
- down_bias_grad: float32 [768], replicated
- gamma_mlp_grad: float32 [768], replicated
The draws below stay inside these ranges and needn't reach their ends.
Inputs may be any that keep to these rules, and one draw needn't show every extreme that they name: `key_mask`: each row holds ones on a prefix of its positions and zeros after it; the first position is always one.
All inputs are finite; a program needn't handle non-finite values.
Results may differ from the reference program's by a relative error of at most 0.013.
The reference program's roundings to bfloat16 on the way count: a program that leaves them out, or rounds other values in their place, can miss the bound.
Values may be sent and summed in bfloat16 or wider, within the bound.
No kernel may reach another device: no remote copies, remote signals or barrier semaphores. Data moves between devices by JAX's collectives and lax.ppermute only.
A program may use at most 192 MiB of HBM per device.

```python
import math
import jax
import jax.numpy as jnp
from jax import lax

D = 768
HEADS = 12
HEAD = 64
FF = 3072
REL = 732
SEQ = 200
GROUPS = 8
IMG_DEV = 20
IMAGES = 160
ROWS = 32000


def draw_key_mask(key, part):
    lengths = jax.random.randint(key, (IMAGES, 1), SEQ // 3, SEQ + 1)
    positions = jnp.arange(SEQ)[None, :]
    return (positions < lengths).astype(jnp.int32)


def plant(values, stream_key, smallest, high):
    longest = values.shape.index(max(values.shape))
    spots = []
    for shift in (0, 1):
        where = [jax.random.randint(jax.random.fold_in(stream_key, axis), (), 0, length) for axis, length in enumerate(values.shape)]
        where[longest] = (where[longest] + shift) % values.shape[longest]
        spots.append(tuple(where))
    return values.at[spots[0]].set(smallest).at[spots[1]].set(high)


def shard_levels(key, dims, split, least, largest):
    level = 1.0
    for position, blocks in split:
        steps = jax.random.uniform(jax.random.fold_in(jax.random.fold_in(key, 6), position), (blocks,), jnp.float32, least / len(split), largest / len(split))
        level = level * jnp.repeat(jnp.exp(steps), dims[position] // blocks).reshape((-1,) + (1,) * (len(dims) - 1 - position))
    return level


def bell_draw(stream_key, dims, width, bound, cuts=(), held_as=jnp.bfloat16):
    values = jax.random.normal(stream_key, dims, jnp.float32) * width
    if len(cuts) > 0:
        values = shard_levels(stream_key, dims, cuts, -0.22, 0.18) * values
    return jnp.clip(values, min=-bound, max=bound).astype(held_as)


def setup_inputs(seed: int = 0) -> dict:
    key_of = jax.random.split(jax.random.key(seed), 24)
    return {
        "patches": bell_draw(key_of[0], (ROWS, D), 1.0, 6.0, ((0, 32),)),
        "dataset_id": plant(jax.random.randint(key_of[1], (IMAGES,), 0, GROUPS), jax.random.fold_in(key_of[1], 1), 0, GROUPS - 1).astype(jnp.int32),
        "patch_masks": plant((jax.random.randint(key_of[2], (GROUPS, SEQ), 0, 5) < 2).astype(jnp.int32), jax.random.fold_in(key_of[2], 1), 0, 1),
        "mask_tokens": bell_draw(key_of[3], (GROUPS, D), 1.0, 6.0),
        "key_mask": draw_key_mask(jax.random.fold_in(key_of[23], 71), 0),
        "bias_index": plant(jax.random.randint(key_of[5], (SEQ, SEQ), 0, REL), jax.random.fold_in(key_of[5], 1), 0, REL - 1).astype(jnp.int32),
        "norm1_gain": jnp.clip(1.0 + 0.1 * jax.random.normal(key_of[6], (D,), jnp.float32), 0.5, 1.5),
        "norm1_shift": bell_draw(key_of[7], (D,), 0.3, 1.8, (), jnp.float32),
        "qkv_weight": bell_draw(key_of[8], (D, 3, D), D ** -0.5, 0.21875, ((2, 4),)),
        "query_bias": bell_draw(key_of[9], (D,), 0.5, 3.0, ((0, 4),)),
        "value_bias": bell_draw(key_of[10], (D,), 0.5, 3.0, ((0, 4),)),
        "bias_table": bell_draw(key_of[11], (REL, HEADS), 1.0, 5.0, ((1, 4),)),
        "out_weight": bell_draw(key_of[12], (D, D), (max(D // 64, 4)) ** -0.5, 1.75, ((0, 4),)),
        "out_bias": bell_draw(key_of[13], (D,), 0.3, 1.8, (), jnp.float32),
        "gamma_attn": jnp.clip(jnp.exp(jax.random.uniform(key_of[14], (D,), jnp.float32, math.log(0.5), math.log(2.0))), 0.5, 2.0),
        "norm2_gain": jnp.clip(1.0 + 0.1 * jax.random.normal(key_of[15], (D,), jnp.float32), 0.5, 1.5),
        "norm2_shift": bell_draw(key_of[16], (D,), 0.3, 1.8, (), jnp.float32),
        "up_weight": bell_draw(key_of[17], (D, FF), D ** -0.5, 0.21875, ((1, 4),)),
        "up_bias": bell_draw(key_of[18], (FF,), 0.5, 3.0, ((0, 4),)),
        "down_weight": bell_draw(key_of[19], (FF, D), FF ** -0.5, 0.109375, ((0, 4),)),
        "down_bias": bell_draw(key_of[20], (D,), 0.3, 1.8, (), jnp.float32),
        "gamma_mlp": jnp.clip(jnp.exp(jax.random.uniform(key_of[21], (D,), jnp.float32, math.log(0.5), math.log(2.0))), 0.5, 2.0),
        "cotangent": bell_draw(key_of[22], (ROWS, D), 1.0, 6.0, ((0, 32),)),
    }


@jax.custom_vjp
def low(v):
    return lax.optimization_barrier(v.astype(jnp.bfloat16)).astype(jnp.float32)

@jax.custom_vjp
def low_back(v):
    return v

def low_keep(v):
    return (low(v), None)

def low_pass(kept, grad):
    return (grad,)

def back_keep(v):
    return (v, None)

def back_low(kept, grad):
    return (low(grad),)
low.defvjp(low_keep, low_pass)
low_back.defvjp(back_keep, back_low)

def rounded_both(values):
    return low(low_back(values))

def matmul(left, right):
    return jnp.dot(left, right, precision=lax.Precision.HIGHEST, preferred_element_type=jnp.float32)

def layer_norm(values, gain, shift):
    mean = lax.optimization_barrier(jnp.mean(values, axis=-1, keepdims=True))
    centred = values - mean
    spread = lax.optimization_barrier(jnp.mean(centred * centred, axis=-1, keepdims=True))
    return centred * lax.rsqrt(spread + 1e-06) * gain + shift

def block_forward(weights, block_patches, tokens, ids, masks, patch_masks, bias_index):
    norm1_gain, norm1_shift, qkv_weight, query_bias, value_bias, bias_table, out_weight, out_bias, gamma_attn, norm2_gain, norm2_shift, up_weight, up_bias, down_weight, down_bias, gamma_mlp = weights
    count = ids.shape[0]
    choose = (ids[:, None] == jnp.arange(GROUPS)[None, :]).astype(jnp.float32)
    selected = matmul(choose, patch_masks.astype(jnp.float32)).reshape(count * SEQ, 1)
    token_rows = jnp.repeat(matmul(choose, tokens), SEQ, axis=0)
    start = block_patches * (1.0 - selected) + selected * token_rows
    normed1 = low(layer_norm(start, norm1_gain, norm1_shift))
    joint = matmul(normed1, qkv_weight.reshape(D, 3 * D))
    scale = HEAD ** (-0.5)
    shape4 = (count, SEQ, HEADS, HEAD)
    queries = rounded_both((joint[:, :D] + query_bias) * scale).reshape(shape4)
    keys = rounded_both(joint[:, D:2 * D]).reshape(shape4)
    values = rounded_both(joint[:, 2 * D:] + value_bias).reshape(shape4)
    bias = jnp.transpose(bias_table[bias_index], (2, 0, 1))
    scores = jnp.einsum('bqhe,bkhe->bhqk', queries, keys, precision=lax.Precision.HIGHEST) + bias[None]
    scores = low_back(scores)
    scores = jnp.where(masks[:, None, None, :] > 0, scores, -1e+30)
    probs = low(jnp.exp(scores - jax.nn.logsumexp(scores, axis=-1, keepdims=True)))
    context = jnp.einsum('bhqk,bkhe->bqhe', probs, values, precision=lax.Precision.HIGHEST)
    context = rounded_both(context.reshape(count * SEQ, D))
    attn_value = low_back(matmul(context, out_weight) + out_bias)
    middle = start + gamma_attn * attn_value
    normed2 = low(layer_norm(middle, norm2_gain, norm2_shift))
    hidden_pre = low_back(matmul(normed2, up_weight) + up_bias)
    hidden = low(jax.nn.gelu(hidden_pre, approximate=False))
    mlp_value = low_back(matmul(hidden, down_weight) + down_bias)
    return middle + gamma_mlp * mlp_value

def add_pair(first, second):
    return first + second

def reference(patches, dataset_id, patch_masks, mask_tokens, key_mask, bias_index, norm1_gain, norm1_shift, qkv_weight, query_bias, value_bias, bias_table, out_weight, out_bias, gamma_attn, norm2_gain, norm2_shift, up_weight, up_bias, down_weight, down_bias, gamma_mlp, cotangent):
    weights = tuple((item.astype(jnp.float32) for item in (norm1_gain, norm1_shift, qkv_weight, query_bias, value_bias, bias_table, out_weight, out_bias, gamma_attn, norm2_gain, norm2_shift, up_weight, up_bias, down_weight, down_bias, gamma_mlp)))
    tokens = mask_tokens.astype(jnp.float32)
    blocks = IMAGES // IMG_DEV
    inputs = (patches.astype(jnp.float32).reshape(blocks, IMG_DEV * SEQ, D), cotangent.astype(jnp.float32).reshape(blocks, IMG_DEV * SEQ, D), dataset_id.reshape(blocks, IMG_DEV), key_mask.reshape(blocks, IMG_DEV, SEQ))

    def step(totals, pieces):
        block_patches, block_grad, ids, masks = pieces

        def run(weights_in, patches_in, tokens_in):
            return block_forward(weights_in, patches_in, tokens_in, ids, masks, patch_masks, bias_index)
        result, pull = jax.vjp(run, weights, block_patches, tokens)
        grad_weights, grad_patches, grad_tokens = pull(block_grad)
        totals = jax.tree.map(add_pair, totals, (grad_weights, grad_tokens))
        return (totals, (result.astype(jnp.bfloat16), grad_patches))
    zeros = jax.tree.map(jnp.zeros_like, (weights, tokens))
    (grads, token_grad), (outputs, patch_grads) = lax.scan(step, zeros, inputs)
    output = outputs.reshape(ROWS, D)
    patch_grad = patch_grads.reshape(ROWS, D)
    return (output, patch_grad, token_grad, grads[0], grads[1], grads[2], grads[3], grads[4], grads[5], grads[6], grads[7], grads[8], grads[9], grads[10], grads[11], grads[12], grads[13], grads[14], grads[15])
```

```python
import functools

import jax
import jax.numpy as jnp
from jax import lax
from jax.experimental import pallas as pl
from jax.experimental.pallas import tpu as pltpu
from jax.sharding import PartitionSpec as P

HEAD = 64
SEQ = 200
GROUPS = 8
LANES = 128
BF = jnp.bfloat16
F32 = jnp.float32
VMEM_LIMIT = 56 << 20


def dot_nn(left, right):
    return lax.dot_general(left, right, (((1,), (0,)), ((), ())), preferred_element_type=F32)


def dot_nt(left, right):
    return lax.dot_general(left, right, (((1,), (1,)), ((), ())), preferred_element_type=F32)


def dot_tn(left, right):
    return lax.dot_general(left, right, (((0,), (0,)), ((), ())), preferred_element_type=F32)


def params(steps=1):
    return pltpu.CompilerParams(
        dimension_semantics=("arbitrary",) * steps, vmem_limit_bytes=VMEM_LIMIT
    )


def cost(micros):
    return pl.CostEstimate(flops=int(micros * 1.1e8), transcendentals=0, bytes_accessed=0)


def whole(shape, at=0):
    zeros = (0,) * (len(shape) - 1)
    return pl.BlockSpec(shape, lambda *_: (at,) + zeros, pipeline_mode=pl.Buffered(1))


def image_spec(width):
    return pl.BlockSpec((1, SEQ, width), lambda i, *_: (i, 0, 0))


def resident(shape):
    zeros = (0,) * len(shape)
    return pl.BlockSpec(shape, lambda *_: zeros)


def shaped(shape, dtype):
    return jax.ShapeDtypeStruct(shape, dtype)


TILE = 40


def normalise(values):
    mean = jnp.mean(values, axis=-1, keepdims=True)
    centred = values - mean
    spread = jnp.mean(centred * centred, axis=-1, keepdims=True)
    scale = lax.rsqrt(spread + 1e-06)
    return centred * scale, scale


def normalise_back(grad, gain, xhat, scale):
    u = grad * gain
    return (
        u - jnp.mean(u, axis=-1, keepdims=True) - xhat * jnp.mean(u * xhat, axis=-1, keepdims=True)
    ) * scale


def line(ref):
    return ref[...].reshape(1, -1)


def token_line(ids_ref, token_ref):
    tokens = token_ref[...].astype(F32)
    group = lax.broadcasted_iota(jnp.int32, tokens.shape, 0)
    return jnp.sum(jnp.where(group == ids_ref[pl.program_id(0)], tokens, 0.0), axis=0, keepdims=True)


def mixed(patch_ref, sel_ref, token, at):
    sel = sel_ref[0, at : at + TILE, :]
    return patch_ref[0, at : at + TILE, :].astype(F32) * (1.0 - sel) + sel * token, sel


def tiles():
    return range(0, SEQ, TILE)


def fold(values):
    return jnp.sum(values.reshape(values.shape[0] // 8, 8, values.shape[1]), axis=0)


SMALL_ROWS = 16


def prepare_kernel(
    side_ref, qkv_ref, out_ref, down_ref, qb_ref, vb_ref, upb_ref, table_ref,
    small_ref, attn_ref, half_ref,
):
    own = qb_ref.shape[0]
    width = small_ref.shape[1]
    small_ref[...] = jnp.zeros_like(small_ref)
    small_ref[0:1, :own] = line(qb_ref)
    small_ref[0:1, 2 * own : 3 * own] = line(vb_ref)
    small_ref[1:2, : upb_ref.shape[0]] = line(upb_ref)
    small_ref[2 : 2 + table_ref.shape[0], : table_ref.shape[1]] = table_ref[...]
    attn_ref[2 * own :, :] = small_ref[...]

    @pl.when(side_ref[0] == 0)
    def _():
        attn_ref[: 2 * own, :] = qkv_ref[: 2 * own, :]
        half_ref[...] = down_ref[:, : width // 2]

    @pl.when(side_ref[0] == 1)
    def _():
        attn_ref[:own, :] = qkv_ref[2 * own :, :]
        attn_ref[own : 2 * own, :] = out_ref[...]
        half_ref[...] = down_ref[:, width // 2 :]


def prepare(side, qkv, out, down, qb, vb, upb, table):
    width = out.shape[1]
    vmem = pl.BlockSpec(memory_space=pltpu.VMEM)
    return pl.pallas_call(
        prepare_kernel,
        out_shape=[
            shaped((SMALL_ROWS, width), BF),
            shaped((2 * qb.shape[0] + SMALL_ROWS, width), BF),
            shaped((down.shape[0], width // 2), BF),
        ],
        in_specs=[pl.BlockSpec(memory_space=pltpu.SMEM)] + [vmem] * 7,
        out_specs=[vmem] * 3,
        compiler_params=pltpu.CompilerParams(vmem_limit_bytes=VMEM_LIMIT),
        cost_estimate=cost(2),
        name="prepare",
    )(side, qkv, out, down, qb, vb, upb, table)


def bias_kernel(near_ref, far_ref, index_ref, out_ref):
    own = out_ref.shape[0] // 2
    chunks = near_ref.shape[1] // LANES
    tables = (near_ref[...].astype(F32), far_ref[...].astype(F32))
    for row in range(0, SEQ, 8):
        for col in range(0, index_ref.shape[1], LANES):
            index = index_ref[row : row + 8, col : col + LANES]
            low = index & (LANES - 1)
            high = index >> 7
            for head in range(2 * own):
                table_ref, at = (0, 2 + head) if head < own else (1, 2 + head - own)
                found = jnp.zeros((8, LANES), F32)
                for chunk in range(chunks):
                    source = jnp.broadcast_to(
                        tables[table_ref][at : at + 1, chunk * LANES : (chunk + 1) * LANES], (8, LANES)
                    )
                    picked = jnp.take_along_axis(source, low, axis=1)
                    found = jnp.where(high == chunk, picked, found)
                out_ref[head, row : row + 8, col : col + LANES] = found


def small_spec(small):
    return whole((SMALL_ROWS, small[0].shape[1]), small[1])


def position_bias(small, heads, index):
    return pl.pallas_call(
        bias_kernel,
        out_shape=shaped((heads, SEQ, index.shape[1]), F32),
        grid=(1,),
        in_specs=[small_spec(item) for item in small] + [whole(index.shape)],
        out_specs=resident((heads, SEQ, index.shape[1])),
        compiler_params=pltpu.CompilerParams(vmem_limit_bytes=VMEM_LIMIT),
        cost_estimate=cost(4),
        name="position_bias",
    )(*[item for item, _ in small], index)


TABLE_ROWS = 8


def table_kernel(*refs):
    total_refs, (index_ref, out_ref) = refs[:4], refs[4:]

    @pl.when(pl.program_id(0) == 0)
    def _():
        out_ref[...] = jnp.zeros_like(out_ref)

    chunks = out_ref.shape[0] // sum(ref.shape[0] for ref in total_refs)
    spots = lax.broadcasted_iota(jnp.int32, (LANES, SEQ), 0)
    acc = jnp.zeros(out_ref.shape, F32)
    for row in range(TABLE_ROWS):
        index = index_ref[row : row + 1, :]
        hot = (spots == (index & (LANES - 1))).astype(F32).astype(BF)
        high = index >> 7
        total = jnp.concatenate([ref[:, row, :] for ref in total_refs], axis=0)
        parts = [jnp.where(high == chunk, total, 0.0) for chunk in range(chunks)]
        acc = acc + dot_nt(jnp.concatenate(parts, axis=0).astype(BF), hot)
    out_ref[...] += acc


def table_sums(totals, index, chunks, first, steps):
    heads = sum(total.shape[0] for total in totals)
    return pl.pallas_call(
        table_kernel,
        out_shape=shaped((chunks * heads, LANES), F32),
        grid=(steps,),
        in_specs=[
            pl.BlockSpec((total.shape[0], TABLE_ROWS, SEQ), lambda i: (0, first + i, 0))
            for total in totals
        ]
        + [pl.BlockSpec((TABLE_ROWS, SEQ), lambda i: (first + i, 0))],
        out_specs=resident((chunks * heads, LANES)),
        compiler_params=params(),
        cost_estimate=cost(8),
        name="table_sums",
    )(*totals, index)


def block(values, at):
    return values[:, at * LANES : (at + 1) * LANES]


def turned(values):
    return pltpu.roll(values, HEAD, 1)


def only(keep, values):
    return jnp.where(keep, values, jnp.zeros_like(values))


def lower_lanes():
    return lax.broadcasted_iota(jnp.int32, (SEQ, LANES), 1) < HEAD


def shard_forward(x, weight_ref, small_ref, bias_ref, mask, joint_ref, probs_ref, context_ref, base):
    width = joint_ref.shape[2]
    own = width // 3
    low = lower_lanes()
    high = jnp.logical_not(low)
    column = lax.broadcasted_iota(jnp.int32, (1, width), 1)
    scale = jnp.where(column < own, HEAD**-0.5, 1.0)
    joint = dot_nt(x, weight_ref[...])
    joint_ref[0] = ((joint + small_ref[...].astype(F32)[0:1, :width]) * scale).astype(BF)
    joint = joint_ref[0]
    b1, b2, b3 = block(joint, 1), block(joint, 2), block(joint, 3)
    t0, t1 = turned(block(joint, 0)), turned(b1)
    left = [only(high, b1), only(low, b2), only(high, b2)]
    right = [t0, t0, t1]
    value = [b3, b3, joint[:, 4 * LANES :]]
    found = []
    for head in range(3):
        scores = dot_nt(left[head], right[head]) + bias_ref[base + head][:, :SEQ] + mask
        raised = jnp.exp(scores - jnp.max(scores, axis=0, keepdims=True))
        probs = (raised * (1.0 / jnp.sum(raised, axis=0, keepdims=True))).astype(BF)
        probs_ref[0, base + head] = probs
        found.append(dot_tn(probs, value[head]))
    context_ref[0, :, :LANES] = jnp.where(low, found[0], found[1]).astype(BF)
    context_ref[0, :, LANES:] = found[2].astype(BF)


def attend_near_kernel(
    ids_ref, patch_ref, sel_ref, token_ref, gain_ref, shift_ref, w0_ref, w1_ref, s0_ref, s1_ref,
    o0_ref, o1_ref, bias_ref, mask_ref,
    normed_ref, joint0_ref, joint1_ref, probs_ref, context0_ref, context1_ref, part_ref,
):
    token = token_line(ids_ref, token_ref)
    for at in tiles():
        start, _ = mixed(patch_ref, sel_ref, token, at)
        xhat, _ = normalise(start)
        normed_ref[0, at : at + TILE, :] = (xhat * line(gain_ref) + line(shift_ref)).astype(BF)
    x = normed_ref[0]
    mask = mask_ref[0]
    own = w0_ref.shape[0] // 3 // HEAD
    shard_forward(x, w0_ref, s0_ref, bias_ref, mask, joint0_ref, probs_ref, context0_ref, 0)
    shard_forward(x, w1_ref, s1_ref, bias_ref, mask, joint1_ref, probs_ref, context1_ref, own)
    part_ref[0] = dot_nn(context0_ref[0], o0_ref[...]) + dot_nn(context1_ref[0], o1_ref[...])


def attend_far_kernel(
    ids_ref, side_ref, patch_ref, sel_ref, token_ref, normed_ref, part_ref, p0_ref, q0_ref, p1_ref,
    q1_ref, s0_ref, s1_ref, bias_ref, mask_ref, obias_ref, gamma_ref, gain_ref, shift_ref,
    joint0_ref, joint1_ref, probs_ref, context0_ref, context1_ref, value_ref, middle_ref, out_ref,
    pack0_ref, pack1_ref,
):
    half = p0_ref.shape[0] - SMALL_ROWS

    @pl.when(pl.program_id(0) == 0)
    def _():
        for side in range(2):
            @pl.when(side_ref[0] == side)
            def _():
                for p_ref, q_ref, pack_ref in ((p0_ref, q0_ref, pack0_ref), (p1_ref, q1_ref, pack1_ref)):
                    pack_ref[side * half : (side + 1) * half, :] = p_ref[:half, :]
                    pack_ref[(1 - side) * half : (2 - side) * half, :] = q_ref[:half, :]

    x = normed_ref[0]
    mask = mask_ref[0]
    joint = joint0_ref.shape[2]
    own = joint // 3 // HEAD
    w0_ref, w1_ref = pack0_ref.at[:joint], pack1_ref.at[:joint]
    o0_ref, o1_ref = pack0_ref.at[joint:], pack1_ref.at[joint:]
    shard_forward(x, w0_ref, s0_ref, bias_ref, mask, joint0_ref, probs_ref, context0_ref, 0)
    shard_forward(x, w1_ref, s1_ref, bias_ref, mask, joint1_ref, probs_ref, context1_ref, own)
    value_ref[0] = (
        dot_nn(context0_ref[0], o0_ref[...]) + dot_nn(context1_ref[0], o1_ref[...]) + part_ref[0]
    )
    token = token_line(ids_ref, token_ref)
    for at in tiles():
        rows = slice(at, at + TILE)
        start, _ = mixed(patch_ref, sel_ref, token, at)
        value = value_ref[0, rows, :] + line(obias_ref)
        middle = start + line(gamma_ref) * value
        xhat, _ = normalise(middle)
        value_ref[0, rows, :] = value
        middle_ref[0, rows, :] = middle
        out_ref[0, rows, :] = (xhat * line(gain_ref) + line(shift_ref)).astype(BF)


def mix_specs(width, groups):
    return [
        image_spec(width),
        pl.BlockSpec((1, SEQ, 1), lambda i, ids, *_: (ids[i], 0, 0)),
        whole((groups, width)),
    ]


def attend(mix, weights, smalls, bias, mask, before, after, first):
    ids, patches, sel_table, tokens = mix[-4:]
    images, _, width = patches.shape
    heads = bias.shape[0]
    joint = 3 * heads // 2 * HEAD
    context = joint // 3
    square = pl.BlockSpec((1, heads, SEQ, SEQ), lambda i, *_: (i, 0, 0, 0))
    rows = shaped(patches.shape, BF)
    wide = shaped(patches.shape, F32)
    per = shaped((images, SEQ, joint), BF)
    con = shaped((images, SEQ, context), BF)
    prob = shaped((images, heads, SEQ, SEQ), BF)
    small_specs = [small_spec(small) for small in smalls]
    smalls = [item for item, _ in smalls]
    position = [whole(bias.shape), image_spec(1)]
    core_out = [per, per, prob, con, con]
    core_spec = [image_spec(joint)] * 2 + [square] + [image_spec(context)] * 2
    vector = whole((width,))
    if first:
        w0, w1, o0, o1 = weights
        prefetch = [ids]
        in_specs = (
            [vector] * 2 + [whole((joint, width))] * 2 + small_specs + [whole((context, width))] * 2
            + position
        )
        operands = [*before, w0, w1, *smalls, o0, o1, bias, mask]
        out_shape = [rows] + core_out + [wide]
        out_specs = [image_spec(width)] + core_spec + [image_spec(width)]
        scratch = []
    else:
        prefetch = [ids, mix[0]]
        in_specs = (
            [image_spec(width)] * 2 + [whole(item.shape) for item in weights] + small_specs + position
            + [vector] * 4
        )
        operands = [*before, *weights, *smalls, bias, mask, *after]
        out_shape = core_out + [wide, wide, rows]
        out_specs = core_spec + [image_spec(width)] * 3
        scratch = [pltpu.VMEM((joint + context, width), BF)] * 2
        out_shape += [shaped((joint + context, width), BF)] * 2
        out_specs += [resident((joint + context, width))] * 2
        scratch = []
    return pl.pallas_call(
        attend_near_kernel if first else attend_far_kernel,
        out_shape=out_shape,
        grid_spec=pltpu.PrefetchScalarGridSpec(
            num_scalar_prefetch=len(prefetch),
            grid=(images,),
            in_specs=mix_specs(width, tokens.shape[0]) + in_specs,
            out_specs=out_specs,
            scratch_shapes=scratch,
        ),
        compiler_params=params(),
        cost_estimate=cost(19),
        name="attend_near" if first else "attend_far",
    )(*prefetch, patches, sel_table, tokens, *operands)


def shard_backward(
    x, grad, joint_ref, probs_ref, context_ref, weight_ref, out_ref, total_ref, sums_ref, acc_ref,
    joint_grad_ref, base,
):
    width = joint_ref.shape[2]
    own = width // 3
    low = lower_lanes()
    high = jnp.logical_not(low)
    grad_context = dot_nt(grad, out_ref[...]).astype(BF)
    d0, d1 = grad_context[:, :LANES], grad_context[:, LANES:]
    joint = joint_ref[0]
    b3 = block(joint, 3)
    t0, t1, t2 = turned(block(joint, 0)), turned(block(joint, 1)), turned(block(joint, 2))
    left = [only(low, b3), only(high, b3), joint[:, 4 * LANES :]]
    right = [d0, d0, d1]
    queries = [t0, t0, t1]
    keys = [t1, t2, t2]
    grads_q, grads_k, grads_v = [], [], []
    for head in range(3):
        probs = probs_ref[0, base + head]
        wide = probs.astype(F32)
        grad_probs = dot_nt(left[head], right[head])
        centre = jnp.sum(wide * grad_probs, axis=0, keepdims=True)
        grad_scores = (wide * (grad_probs - centre)).astype(BF)
        total_ref[base + head] += grad_scores.astype(F32)
        grads_v.append(dot_nn(probs, right[head]))
        grads_k.append(dot_nn(grad_scores, queries[head]))
        grads_q.append(dot_tn(grad_scores, keys[head]))
    scale = HEAD**-0.5
    blocks = [
        jnp.where(low, grads_q[0], grads_q[1]) * scale,
        jnp.where(low, grads_q[2] * scale, grads_k[0]),
        jnp.where(low, grads_k[1], grads_k[2]),
        jnp.where(low, grads_v[0], grads_v[1]),
        grads_v[2],
    ]
    for at, values in enumerate(blocks):
        cols = slice(at * LANES, at * LANES + values.shape[1])
        held = values.astype(BF)
        joint_grad_ref[:, cols] = held
        sums_ref[:, cols] += fold(held.astype(F32))
    joint_grad = joint_grad_ref[...]
    acc_ref[:width, :] += dot_tn(joint_grad, x)
    acc_ref[width:, :] += dot_tn(context_ref[0], grad)
    return dot_nn(joint_grad, weight_ref[...])


def attend_back_kernel(first, last, *refs):
    if last:
        ids_ref, patch_ref, sel_ref, token_ref, gmiddle_ref, gain_ref = refs[:6]
        refs = refs[6:]
    else:
        refs = refs[1:]
    if not first:
        carried_ref, refs = refs[0], refs[1:]
    x_ref, grad_ref, joint_ref, probs_ref, context_ref, weight_ref, out_ref = refs[:7]
    refs = refs[7:]
    g_ref, total_ref, sums_ref = refs[:3]
    refs = refs[3:]
    if last:
        patch_out_ref, norm_ref, token_out_ref, acc_ref, joint_grad_ref, carry_ref = refs
    else:
        carry_out_ref, acc_ref, joint_grad_ref = refs
    step = pl.program_id(0)

    @pl.when(step == 0)
    def _():
        for ref in (total_ref, sums_ref, acc_ref) + ((norm_ref,) if last else ()):
            ref[...] = jnp.zeros_like(ref)

    x = x_ref[0]
    part = shard_backward(
        x, grad_ref[0], joint_ref, probs_ref, context_ref, weight_ref, out_ref, total_ref, sums_ref,
        acc_ref, joint_grad_ref, 0,
    )
    if not first:
        part = part + carried_ref[0]
    if last:
        carry_ref[...] = part
        token = token_line(ids_ref, token_ref)
        token_sum = jnp.zeros((8, x.shape[1]), F32)
        for at in tiles():
            rows = slice(at, at + TILE)
            start, sel = mixed(patch_ref, sel_ref, token, at)
            xhat, scale = normalise(start)
            grad_normed = carry_ref[rows, :]
            norm_ref[0:8, :] += fold(grad_normed * xhat)
            norm_ref[8:16, :] += fold(grad_normed)
            grad_start = gmiddle_ref[0, rows, :] + normalise_back(
                grad_normed, line(gain_ref), xhat, scale
            )
            patch_out_ref[0, rows, :] = grad_start * (1.0 - sel)
            token_sum = token_sum + fold(grad_start * sel)
        token_out_ref[0] = token_sum
    else:
        carry_out_ref[0] = part

    @pl.when(step == pl.num_programs(0) - 1)
    def _():
        g_ref[...] = acc_ref[...].astype(BF)


def attend_back(ids, x, grad, joint, probs, turn, context, weight, out, carried, tail):
    images, _, width = x.shape
    joint_width = joint.shape[2]
    own = joint_width // 3
    heads = own // HEAD
    square = pl.BlockSpec((1, heads, SEQ, SEQ), lambda i, *_: (i, turn, 0, 0))
    first, last = carried is None, tail is not None
    in_specs = (
        [image_spec(width)] * 2
        + [image_spec(joint_width), square, image_spec(own)]
        + [whole((joint_width, width), weight[1]), whole((own, width), out[1])]
    )
    operands = [x, grad, joint, probs, context, weight[0], out[0]]
    if not first:
        in_specs = [image_spec(width)] + in_specs
        operands = [carried] + operands
    out_shape = [
        shaped((joint_width + own, width), BF),
        shaped((heads, SEQ, SEQ), F32),
        shaped((8, joint_width), F32),
    ]
    out_specs = [resident(item.shape) for item in out_shape]
    scratch = [pltpu.VMEM((joint_width + own, width), F32), pltpu.VMEM((SEQ, joint_width), BF)]
    if last:
        patches, sel_table, tokens, grad_middle, gain = tail
        in_specs = (
            mix_specs(width, tokens.shape[0]) + [image_spec(width), whole((width,))] + in_specs
        )
        operands = [patches, sel_table, tokens, grad_middle, gain] + operands
        out_shape += [
            shaped(x.shape, F32), shaped((16, width), F32), shaped((images, 8, width), F32)
        ]
        out_specs += [
            image_spec(width),
            resident((16, width)),
            pl.BlockSpec((1, 8, width), lambda i, *_: (i, 0, 0)),
        ]
        scratch.append(pltpu.VMEM((SEQ, width), F32))
    else:
        out_shape.append(shaped(x.shape, F32))
        out_specs.append(image_spec(width))
    return pl.pallas_call(
        functools.partial(attend_back_kernel, first, last),
        out_shape=out_shape,
        grid_spec=pltpu.PrefetchScalarGridSpec(
            num_scalar_prefetch=1,
            grid=(images,),
            in_specs=in_specs,
            out_specs=out_specs,
            scratch_shapes=scratch,
        ),
        compiler_params=params(),
        cost_estimate=cost(14),
        name="attend_back_last" if last else "attend_back",
    )(ids, *operands)


CHUNK = 256


def mlp_kernel(first, parted, *refs):
    if parted:
        side_ref, refs = refs[0], refs[1:]
    x_ref, cot_ref, gamma_ref, up_ref = refs[:4]
    refs = refs[4:]
    if parted:
        p_ref, q_ref = refs[:2]
        refs = refs[2:]
    else:
        down_ref = refs[0]
        refs = refs[1:]
    small_ref, refs = refs[0], refs[1:]
    if not first:
        value_in, grad_in = refs[:2]
        refs = refs[2:]
    value_ref, grad_ref, up_grad_ref, down_grad_ref, upb_grad_ref, gm_ref = refs[:6]
    step = pl.program_id(0)

    @pl.when(step == 0)
    def _():
        gm_ref[...] = (line(gamma_ref) * cot_ref[...].astype(F32)).astype(BF)
        if first:
            value_ref[...] = jnp.zeros_like(value_ref)
            grad_ref[...] = jnp.zeros_like(grad_ref)
        else:
            value_ref[...] = value_in[...]
            grad_ref[...] = grad_in[...]

    if parted:
        down_ref = refs[6]
        half = p_ref.shape[1]
        for side in range(2):
            @pl.when(side_ref[0] == side)
            def _():
                down_ref[:, side * half : (side + 1) * half] = p_ref[...]
                down_ref[:, (1 - side) * half : (2 - side) * half] = q_ref[...]

    x = x_ref[...]
    gm = gm_ref[...]
    up = up_ref[...]
    down = down_ref[...]
    before = dot_nn(x, up) + small_ref[...].astype(F32)[1:2, :]
    share = 0.5 + 0.5 * lax.erf(before * (0.5**0.5))
    density = jnp.exp(before * before * -0.5) * ((2.0 * jnp.pi) ** -0.5)
    hidden = (before * share).astype(BF)
    slope = share + before * density
    value_ref[...] += dot_nn(hidden, down)
    down_grad_ref[...] = dot_tn(hidden, gm).astype(BF)
    grad_before = (dot_nt(gm, down) * slope).astype(BF)
    upb_grad_ref[...] = fold(grad_before.astype(F32))
    up_grad_ref[...] = dot_tn(x, grad_before).astype(BF)
    grad_ref[...] += dot_nt(grad_before, up)


def mlp(x, cot, gamma, up, down, small, carried, side=None):
    rows, width = x.shape
    hidden = up.shape[1]
    parted = side is not None
    first = carried is None
    full = pl.BlockSpec((rows, width), lambda i, *_: (0, 0), pipeline_mode=pl.Buffered(1))
    up_spec = pl.BlockSpec((width, CHUNK), lambda i, *_: (0, i))
    down_spec = pl.BlockSpec((CHUNK, width), lambda i, *_: (i, 0))
    half_spec = pl.BlockSpec((CHUNK, width // 2), lambda i, *_: (i, 0))
    in_specs = [full, full, whole((width,)), up_spec]
    in_specs += [half_spec] * 2 if parted else [down_spec]
    in_specs += [pl.BlockSpec((SMALL_ROWS, CHUNK), lambda i, *_: (small[1], i))]
    operands = ([side] if parted else []) + [x, cot, gamma, up] + list(down) + [small[0]]
    aliases = {}
    if not first:
        aliases = {len(operands): 0, len(operands) + 1: 1}
        in_specs += [full, full]
        operands += list(carried)
    scratch = [pltpu.VMEM((rows, width), BF)]
    if parted:
        scratch.append(pltpu.VMEM((CHUNK, width), BF))
    return pl.pallas_call(
        functools.partial(mlp_kernel, first, parted),
        out_shape=(
            shaped((rows, width), F32),
            shaped((rows, width), F32),
            shaped((width, hidden), BF),
            shaped((hidden, width), BF),
            shaped((8, hidden), F32),
        ),
        grid_spec=pltpu.PrefetchScalarGridSpec(
            num_scalar_prefetch=1 if parted else 0,
            grid=(hidden // CHUNK,),
            in_specs=in_specs,
            out_specs=(
                full, full, up_spec, down_spec, pl.BlockSpec((8, CHUNK), lambda i, *_: (0, i))
            ),
            scratch_shapes=scratch,
        ),
        input_output_aliases=aliases,
        compiler_params=params(),
        cost_estimate=cost(16),
        name="mlp_far" if parted else "mlp_near",
    )(*operands)


def middle_back_kernel(
    value_ref, grad_ref, middle_ref, attn_ref, cot_ref, dbias_ref, gmlp_ref, gattn_ref, gain_ref,
    out_ref, gmiddle_ref, gattn_out_ref, sums_ref,
):
    @pl.when(pl.program_id(0) == 0)
    def _():
        sums_ref[...] = jnp.zeros_like(sums_ref)

    def add(row, values):
        sums_ref[8 * row : 8 * row + 8, :] += fold(values)

    for at in tiles():
        rows = slice(at, at + TILE)
        value = value_ref[0, rows, :] + line(dbias_ref)
        cot = cot_ref[0, rows, :].astype(F32)
        middle = middle_ref[0, rows, :]
        out_ref[0, rows, :] = (middle + line(gmlp_ref) * value).astype(BF)
        add(0, cot * value)
        add(1, (line(gmlp_ref) * cot).astype(BF).astype(F32))
        xhat, scale = normalise(middle)
        grad = grad_ref[0, rows, :]
        add(2, grad * xhat)
        add(3, grad)
        grad_middle = cot + normalise_back(grad, line(gain_ref), xhat, scale)
        gmiddle_ref[0, rows, :] = grad_middle
        add(4, grad_middle * attn_ref[0, rows, :])
        grad_attn = (line(gattn_ref) * grad_middle).astype(BF)
        gattn_out_ref[0, rows, :] = grad_attn
        add(5, grad_attn.astype(F32))


def middle_back(value, grad, middle, attn, cot, vectors):
    images, _, width = middle.shape
    return pl.pallas_call(
        middle_back_kernel,
        out_shape=(
            shaped(middle.shape, BF),
            shaped(middle.shape, F32),
            shaped(middle.shape, BF),
            shaped((48, width), F32),
        ),
        grid=(images,),
        in_specs=[image_spec(width)] * 5 + [whole((width,))] * 4,
        out_specs=(image_spec(width),) * 3 + (resident((48, width)),),
        compiler_params=params(),
        cost_estimate=cost(8),
        name="middle_back",
    )(value, grad, middle, attn, cot, *vectors)


def swap(values, axis, mask):
    count = lax.axis_size(axis)
    return lax.ppermute(values, axis, [(i, i ^ mask) for i in range(count)])


def dp_masks():
    count = lax.axis_size("dp")
    return [1 << bit for bit in range(count.bit_length() - 1)]


def pinned(value, *others):
    return lax.optimization_barrier((value,) + others)[0]


def plus(left, right):
    return (left.astype(F32) + right.astype(F32)).astype(BF)


ORDERS = ((0, 1), (1, 2))


def axis_bits():
    place = lax.axis_index("dp")
    return jnp.stack([(place >> bit) & 1 for bit in range(len(dp_masks()))]).astype(jnp.int32)


def halves_of(ref, base, size, bit):
    keep = pl.multiple_of(base + bit * size, 16)
    sent = pl.multiple_of(base + (1 - bit) * size, 16)
    return ref[pl.ds(keep, size), :], ref[pl.ds(sent, size), :]


def split_kernel(bits_ref, a_ref, b_ref, c_ref, *refs):
    outs, total_ref = refs[:4], refs[4]
    for at in range(0, total_ref.shape[0], 64):
        rows = slice(at, at + 64)
        total_ref[rows, :] = (
            a_ref[rows, :].astype(F32) + b_ref[rows, :].astype(F32) + c_ref[rows, :].astype(F32)
        ).astype(BF)
    part = total_ref.shape[0] // 2
    for which in range(2):
        keep, sent = halves_of(total_ref, which * part, part // 2, bits_ref[ORDERS[which][0]])
        outs[2 * which][...] = keep
        outs[2 * which + 1][...] = sent


def again_kernel(bits_ref, *refs):
    ins, outs, totals = refs[:4], refs[4:8], refs[8:]
    for which in range(2):
        total_ref = totals[which]
        total_ref[...] = plus(ins[2 * which][...], ins[2 * which + 1][...])
        size = total_ref.shape[0] // 2
        keep, sent = halves_of(total_ref, 0, size, bits_ref[ORDERS[which][1]])
        outs[2 * which][...] = keep
        outs[2 * which + 1][...] = sent


def both_kernel(bits_ref, *refs):
    for which in range(2):
        refs[4 + which][...] = plus(refs[2 * which][...], refs[2 * which + 1][...])


def put(out_ref, base, own, other, bit):
    size = own.shape[0]
    out_ref[pl.ds(pl.multiple_of(base + bit * size, 16), size), :] = own.astype(out_ref.dtype)
    out_ref[pl.ds(pl.multiple_of(base + (1 - bit) * size, 16), size), :] = other.astype(out_ref.dtype)


def grow_kernel(bits_ref, *refs):
    for which in range(2):
        put(refs[4 + which], 0, refs[2 * which][...], refs[2 * which + 1][...], bits_ref[ORDERS[which][1]])


def whole_kernel(bits_ref, *refs):
    ins, (first_ref, second_ref, total_ref) = refs[:4], refs[4:]
    part = total_ref.shape[0] // 2
    for which in range(2):
        put(total_ref, which * part, ins[2 * which][...], ins[2 * which + 1][...], bits_ref[ORDERS[which][0]])
    cut = first_ref.shape[0]
    first_ref[...] = total_ref[:cut, :].astype(F32)
    second_ref[...] = total_ref[cut:, :].astype(F32)


def step_call(kernel, bits, arrays, outs, scratch, name):
    vmem = pl.BlockSpec(memory_space=pltpu.VMEM)
    return pl.pallas_call(
        kernel,
        out_shape=outs,
        in_specs=[pl.BlockSpec(memory_space=pltpu.SMEM)] + [vmem] * len(arrays),
        out_specs=[vmem] * len(outs),
        scratch_shapes=scratch,
        compiler_params=pltpu.CompilerParams(vmem_limit_bytes=VMEM_LIMIT),
        cost_estimate=cost(1),
        name=name,
    )(bits, *arrays)


def dp_total(pieces, sizes, between):
    bits = axis_bits()
    masks = dp_masks()
    rows, width = pieces[0].shape
    quarter, eighth = shaped((rows // 4, width), BF), shaped((rows // 8, width), BF)

    def send(arrays, axes):
        got = [swap(array, "dp", masks[axis]) for array, axis in zip(arrays, axes)]
        between(got)
        return got

    a, a_sent, b, b_sent = step_call(
        split_kernel, bits, pieces, [quarter] * 4, [pltpu.VMEM((rows, width), BF)], "dp_split"
    )
    a_got, b_got = send([a_sent, b_sent], [ORDERS[0][0], ORDERS[1][0]])
    a, a_sent, b, b_sent = step_call(
        again_kernel, bits, [a, a_got, b, b_got], [eighth] * 4,
        [pltpu.VMEM((rows // 4, width), BF)] * 2, "dp_again",
    )
    a_got, b_got = send([a_sent, b_sent], [ORDERS[0][1], ORDERS[1][1]])
    rest = [[axis for axis in range(len(masks)) if axis not in order] for order in ORDERS]
    a, b = step_call(both_kernel, bits, [a, a_got, b, b_got], [eighth] * 2, [], "dp_both")
    for axes in zip(*rest):
        a_got, b_got = send([a, b], axes)
        a, b = step_call(both_kernel, bits, [a, a_got, b, b_got], [eighth] * 2, [], "dp_both")
    a_got, b_got = send([a, b], [ORDERS[0][1], ORDERS[1][1]])
    a, b = step_call(grow_kernel, bits, [a, a_got, b, b_got], [quarter] * 2, [], "dp_grow")
    a_got, b_got = send([a, b], [ORDERS[0][0], ORDERS[1][0]])
    return step_call(
        whole_kernel, bits, [a, a_got, b, b_got],
        [shaped((size, width), F32) for size in sizes], [pltpu.VMEM((rows, width), BF)], "dp_whole",
    )


def collect_kernel(ids_ref, sums2_ref, sums1_ref, tokens_ref, table0_ref, table1_ref, *refs):
    upb_refs, joint_refs, (out_ref, sent_ref) = refs[:4], refs[4:8], refs[8:]
    out_ref[...] = jnp.zeros_like(out_ref)
    sent_ref[...] = jnp.zeros_like(sent_ref)
    table = table0_ref[...] + table1_ref[...]

    def total(values):
        return jnp.sum(values, axis=0, keepdims=True)

    lines = [total(sums2_ref[8 * i : 8 * i + 8, :]) for i in range(6)]
    lines += [total(sums1_ref[8 * i : 8 * i + 8, :]) for i in range(2)]
    images = [total(tokens_ref[i]) for i in range(tokens_ref.shape[0])]
    for group in range(GROUPS):
        found = jnp.zeros_like(images[0])
        for at, values in enumerate(images):
            found = found + jnp.where(ids_ref[at] == group, values, 0.0)
        lines.append(found)
    for at, values in enumerate(lines):
        out_ref[8 + at : 9 + at, :] = values
        sent_ref[8 + at : 9 + at, :] = values
    hidden = upb_refs[0].shape[1]
    for which in range(4):
        ref = out_ref if which % 2 == 0 else sent_ref
        base = 0 if which < 2 else 24
        ref[base : base + 1, :hidden] = total(upb_refs[which][...])
        joint = total(joint_refs[which][...])
        ref[base + 1 : base + 2, : joint.shape[1]] = joint
        per = table.shape[0] // (out_ref.shape[1] // LANES)
        own = per // 4
        for chunk in range(out_ref.shape[1] // LANES):
            ref[base + 2 : base + 2 + own, chunk * LANES : (chunk + 1) * LANES] = table[
                chunk * per + which * own : chunk * per + (which + 1) * own, :
            ]


def collect(ids, sums2, sums1, tokens, tables, upbs, joints):
    width = sums2.shape[1]
    vmem = pl.BlockSpec(memory_space=pltpu.VMEM)
    return pl.pallas_call(
        collect_kernel,
        out_shape=(shaped((32, width), F32), shaped((32, width), F32)),
        in_specs=[pl.BlockSpec(memory_space=pltpu.SMEM)] + [vmem] * 13,
        out_specs=(vmem, vmem),
        cost_estimate=cost(1),
        name="collect",
    )(ids, sums2, sums1, tokens, *tables, *upbs, *joints)


def emit_kernel(held_ref, got_ref, *outs):
    own = outs[9].shape[0]
    value = held_ref[...] + got_ref[...]
    for at in range(8):
        outs[at][...] = value[8 + at : 9 + at, :].reshape(-1)
    outs[8][...] = value[16:24, :]
    outs[9][...] = value[1:2, :own].reshape(-1)
    outs[10][...] = value[1:2, 2 * own : 3 * own].reshape(-1)
    outs[11][...] = value[2 : 2 + outs[11].shape[0], : outs[11].shape[1]]
    outs[12][...] = value[0:1, : outs[12].shape[0]].reshape(-1)


def emit(held, got, own, table_shape, hidden):
    width = held.shape[1]
    return pl.pallas_call(
        emit_kernel,
        out_shape=[shaped((width,), F32)] * 8
        + [
            shaped((GROUPS, width), F32),
            shaped((own,), F32),
            shaped((own,), F32),
            shaped(table_shape, F32),
            shaped((hidden,), F32),
        ],
        cost_estimate=cost(1),
        name="emit",
    )(held, got)


def local(
    patches, dataset_id, patch_masks, mask_tokens, key_mask, bias_index, norm1_gain, norm1_shift,
    qkv_weight, query_bias, value_bias, bias_table, out_weight, out_bias, gamma_attn, norm2_gain,
    norm2_shift, up_weight, up_bias, down_weight, down_bias, gamma_mlp, cotangent,
):
    rows, width = patches.shape
    images = rows // SEQ
    place = lax.axis_index("mp")
    own = qkv_weight.shape[2]
    own_heads = own // HEAD
    table_rows = bias_table.shape[0]
    chunks = width // LANES
    hidden = up_weight.shape[1]

    ids = lax.dynamic_slice_in_dim(dataset_id, place * images, images, 0)
    keys_here = lax.dynamic_slice_in_dim(key_mask, place * images, images, 0)
    mask = jnp.where(keys_here > 0, 0.0, -1e30).astype(F32)[:, :, None]
    sel_table = patch_masks.astype(F32)[:, :, None]
    images3 = patches.reshape(images, SEQ, width)
    cot3 = cotangent.reshape(images, SEQ, width)
    index = bias_index.T
    index_wide = jnp.pad(index, ((0, 0), (0, 2 * LANES - SEQ)))
    mix = (ids, images3, sel_table, mask_tokens)

    parity = lax.axis_index("dp") & 1
    side = parity.reshape(1)
    qkv_own = qkv_weight.transpose(1, 2, 0).reshape(3 * own, width)
    small, attn_half, down_half = prepare(
        side, qkv_own, out_weight, down_weight, query_bias, value_bias, up_bias, bias_table.T
    )
    small0, small1 = (small, 0), (swap(small, "mp", 1), 0)
    attn_p2 = swap(attn_half, "mp", 2)
    down_p2 = swap(down_half, "mp", 2)
    qkv1, out1 = swap(qkv_own, "mp", 1), swap(out_weight, "mp", 1)
    bias_near = position_bias([small0, small1], 2 * own_heads, index_wide)
    up2 = swap(pinned(up_weight, bias_near), "mp", 2)
    up1, down1 = swap(up_weight, "mp", 1), swap(down_weight, "mp", 1)

    attn_p2, bias_near = lax.optimization_barrier((attn_p2, bias_near))
    attn_q2 = swap(attn_p2, "dp", 1)
    attn_p3 = swap(attn_p2, "mp", 1)
    small2, small3 = (attn_p2, 2 * own // SMALL_ROWS), (attn_p3, 2 * own // SMALL_ROWS)
    normed1, j0, j1, probs_near, c0, c1, part = attend(
        mix, [qkv_own, qkv1, out_weight, out1], [small0, small1], bias_near, mask,
        [norm1_gain, norm1_shift], [], True,
    )
    part, attn_q2, down_p2 = lax.optimization_barrier((part, attn_q2, down_p2))
    attn_q3 = swap(attn_q2, "mp", 1)
    bias_far = position_bias([small2, small3], 2 * own_heads, pinned(index_wide, part))
    down_q2 = swap(down_p2, "dp", 1)
    down_p3 = swap(down_p2, "mp", 1)
    j2, j3, probs_far, c2, c3, attn_value, middle, normed2, pack2, pack3 = attend(
        (side,) + mix, [attn_p2, attn_q2, attn_p3, attn_q3], [small2, small3], bias_far, mask,
        [normed1, part], [out_bias, gamma_attn, norm2_gain, norm2_shift], False,
    )
    normed2, up2, down_q2 = lax.optimization_barrier((normed2, up2, down_q2))
    up3 = swap(up2, "mp", 1)
    down_q3 = swap(down_q2, "mp", 1)

    flat2 = normed2.reshape(rows, width)
    value, grad2, up_g1, down_g1, upb1 = mlp(
        flat2, cotangent, gamma_mlp, up1, [down1], small1, None
    )
    up_r1, down_r1 = swap(up_g1, "mp", 1), swap(down_g1, "mp", 1)
    value, grad2, up_g3, down_g3, upb3 = mlp(
        flat2, cotangent, gamma_mlp, up3, [down_p3, down_q3], small3, (value, grad2), side
    )
    up_r3, down_r3 = swap(up_g3, "mp", 1), swap(down_g3, "mp", 1)
    value, grad2, up_g2, down_g2, upb2 = mlp(
        flat2, cotangent, gamma_mlp, up2, [down_p2, down_q2], small2, (value, grad2), side
    )
    up_far, down_far = plus(up_g2, up_r3), plus(down_g2, down_r3)
    flat2, up_far = lax.optimization_barrier((flat2, up_far))
    up_r2 = swap(up_far, "mp", 2)
    value, grad2, up_g0, down_g0, upb0 = mlp(
        flat2, cotangent, gamma_mlp, up_weight, [down_weight], small0, (value, grad2)
    )
    value, down_far = lax.optimization_barrier((value, down_far))
    down_r2 = swap(down_far, "mp", 2)

    shape3 = (images, SEQ, width)
    output, grad_middle, grad_attn, sums2 = middle_back(
        value.reshape(shape3), grad2.reshape(shape3), middle, attn_value, cot3,
        [down_bias, gamma_mlp, gamma_attn, norm2_gain],
    )

    g3, total3, js3, carried = attend_back(
        ids, normed1, grad_attn, j3, probs_far, 1, c3, (pack3, 0), (pack3, 3), None, None
    )
    r3 = swap(g3, "mp", 1)
    up_sum = (up_g0.astype(F32) + up_r1.astype(F32) + up_r2.astype(F32)).astype(BF)
    down_sum = (down_g0.astype(F32) + down_r1.astype(F32) + down_r2.astype(F32)).astype(BF)
    carried, up_sum, down_sum = lax.optimization_barrier((carried, up_sum, down_sum))
    up_sum, down_sum = lax.psum((up_sum, down_sum), "dp")
    g2, total2, js2, carried = attend_back(
        ids, normed1, grad_attn, j2, probs_far, 0, c2, (pack2, 0), (pack2, 3), carried, None
    )
    far = plus(g2, r3)
    carried, far = lax.optimization_barrier((carried, far))
    r2 = swap(far, "mp", 2)
    g1, total1, js1, carried = attend_back(
        ids, normed1, grad_attn, j1, probs_near, 1, c1, (qkv1, 0), (out1, 0), carried, None
    )
    r1 = swap(g1, "mp", 1)
    g0, total0, js0, patch_grad, sums1, token_images = attend_back(
        ids, normed1, grad_attn, j0, probs_near, 0, c0, (qkv_own, 0), (out_weight, 0), carried,
        (images3, sel_table, mask_tokens, grad_middle, norm1_gain),
    )
    totals = [total0, total1, total2, total3]
    blocks = SEQ // TABLE_ROWS
    tables = []

    def between(got):
        nonlocal index
        if len(tables) < 2:
            first = len(tables) * (blocks // 2)
            steps = blocks // 2 if not tables else blocks - blocks // 2
            tables.append(table_sums(totals, index, chunks, first, steps))

    qkv_sum, out_sum = dp_total([g0, r1, r2], [3 * own, own], between)

    held, sent = collect(
        ids, sums2, sums1, token_images, tables, [upb0, upb1, upb2, upb3], [js0, js1, js2, js3]
    )
    held = held + swap(sent, "mp", 1)
    sent = jnp.concatenate([held[24:], held[8:24]], axis=0)
    held = held[:24] + swap(sent, "mp", 2)
    masks = dp_masks()
    for shift in masks[:-1]:
        held = held + swap(held, "dp", shift)
    (
        gamma_mlp_grad, down_bias_grad, gain2_grad, shift2_grad, gamma_attn_grad, out_bias_grad,
        gain1_grad, shift1_grad, token_grad, qb_grad, vb_grad, table_grad, upb_grad,
    ) = emit(held, swap(held, "dp", masks[-1]), own, (own_heads, table_rows), hidden)

    return (
        output.reshape(rows, width),
        patch_grad.reshape(rows, width),
        token_grad,
        gain1_grad,
        shift1_grad,
        qkv_sum.reshape(3, own, width).transpose(2, 0, 1),
        qb_grad,
        vb_grad,
        table_grad.T,
        out_sum,
        out_bias_grad,
        gamma_attn_grad,
        gain2_grad,
        shift2_grad,
        up_sum.astype(F32),
        upb_grad,
        down_sum.astype(F32),
        down_bias_grad,
        gamma_mlp_grad,
    )


def solution(mesh):
    return jax.shard_map(
        local,
        mesh=mesh,
        in_specs=(
            P(("dp", "mp"), None), P("dp"), P(), P(), P("dp", None), P(), P(), P(),
            P(None, None, "mp"), P("mp"), P("mp"), P(None, "mp"), P("mp", None), P(), P(), P(), P(),
            P(None, "mp"), P("mp"), P("mp", None), P(), P(), P(("dp", "mp"), None),
        ),
        out_specs=(
            P(("dp", "mp"), None), P(("dp", "mp"), None), P(), P(), P(), P(None, None, "mp"),
            P("mp"), P("mp"), P(None, "mp"), P("mp", None), P(), P(), P(), P(), P(None, "mp"),
            P("mp"), P("mp", None), P(), P(),
        ),
        check_vma=False,
    )
```

```python
import functools

import jax
import jax.numpy as jnp
from jax import lax
from jax.experimental import pallas as pl
from jax.experimental.pallas import tpu as pltpu
from jax.sharding import PartitionSpec as P

HEAD = 64
SEQ = 200
GROUPS = 8
LANES = 128
BF = jnp.bfloat16
F32 = jnp.float32


def dot_nn(left, right):
    return lax.dot_general(left, right, (((1,), (0,)), ((), ())), preferred_element_type=F32)


def dot_nt(left, right):
    return lax.dot_general(left, right, (((1,), (1,)), ((), ())), preferred_element_type=F32)


def dot_tn(left, right):
    return lax.dot_general(left, right, (((0,), (0,)), ((), ())), preferred_element_type=F32)


def params(mib, steps=1):
    return pltpu.CompilerParams(
        dimension_semantics=("arbitrary",) * steps, vmem_limit_bytes=mib << 20
    )


def cost(micros):
    return pl.CostEstimate(flops=int(micros * 1.1e8), transcendentals=0, bytes_accessed=0)


def whole(shape, at=0):
    zeros = (0,) * (len(shape) - 1)
    return pl.BlockSpec(shape, lambda *_: (at,) + zeros, pipeline_mode=pl.Buffered(1))


def image_spec(width):
    return pl.BlockSpec((1, SEQ, width), lambda i, *_: (i, 0, 0))


def resident(shape):
    zeros = (0,) * len(shape)
    return pl.BlockSpec(shape, lambda *_: zeros)


def placed(operands, keep=()):
    return [
        item
        if any(item is kept for kept in keep)
        else pltpu.with_memory_space_constraint(item, pltpu.HBM)
        for item in operands
    ]


def in_hbm(shape, dtype):
    return pltpu.HBM(tuple(shape), dtype)


def shaped(shape, dtype):
    return jax.ShapeDtypeStruct(shape, dtype)


TILE = 40


def normalise(values):
    mean = jnp.mean(values, axis=-1, keepdims=True)
    centred = values - mean
    spread = jnp.mean(centred * centred, axis=-1, keepdims=True)
    scale = lax.rsqrt(spread + 1e-06)
    return centred * scale, scale


def normalise_back(grad, gain, xhat, scale):
    u = grad * gain
    return (
        u - jnp.mean(u, axis=-1, keepdims=True) - xhat * jnp.mean(u * xhat, axis=-1, keepdims=True)
    ) * scale


def line(ref):
    return ref[...].reshape(1, -1)


def token_line(ids_ref, token_ref):
    tokens = token_ref[...].astype(F32)
    group = lax.broadcasted_iota(jnp.int32, tokens.shape, 0)
    return jnp.sum(jnp.where(group == ids_ref[pl.program_id(0)], tokens, 0.0), axis=0, keepdims=True)


def mixed(patch_ref, sel_ref, token, at):
    sel = sel_ref[0, at : at + TILE, :]
    return patch_ref[0, at : at + TILE, :].astype(F32) * (1.0 - sel) + sel * token, sel


def tiles():
    return range(0, SEQ, TILE)


def fold(values):
    return jnp.sum(values.reshape(values.shape[0] // 8, 8, values.shape[1]), axis=0)


SMALL_ROWS = 16


def prepare_kernel(
    side_ref, qkv_ref, out_ref, down_ref, qb_ref, vb_ref, upb_ref, table_ref,
    small_ref, attn_ref, half_ref,
):
    own = qb_ref.shape[0]
    width = small_ref.shape[1]
    small_ref[...] = jnp.zeros_like(small_ref)
    small_ref[0:1, :own] = line(qb_ref)
    small_ref[0:1, 2 * own : 3 * own] = line(vb_ref)
    small_ref[1:2, : upb_ref.shape[0]] = line(upb_ref)
    small_ref[2 : 2 + table_ref.shape[0], : table_ref.shape[1]] = table_ref[...]
    attn_ref[2 * own :, :] = small_ref[...]

    @pl.when(side_ref[0] == 0)
    def _():
        attn_ref[: 2 * own, :] = qkv_ref[: 2 * own, :]
        half_ref[...] = down_ref[:, : width // 2]

    @pl.when(side_ref[0] == 1)
    def _():
        attn_ref[:own, :] = qkv_ref[2 * own :, :]
        attn_ref[own : 2 * own, :] = out_ref[...]
        half_ref[...] = down_ref[:, width // 2 :]


def prepare(side, qkv, out, down, qb, vb, upb, table):
    width = out.shape[1]
    vmem = pl.BlockSpec(memory_space=pltpu.VMEM)
    return pl.pallas_call(
        prepare_kernel,
        out_shape=[
            shaped((SMALL_ROWS, width), BF),
            shaped((2 * qb.shape[0] + SMALL_ROWS, width), BF),
            shaped((down.shape[0], width // 2), BF),
        ],
        in_specs=[pl.BlockSpec(memory_space=pltpu.SMEM)] + [vmem] * 7,
        out_specs=[vmem] * 3,
        compiler_params=params(8, 0),
        cost_estimate=cost(2),
        name="prepare",
    )(side, *placed([qkv, out, down, qb, vb, upb, table]))


def bias_kernel(near_ref, far_ref, index_ref, out_ref):
    own = out_ref.shape[0] // 2
    chunks = near_ref.shape[1] // LANES
    tables = (near_ref[...].astype(F32), far_ref[...].astype(F32))
    for row in range(0, SEQ, 8):
        for col in range(0, index_ref.shape[1], LANES):
            index = index_ref[row : row + 8, col : col + LANES]
            low = index & (LANES - 1)
            high = index >> 7
            for head in range(2 * own):
                table_ref, at = (0, 2 + head) if head < own else (1, 2 + head - own)
                found = jnp.zeros((8, LANES), F32)
                for chunk in range(chunks):
                    source = jnp.broadcast_to(
                        tables[table_ref][at : at + 1, chunk * LANES : (chunk + 1) * LANES], (8, LANES)
                    )
                    picked = jnp.take_along_axis(source, low, axis=1)
                    found = jnp.where(high == chunk, picked, found)
                out_ref[head, row : row + 8, col : col + LANES] = found


def small_spec(small):
    return whole((SMALL_ROWS, small[0].shape[1]), small[1])


def position_bias(small, heads, index):
    return pl.pallas_call(
        bias_kernel,
        out_shape=shaped((heads, SEQ, index.shape[1]), F32),
        grid=(1,),
        in_specs=[small_spec(item) for item in small] + [whole(index.shape)],
        out_specs=resident((heads, SEQ, index.shape[1])),
        compiler_params=params(6),
        cost_estimate=cost(2),
        name="position_bias",
    )(*placed([item for item, _ in small] + [index]))


TABLE_ROWS = 8


def table_kernel(*refs):
    total_refs, (index_ref, out_ref) = refs[:4], refs[4:]

    @pl.when(pl.program_id(0) == 0)
    def _():
        out_ref[...] = jnp.zeros_like(out_ref)

    chunks = out_ref.shape[0] // sum(ref.shape[0] for ref in total_refs)
    spots = lax.broadcasted_iota(jnp.int32, (LANES, SEQ), 0)
    acc = jnp.zeros(out_ref.shape, F32)
    for row in range(TABLE_ROWS):
        index = index_ref[row : row + 1, :]
        hot = (spots == (index & (LANES - 1))).astype(F32).astype(BF)
        high = index >> 7
        total = jnp.concatenate([ref[:, row, :] for ref in total_refs], axis=0)
        parts = [jnp.where(high == chunk, total, 0.0) for chunk in range(chunks)]
        acc = acc + dot_nt(jnp.concatenate(parts, axis=0).astype(BF), hot)
    out_ref[...] += acc


def table_sums(totals, index, chunks, first, steps):
    heads = sum(total.shape[0] for total in totals)
    return pl.pallas_call(
        table_kernel,
        out_shape=shaped((chunks * heads, LANES), F32),
        grid=(steps,),
        in_specs=[
            pl.BlockSpec((total.shape[0], TABLE_ROWS, SEQ), lambda i: (0, first + i, 0))
            for total in totals
        ]
        + [pl.BlockSpec((TABLE_ROWS, SEQ), lambda i: (first + i, 0))],
        out_specs=resident((chunks * heads, LANES)),
        compiler_params=params(6),
        cost_estimate=cost(5),
        name="table_sums",
    )(*placed(list(totals) + [index]))


def block(values, at):
    return values[:, at * LANES : (at + 1) * LANES]


def turned(values):
    return pltpu.roll(values, HEAD, 1)


def only(keep, values):
    return jnp.where(keep, values, jnp.zeros_like(values))


def lower_lanes():
    return lax.broadcasted_iota(jnp.int32, (SEQ, LANES), 1) < HEAD


def shard_forward(x, weight_ref, small_ref, bias_ref, mask, joint_ref, probs_ref, context_ref, base):
    width = joint_ref.shape[2]
    own = width // 3
    low = lower_lanes()
    high = jnp.logical_not(low)
    column = lax.broadcasted_iota(jnp.int32, (1, width), 1)
    scale = jnp.where(column < own, HEAD**-0.5, 1.0)
    joint = dot_nt(x, weight_ref[...])
    joint_ref[0] = ((joint + small_ref[...].astype(F32)[0:1, :width]) * scale).astype(BF)
    joint = joint_ref[0]
    b1, b2, b3 = block(joint, 1), block(joint, 2), block(joint, 3)
    t0, t1 = turned(block(joint, 0)), turned(b1)
    left = [only(high, b1), only(low, b2), only(high, b2)]
    right = [t0, t0, t1]
    value = [b3, b3, joint[:, 4 * LANES :]]
    found = []
    for head in range(3):
        scores = dot_nt(left[head], right[head]) + bias_ref[base + head][:, :SEQ] + mask
        raised = jnp.exp(scores - jnp.max(scores, axis=0, keepdims=True))
        probs = (raised * (1.0 / jnp.sum(raised, axis=0, keepdims=True))).astype(BF)
        probs_ref[0, base + head] = probs
        found.append(dot_tn(probs, value[head]))
    context_ref[0, :, :LANES] = jnp.where(low, found[0], found[1]).astype(BF)
    context_ref[0, :, LANES:] = found[2].astype(BF)


def attend_kernel(first, last, parted, *refs):
    refs = list(refs)

    def take(count):
        found = refs[:count]
        del refs[:count]
        return found

    if first or last:
        (ids_ref,) = take(1)
    if parted:
        (side_ref,) = take(1)
    if first or last:
        patch_ref, sel_ref, token_ref, gain_ref, shift_ref = take(5)
    if last:
        obias_ref, gamma_ref = take(2)
    if not first:
        x_ref, part_in_ref = take(2)
    weight_ref, out_ref, small_ref, bias_ref, mask_ref = take(5)
    if first:
        (x_ref,) = take(1)
    joint_ref, probs_ref, context_ref, part_ref = take(4)
    if last:
        middle_ref, normed_ref = take(2)
    if parted:
        p_ref, q_ref = weight_ref, out_ref
        (pack_ref,) = take(1)
        half = p_ref.shape[0] - SMALL_ROWS

        @pl.when(pl.program_id(0) == 0)
        def _():
            for side in range(2):
                @pl.when(side_ref[0] == side)
                def _():
                    pack_ref[side * half : (side + 1) * half, :] = p_ref[:half, :]
                    pack_ref[(1 - side) * half : (2 - side) * half, :] = q_ref[:half, :]

        joint = joint_ref.shape[2]
        weight_ref, out_ref = pack_ref.at[:joint], pack_ref.at[joint:]
    if first:
        token = token_line(ids_ref, token_ref)
        for at in tiles():
            start, _ = mixed(patch_ref, sel_ref, token, at)
            xhat, _ = normalise(start)
            x_ref[0, at : at + TILE, :] = (xhat * line(gain_ref) + line(shift_ref)).astype(BF)
    shard_forward(
        x_ref[0], weight_ref, small_ref, bias_ref, mask_ref[0], joint_ref, probs_ref, context_ref, 0
    )
    part = dot_nn(context_ref[0], out_ref[...])
    part_ref[0] = part if first else part + part_in_ref[0]
    if last:
        token = token_line(ids_ref, token_ref)
        for at in tiles():
            rows = slice(at, at + TILE)
            start, _ = mixed(patch_ref, sel_ref, token, at)
            value = part_ref[0, rows, :] + line(obias_ref)
            middle = start + line(gamma_ref) * value
            xhat, _ = normalise(middle)
            part_ref[0, rows, :] = value
            middle_ref[0, rows, :] = middle
            normed_ref[0, rows, :] = (xhat * line(gain_ref) + line(shift_ref)).astype(BF)


def mix_specs(width, groups):
    return [
        image_spec(width),
        pl.BlockSpec((1, SEQ, 1), lambda i, ids, *_: (ids[i], 0, 0)),
        whole((groups, width)),
    ]


def attend(mix, norm, weight, out, small, bias, turn, mask, x=None, part=None, side=None, after=None):
    ids, patches, sel_table, tokens = mix
    images, _, width = patches.shape
    heads = bias.shape[0] // 2
    own = heads * HEAD
    first, last, parted = x is None, after is not None, side is not None
    prefetch, in_specs, operands = [], [], []
    if first or last:
        prefetch.append(ids)
    if parted:
        prefetch.append(side)
    if first or last:
        in_specs += mix_specs(width, tokens.shape[0]) + [whole((width,))] * 2
        operands += [patches, sel_table, tokens, *norm]
    if last:
        in_specs += [whole((width,))] * 2
        operands += list(after)
    if not first:
        in_specs += [image_spec(width)] * 2
        operands += [x, part]
    in_specs += [whole(weight.shape), whole(out.shape), small_spec(small)]
    in_specs += [whole((heads,) + bias.shape[1:], turn), image_spec(1)]
    operands += [weight, out, small[0], bias, mask]
    outs = [
        (in_hbm((images, SEQ, 3 * own), BF), image_spec(3 * own)),
        (
            in_hbm((images, heads, SEQ, SEQ), BF),
            pl.BlockSpec((1, heads, SEQ, SEQ), lambda i, *_: (i, 0, 0, 0)),
        ),
        (in_hbm((images, SEQ, own), BF), image_spec(own)),
        (shaped(patches.shape, F32), image_spec(width)),
    ]
    if first:
        outs = [(in_hbm(patches.shape, BF), image_spec(width))] + outs
    if last:
        outs += [
            (shaped(patches.shape, F32), image_spec(width)),
            (shaped(patches.shape, BF), image_spec(width)),
        ]
    if parted:
        outs.append((in_hbm((4 * own, width), BF), resident((4 * own, width))))
    return pl.pallas_call(
        functools.partial(attend_kernel, first, last, parted),
        out_shape=[shape for shape, _ in outs],
        grid_spec=pltpu.PrefetchScalarGridSpec(
            num_scalar_prefetch=len(prefetch),
            grid=(images,),
            in_specs=in_specs,
            out_specs=[spec for _, spec in outs],
        ),
        compiler_params=params(14),
        cost_estimate=cost(9),
        name="attend",
    )(*prefetch, *placed(operands, [part, bias]))


def shard_backward(
    x, grad, joint_ref, probs_ref, context_ref, weight_ref, out_ref, total_ref, sums_ref, acc_ref,
    joint_grad_ref, base,
):
    width = joint_ref.shape[2]
    own = width // 3
    low = lower_lanes()
    high = jnp.logical_not(low)
    grad_context = dot_nt(grad, out_ref[...]).astype(BF)
    d0, d1 = grad_context[:, :LANES], grad_context[:, LANES:]
    joint = joint_ref[0]
    b3 = block(joint, 3)
    t0, t1, t2 = turned(block(joint, 0)), turned(block(joint, 1)), turned(block(joint, 2))
    left = [only(low, b3), only(high, b3), joint[:, 4 * LANES :]]
    right = [d0, d0, d1]
    queries = [t0, t0, t1]
    keys = [t1, t2, t2]
    grads_q, grads_k, grads_v = [], [], []
    for head in range(3):
        probs = probs_ref[0, base + head]
        wide = probs.astype(F32)
        grad_probs = dot_nt(left[head], right[head])
        centre = jnp.sum(wide * grad_probs, axis=0, keepdims=True)
        grad_scores = (wide * (grad_probs - centre)).astype(BF)
        total_ref[base + head] += grad_scores.astype(F32)
        grads_v.append(dot_nn(probs, right[head]))
        grads_k.append(dot_nn(grad_scores, queries[head]))
        grads_q.append(dot_tn(grad_scores, keys[head]))
    scale = HEAD**-0.5
    blocks = [
        jnp.where(low, grads_q[0], grads_q[1]) * scale,
        jnp.where(low, grads_q[2] * scale, grads_k[0]),
        jnp.where(low, grads_k[1], grads_k[2]),
        jnp.where(low, grads_v[0], grads_v[1]),
        grads_v[2],
    ]
    for at, values in enumerate(blocks):
        cols = slice(at * LANES, at * LANES + values.shape[1])
        held = values.astype(BF)
        joint_grad_ref[:, cols] = held
        sums_ref[:, cols] += fold(held.astype(F32))
    joint_grad = joint_grad_ref[...]
    acc_ref[:width, :] += dot_tn(joint_grad, x)
    acc_ref[width:, :] += dot_tn(context_ref[0], grad)
    return dot_nn(joint_grad, weight_ref[...])


def attend_back_kernel(first, last, *refs):
    if last:
        ids_ref, patch_ref, sel_ref, token_ref, gmiddle_ref, gain_ref = refs[:6]
        refs = refs[6:]
    else:
        refs = refs[1:]
    if not first:
        carried_ref, refs = refs[0], refs[1:]
    x_ref, grad_ref, joint_ref, probs_ref, context_ref, weight_ref, out_ref = refs[:7]
    refs = refs[7:]
    g_ref, total_ref, sums_ref = refs[:3]
    refs = refs[3:]
    if last:
        patch_out_ref, norm_ref, token_out_ref, acc_ref, joint_grad_ref, carry_ref = refs
    else:
        carry_out_ref, acc_ref, joint_grad_ref = refs
    step = pl.program_id(0)

    @pl.when(step == 0)
    def _():
        for ref in (total_ref, sums_ref, acc_ref) + ((norm_ref,) if last else ()):
            ref[...] = jnp.zeros_like(ref)

    x = x_ref[0]
    part = shard_backward(
        x, grad_ref[0], joint_ref, probs_ref, context_ref, weight_ref, out_ref, total_ref, sums_ref,
        acc_ref, joint_grad_ref, 0,
    )
    if not first:
        part = part + carried_ref[0]
    if last:
        carry_ref[...] = part
        token = token_line(ids_ref, token_ref)
        token_sum = jnp.zeros((8, x.shape[1]), F32)
        for at in tiles():
            rows = slice(at, at + TILE)
            start, sel = mixed(patch_ref, sel_ref, token, at)
            xhat, scale = normalise(start)
            grad_normed = carry_ref[rows, :]
            norm_ref[0:8, :] += fold(grad_normed * xhat)
            norm_ref[8:16, :] += fold(grad_normed)
            grad_start = gmiddle_ref[0, rows, :] + normalise_back(
                grad_normed, line(gain_ref), xhat, scale
            )
            patch_out_ref[0, rows, :] = grad_start * (1.0 - sel)
            token_sum = token_sum + fold(grad_start * sel)
        token_out_ref[0] = token_sum
    else:
        carry_out_ref[0] = part

    @pl.when(step == pl.num_programs(0) - 1)
    def _():
        g_ref[...] = acc_ref[...].astype(BF)


def attend_back(ids, x, grad, joint, probs, turn, context, weight, out, carried, tail):
    images, _, width = x.shape
    joint_width = joint.shape[2]
    own = joint_width // 3
    heads = own // HEAD
    square = pl.BlockSpec((1, heads, SEQ, SEQ), lambda i, *_: (i, turn, 0, 0))
    first, last = carried is None, tail is not None
    in_specs = (
        [image_spec(width)] * 2
        + [image_spec(joint_width), square, image_spec(own)]
        + [whole((joint_width, width), weight[1]), whole((own, width), out[1])]
    )
    operands = [x, grad, joint, probs, context, weight[0], out[0]]
    if not first:
        in_specs = [image_spec(width)] + in_specs
        operands = [carried] + operands
    out_shape = [
        in_hbm((joint_width + own, width), BF),
        in_hbm((heads, SEQ, SEQ), F32),
        in_hbm((8, joint_width), F32),
    ]
    out_specs = [resident((joint_width + own, width)), resident((heads, SEQ, SEQ)), resident((8, joint_width))]
    scratch = [pltpu.VMEM((joint_width + own, width), F32), pltpu.VMEM((SEQ, joint_width), BF)]
    if last:
        patches, sel_table, tokens, grad_middle, gain = tail
        in_specs = (
            mix_specs(width, tokens.shape[0]) + [image_spec(width), whole((width,))] + in_specs
        )
        operands = [patches, sel_table, tokens, grad_middle, gain] + operands
        out_shape += [
            shaped(x.shape, F32), shaped((16, width), F32), shaped((images, 8, width), F32)
        ]
        out_specs += [
            image_spec(width),
            resident((16, width)),
            pl.BlockSpec((1, 8, width), lambda i, *_: (i, 0, 0)),
        ]
        scratch.append(pltpu.VMEM((SEQ, width), F32))
    else:
        out_shape.append(shaped(x.shape, F32))
        out_specs.append(image_spec(width))
    return pl.pallas_call(
        functools.partial(attend_back_kernel, first, last),
        out_shape=out_shape,
        grid_spec=pltpu.PrefetchScalarGridSpec(
            num_scalar_prefetch=1,
            grid=(images,),
            in_specs=in_specs,
            out_specs=out_specs,
            scratch_shapes=scratch,
        ),
        compiler_params=params(14),
        cost_estimate=cost(13),
        name="attend_back_last" if last else "attend_back",
    )(ids, *placed(operands, [carried, grad] + ([grad_middle] if last else [])))


MLP_MIB = 40


def mlp_kernel(first, lengths, *refs):
    refs = list(refs)

    def take(number):
        found = refs[:number]
        del refs[:number]
        return found

    count = len(lengths)
    (side_ref,) = take(1)
    x_ref, cot_ref, gamma_ref = take(3)
    shards = [take(length) for length in lengths]
    if not first:
        carried = take(2)
    totals = take(2)
    grads = take(count)
    upb_grad_ref, gm_ref, up_ref, down_ref, upb_ref, value_ref, grad_ref, sems = refs
    accs = (value_ref, grad_ref)
    step = pl.program_id(0)

    def moves(sources, targets):
        return [
            pltpu.make_async_copy(source, target, sems.at[at])
            for at, (source, target) in enumerate(zip(sources, targets))
        ]

    @pl.when(step == 0)
    def _():
        if first:
            for ref in accs:
                ref[...] = jnp.zeros_like(ref)
        else:
            for move in moves(carried, accs):
                move.start()
        gm_ref[...] = (line(gamma_ref) * cot_ref[...].astype(F32)).astype(BF)

    for at, shard in enumerate(shards):
        @pl.when(step == at)
        def _():
            up_ref[...] = shard[0][...]
            upb_ref[...] = shard[-1][...].astype(F32)[1:2, :]
            if len(shard) == 3:
                down_ref[...] = shard[1][...]

        if len(shard) == 4:
            half = shard[1].shape[1]
            for side in range(2):
                @pl.when(jnp.logical_and(step == at, side_ref[0] == side))
                def _():
                    down_ref[:, side * half : (side + 1) * half] = shard[1][...]
                    down_ref[:, (1 - side) * half : (2 - side) * half] = shard[2][...]

    x = x_ref[...]
    gm = gm_ref[...]
    before = dot_nn(x, up_ref[...]) + upb_ref[...]
    share = 0.5 + 0.5 * lax.erf(before * (0.5**0.5))
    density = jnp.exp(before * before * -0.5) * ((2.0 * jnp.pi) ** -0.5)
    hidden = (before * share).astype(BF)
    slope = share + before * density
    grad_before = (dot_nt(gm, down_ref[...]) * slope).astype(BF)
    upb_grad_ref[...] = fold(grad_before.astype(F32))
    down_grad = dot_tn(hidden, gm).astype(BF)
    up_grad = dot_tn(x, grad_before).astype(BF)
    for at, grads_ref in enumerate(grads):
        @pl.when(step == at)
        def _():
            grads_ref[: x.shape[1], :] = up_grad
            grads_ref[x.shape[1] :, :] = down_grad

    if not first:
        @pl.when(step == 0)
        def _():
            for move in moves(carried, accs):
                move.wait()

    value_ref[...] += dot_nn(hidden, down_ref[...])
    grad_ref[...] += dot_nt(grad_before, up_ref[...])

    @pl.when(step == count - 1)
    def _():
        for move in moves(accs, totals):
            move.start()
        for move in moves(accs, totals):
            move.wait()


def mlp(x, cot, gamma, shards, carried, side):
    rows, width = x.shape
    hidden = shards[0][0].shape[1]
    first = carried is None
    count = len(shards)
    anywhere = pl.BlockSpec(memory_space=pl.ANY)
    in_specs = [whole((rows, width)), whole((rows, width)), whole((width,))]
    operands = [x, cot, gamma]
    for shard in shards:
        in_specs += [whole(item.shape) for item in shard[:-1]] + [small_spec(shard[-1])]
        operands += list(shard[:-1]) + [shard[-1][0]]
    aliases = {}
    if not first:
        at = len(operands) + 1
        aliases = {at: 0, at + 1: 1}
        in_specs += [anywhere] * 2
        operands += list(carried)
    total = shaped((rows, width), F32)
    grads = [in_hbm((width + hidden, width), BF)]
    grad_specs = [whole((width + hidden, width))]
    return pl.pallas_call(
        functools.partial(mlp_kernel, first, [len(shard) for shard in shards]),
        out_shape=[total, total] + grads * count + [shaped((8 * count, hidden), F32)],
        grid_spec=pltpu.PrefetchScalarGridSpec(
            num_scalar_prefetch=1,
            grid=(count,),
            in_specs=in_specs,
            out_specs=[anywhere] * 2
            + grad_specs * count
            + [pl.BlockSpec((8, hidden), lambda i, *_: (i, 0))],
            scratch_shapes=[
                pltpu.VMEM((rows, width), BF),
                pltpu.VMEM((width, hidden), BF),
                pltpu.VMEM((hidden, width), BF),
                pltpu.VMEM((1, hidden), F32),
                pltpu.VMEM((rows, width), F32),
                pltpu.VMEM((rows, width), F32),
                pltpu.SemaphoreType.DMA((2,)),
            ],
        ),
        input_output_aliases=aliases,
        compiler_params=params(MLP_MIB),
        cost_estimate=cost(9 * count),
        name="mlp",
    )(side, *placed(operands, [x] + list(carried or [])))


def middle_back_kernel(
    value_ref, grad_ref, middle_ref, attn_ref, cot_ref, dbias_ref, gmlp_ref, gattn_ref, gain_ref,
    out_ref, gmiddle_ref, gattn_out_ref, sums_ref,
):
    @pl.when(pl.program_id(0) == 0)
    def _():
        sums_ref[...] = jnp.zeros_like(sums_ref)

    def add(row, values):
        sums_ref[8 * row : 8 * row + 8, :] += fold(values)

    for at in tiles():
        rows = slice(at, at + TILE)
        value = value_ref[0, rows, :] + line(dbias_ref)
        cot = cot_ref[0, rows, :].astype(F32)
        middle = middle_ref[0, rows, :]
        out_ref[0, rows, :] = (middle + line(gmlp_ref) * value).astype(BF)
        add(0, cot * value)
        add(1, (line(gmlp_ref) * cot).astype(BF).astype(F32))
        xhat, scale = normalise(middle)
        grad = grad_ref[0, rows, :]
        add(2, grad * xhat)
        add(3, grad)
        grad_middle = cot + normalise_back(grad, line(gain_ref), xhat, scale)
        gmiddle_ref[0, rows, :] = grad_middle
        add(4, grad_middle * attn_ref[0, rows, :])
        grad_attn = (line(gattn_ref) * grad_middle).astype(BF)
        gattn_out_ref[0, rows, :] = grad_attn
        add(5, grad_attn.astype(F32))


def middle_back(value, grad, middle, attn, cot, vectors):
    images, _, width = middle.shape
    return pl.pallas_call(
        middle_back_kernel,
        out_shape=(
            shaped(middle.shape, BF),
            shaped(middle.shape, F32),
            shaped(middle.shape, BF),
            shaped((48, width), F32),
        ),
        grid=(images,),
        in_specs=[image_spec(width)] * 5 + [whole((width,))] * 4,
        out_specs=(image_spec(width),) * 3 + (resident((48, width)),),
        compiler_params=params(12),
        cost_estimate=cost(5),
        name="middle_back",
    )(*placed([value, grad, middle, attn, cot, *vectors], [value, grad, middle, attn]))


def swap(values, axis, mask):
    count = lax.axis_size(axis)
    return lax.ppermute(values, axis, [(i, i ^ mask) for i in range(count)])


def dp_masks():
    count = lax.axis_size("dp")
    return [1 << bit for bit in range(count.bit_length() - 1)]


def pinned(value, *others):
    return lax.optimization_barrier((value,) + others)[0]


def plus(left, right):
    return (left.astype(F32) + right.astype(F32)).astype(BF)


ORDERS = ((0, 1), (1, 2))


def axis_bits():
    place = lax.axis_index("dp")
    return jnp.stack([(place >> bit) & 1 for bit in range(len(dp_masks()))]).astype(jnp.int32)


def halves_of(ref, base, size, bit):
    keep = pl.multiple_of(base + bit * size, 16)
    sent = pl.multiple_of(base + (1 - bit) * size, 16)
    return ref[pl.ds(keep, size), :], ref[pl.ds(sent, size), :]


def split_kernel(bits_ref, a_ref, b_ref, c_ref, *refs):
    outs, total_ref = refs[:4], refs[4]
    for at in range(0, total_ref.shape[0], 64):
        rows = slice(at, at + 64)
        total_ref[rows, :] = (
            a_ref[rows, :].astype(F32) + b_ref[rows, :].astype(F32) + c_ref[rows, :].astype(F32)
        ).astype(BF)
    part = total_ref.shape[0] // 2
    for which in range(2):
        keep, sent = halves_of(total_ref, which * part, part // 2, bits_ref[ORDERS[which][0]])
        outs[2 * which][...] = keep
        outs[2 * which + 1][...] = sent


def again_kernel(bits_ref, *refs):
    ins, outs, totals = refs[:4], refs[4:8], refs[8:]
    for which in range(2):
        total_ref = totals[which]
        total_ref[...] = plus(ins[2 * which][...], ins[2 * which + 1][...])
        size = total_ref.shape[0] // 2
        keep, sent = halves_of(total_ref, 0, size, bits_ref[ORDERS[which][1]])
        outs[2 * which][...] = keep
        outs[2 * which + 1][...] = sent


def both_kernel(bits_ref, *refs):
    for which in range(2):
        refs[4 + which][...] = plus(refs[2 * which][...], refs[2 * which + 1][...])


def put(out_ref, base, own, other, bit):
    size = own.shape[0]
    out_ref[pl.ds(pl.multiple_of(base + bit * size, 16), size), :] = own.astype(out_ref.dtype)
    out_ref[pl.ds(pl.multiple_of(base + (1 - bit) * size, 16), size), :] = other.astype(out_ref.dtype)


def grow_kernel(bits_ref, *refs):
    for which in range(2):
        put(refs[4 + which], 0, refs[2 * which][...], refs[2 * which + 1][...], bits_ref[ORDERS[which][1]])


def whole_kernel(bits_ref, *refs):
    ins, (*out_refs, total_ref) = refs[:4], refs[4:]
    part = total_ref.shape[0] // 2
    for which in range(2):
        put(total_ref, which * part, ins[2 * which][...], ins[2 * which + 1][...], bits_ref[ORDERS[which][0]])
    base = 0
    for out_ref in out_refs:
        out_ref[...] = total_ref[base : base + out_ref.shape[0], :].astype(F32)
        base += out_ref.shape[0]


def step_call(kernel, bits, arrays, outs, scratch, name):
    vmem = pl.BlockSpec(memory_space=pltpu.VMEM)
    return pl.pallas_call(
        kernel,
        out_shape=outs,
        in_specs=[pl.BlockSpec(memory_space=pltpu.SMEM)] + [vmem] * len(arrays),
        out_specs=[vmem] * len(outs),
        scratch_shapes=scratch,
        compiler_params=params(12, 0),
        cost_estimate=cost(1),
        name=name,
    )(bits, *arrays)


def dp_chain(pieces, sizes):
    bits = axis_bits()
    masks = dp_masks()
    rows, width = pieces[0].shape
    quarter, eighth = shaped((rows // 4, width), BF), shaped((rows // 8, width), BF)
    rest = [[axis for axis in range(len(masks)) if axis not in order] for order in ORDERS]

    def send(a, b, axes):
        return [swap(array, "dp", masks[axis]) for array, axis in zip((a, b), axes)]

    a, a_sent, b, b_sent = step_call(
        split_kernel, bits, placed(pieces), [quarter] * 4, [pltpu.VMEM((rows, width), BF)], "dp_split"
    )
    a_got, b_got = yield send(a_sent, b_sent, [ORDERS[0][0], ORDERS[1][0]])
    a, a_sent, b, b_sent = step_call(
        again_kernel, bits, [a, a_got, b, b_got], [eighth] * 4,
        [pltpu.VMEM((rows // 4, width), BF)] * 2, "dp_again",
    )
    a_got, b_got = yield send(a_sent, b_sent, [ORDERS[0][1], ORDERS[1][1]])
    a, b = step_call(both_kernel, bits, [a, a_got, b, b_got], [eighth] * 2, [], "dp_both")
    for axes in zip(*rest):
        a_got, b_got = yield send(a, b, axes)
        a, b = step_call(both_kernel, bits, [a, a_got, b, b_got], [eighth] * 2, [], "dp_both")
    a_got, b_got = yield send(a, b, [ORDERS[0][1], ORDERS[1][1]])
    a, b = step_call(grow_kernel, bits, [a, a_got, b, b_got], [quarter] * 2, [], "dp_grow")
    a_got, b_got = yield send(a, b, [ORDERS[0][0], ORDERS[1][0]])
    return step_call(
        whole_kernel, bits, [a, a_got, b, b_got],
        [shaped((size, width), F32) for size in sizes], [pltpu.VMEM((rows, width), BF)], "dp_whole",
    )


class Chain:
    def __init__(self, pieces, sizes):
        self.steps = dp_chain(pieces, sizes)
        self.done = None
        self.got = next(self.steps)

    def go_on(self):
        try:
            self.got = self.steps.send(self.got)
        except StopIteration as stop:
            self.done, self.got = stop.value, []


def wait_for(value, *chains):
    flat = [item for chain in chains for item in chain.got]
    value, *flat = lax.optimization_barrier((value, *flat))
    for chain in chains:
        chain.got, flat = flat[: len(chain.got)], flat[len(chain.got) :]
    return value


def collect_kernel(ids_ref, sums2_ref, sums1_ref, tokens_ref, table0_ref, table1_ref, *refs):
    upb_refs, joint_refs, (out_ref, sent_ref) = refs[:2], refs[2:5], refs[5:]
    upb_lines = [upb_refs[1][8:16, :], upb_refs[0][0:8, :], upb_refs[1][0:8, :], upb_refs[0][8:16, :]]
    out_ref[...] = jnp.zeros_like(out_ref)
    sent_ref[...] = jnp.zeros_like(sent_ref)
    table = table0_ref[...] + table1_ref[...]

    def total(values):
        return jnp.sum(values, axis=0, keepdims=True)

    lines = [total(sums2_ref[8 * i : 8 * i + 8, :]) for i in range(6)]
    lines += [total(sums1_ref[8 * i : 8 * i + 8, :]) for i in range(2)]
    images = [total(tokens_ref[i]) for i in range(tokens_ref.shape[0])]
    for group in range(GROUPS):
        found = jnp.zeros_like(images[0])
        for at, values in enumerate(images):
            found = found + jnp.where(ids_ref[at] == group, values, 0.0)
        lines.append(found)
    for at, values in enumerate(lines):
        out_ref[8 + at : 9 + at, :] = values
        sent_ref[8 + at : 9 + at, :] = values
    hidden = upb_refs[0].shape[1]
    for which in range(4):
        ref = out_ref if which % 2 == 0 else sent_ref
        base = 0 if which < 2 else 24
        ref[base : base + 1, :hidden] = total(upb_lines[which])
        if which < 3:
            joint = total(joint_refs[which][...])
            ref[base + 1 : base + 2, : joint.shape[1]] = joint
        per = table.shape[0] // (out_ref.shape[1] // LANES)
        own = per // 4
        for chunk in range(out_ref.shape[1] // LANES):
            ref[base + 2 : base + 2 + own, chunk * LANES : (chunk + 1) * LANES] = table[
                chunk * per + which * own : chunk * per + (which + 1) * own, :
            ]


def collect(ids, sums2, sums1, tokens, tables, upbs, joints):
    width = sums2.shape[1]
    vmem = pl.BlockSpec(memory_space=pltpu.VMEM)
    return pl.pallas_call(
        collect_kernel,
        out_shape=(shaped((32, width), F32), shaped((32, width), F32)),
        in_specs=[pl.BlockSpec(memory_space=pltpu.SMEM)] + [vmem] * 10,
        out_specs=(vmem, vmem),
        cost_estimate=cost(1),
        name="collect",
    )(ids, *placed([sums2, sums1, tokens, *tables, *upbs, *joints], [sums1, tokens, *tables]))


def emit_kernel(held_ref, got_ref, *outs):
    own = outs[9].shape[0]
    value = held_ref[...] + got_ref[...]
    for at in range(8):
        outs[at][...] = value[8 + at : 9 + at, :].reshape(-1)
    outs[8][...] = value[16:24, :]
    outs[9][...] = value[1:2, :own].reshape(-1)
    outs[10][...] = value[1:2, 2 * own : 3 * own].reshape(-1)
    outs[11][...] = value[2 : 2 + outs[11].shape[0], : outs[11].shape[1]]
    outs[12][...] = value[0:1, : outs[12].shape[0]].reshape(-1)


def emit(held, got, own, table_shape, hidden):
    width = held.shape[1]
    return pl.pallas_call(
        emit_kernel,
        out_shape=[shaped((width,), F32)] * 8
        + [
            shaped((GROUPS, width), F32),
            shaped((own,), F32),
            shaped((own,), F32),
            shaped(table_shape, F32),
            shaped((hidden,), F32),
        ],
        cost_estimate=cost(1),
        name="emit",
    )(held, got)


def local(
    patches, dataset_id, patch_masks, mask_tokens, key_mask, bias_index, norm1_gain, norm1_shift,
    qkv_weight, query_bias, value_bias, bias_table, out_weight, out_bias, gamma_attn, norm2_gain,
    norm2_shift, up_weight, up_bias, down_weight, down_bias, gamma_mlp, cotangent,
):
    rows, width = patches.shape
    images = rows // SEQ
    place = lax.axis_index("mp")
    own = qkv_weight.shape[2]
    own_heads = own // HEAD
    table_rows = bias_table.shape[0]
    chunks = width // LANES
    hidden = up_weight.shape[1]

    ids = lax.dynamic_slice_in_dim(dataset_id, place * images, images, 0)
    keys_here = lax.dynamic_slice_in_dim(key_mask, place * images, images, 0)
    mask = jnp.where(keys_here > 0, 0.0, -1e30).astype(F32)[:, :, None]
    sel_table = patch_masks.astype(F32)[:, :, None]
    images3 = patches.reshape(images, SEQ, width)
    cot3 = cotangent.reshape(images, SEQ, width)
    index = bias_index.T
    index_wide = jnp.pad(index, ((0, 0), (0, 2 * LANES - SEQ)))
    mix = (ids, images3, sel_table, mask_tokens)

    parity = lax.axis_index("dp") & 1
    side = parity.reshape(1)
    qkv_own = qkv_weight.transpose(1, 2, 0).reshape(3 * own, width)
    small, attn_half, down_half = prepare(
        side, qkv_own, out_weight, down_weight, query_bias, value_bias, up_bias, bias_table.T
    )
    small0, small1 = (small, 0), (swap(small, "mp", 1), 0)
    attn_p2 = swap(attn_half, "mp", 2)
    down_p2 = swap(down_half, "mp", 2)
    qkv1, out1 = swap(qkv_own, "mp", 1), swap(out_weight, "mp", 1)
    bias_near = position_bias([small0, small1], 2 * own_heads, index_wide)
    up2 = swap(pinned(up_weight, bias_near), "mp", 2)
    up1, down1 = swap(up_weight, "mp", 1), swap(down_weight, "mp", 1)

    norm1 = [norm1_gain, norm1_shift]
    x1, j0, probs0, c0, part = attend(
        mix, norm1, qkv_own, out_weight, small0, bias_near, 0, mask
    )
    part, attn_p2 = lax.optimization_barrier((part, attn_p2))
    attn_q2 = swap(attn_p2, "dp", 1)
    attn_p3 = swap(attn_p2, "mp", 1)
    small2, small3 = (attn_p2, 2 * own // SMALL_ROWS), (attn_p3, 2 * own // SMALL_ROWS)
    j1, probs1, c1, part = attend(mix, norm1, qkv1, out1, small1, bias_near, 1, mask, x1, part)
    part, attn_q2, down_p2 = lax.optimization_barrier((part, attn_q2, down_p2))
    attn_q3 = swap(attn_q2, "mp", 1)
    down_q2 = swap(down_p2, "dp", 1)
    bias_far = position_bias([small2, small3], 2 * own_heads, pinned(index_wide, part))
    j2, probs2, c2, part, pack2 = attend(
        mix, norm1, attn_p2, attn_q2, small2, bias_far, 0, mask, x1, part, side
    )
    part, down_q2 = lax.optimization_barrier((part, down_q2))
    down_p3, down_q3 = swap(down_p2, "mp", 1), swap(down_q2, "mp", 1)
    j3, probs3, c3, attn_value, middle, normed2, pack3 = attend(
        mix, [norm2_gain, norm2_shift], attn_p3, attn_q3, small3, bias_far, 1, mask, x1, part, side,
        [out_bias, gamma_attn],
    )

    x2 = normed2.reshape(rows, width)
    x2, up2 = lax.optimization_barrier((x2, up2))
    up3 = swap(up2, "mp", 1)
    value, grad2, m1, m3, upb13 = mlp(
        x2, cotangent, gamma_mlp, [(up1, down1, small1), (up3, down_p3, down_q3, small3)], None, side
    )
    mr1, mr3 = swap(m1, "mp", 1), swap(m3, "mp", 1)
    value, grad2, m2, m0, upb20 = mlp(
        x2, cotangent, gamma_mlp,
        [(up2, down_p2, down_q2, small2), (up_weight, down_weight, small0)], (value, grad2), side,
    )
    mlp_far = plus(m2, mr3)
    value, mlp_far, mr1 = lax.optimization_barrier((value, mlp_far, mr1))
    mr2 = swap(mlp_far, "mp", 2)

    shape3 = (images, SEQ, width)
    output, grad_middle, grad_attn, sums2 = middle_back(
        value.reshape(shape3), grad2.reshape(shape3), middle, attn_value, cot3,
        [down_bias, gamma_mlp, gamma_attn, norm2_gain],
    )

    g3, total3, js3, carried = attend_back(
        ids, x1, grad_attn, j3, probs3, 0, c3, (pack3, 0), (pack3, 3), None, None
    )
    r3 = swap(g3, "mp", 1)
    g2, total2, js2, carried = attend_back(
        ids, x1, grad_attn, j2, probs2, 0, c2, (pack2, 0), (pack2, 3), carried, None
    )
    far = plus(g2, r3)
    carried, far, js3 = lax.optimization_barrier((carried, far, js3))
    r2 = swap(far, "mp", 2)
    js2 = js2 + swap(js3, "mp", 1)
    g1, total1, js1, carried = attend_back(
        ids, x1, grad_attn, j1, probs1, 0, c1, (qkv1, 0), (out1, 0), carried, None
    )
    r1 = swap(g1, "mp", 1)
    mlp_sum = (m0.astype(F32) + mr1.astype(F32) + mr2.astype(F32)).astype(BF)
    carried, js2, mlp_sum = lax.optimization_barrier((carried, js2, mlp_sum))
    mlp_sum = lax.psum(mlp_sum, "dp")
    g0, total0, js0, patch_grad, sums1, token_images = attend_back(
        ids, x1, grad_attn, j0, probs0, 0, c0, (qkv_own, 0), (out_weight, 0), carried,
        (images3, sel_table, mask_tokens, grad_middle, norm1_gain),
    )
    totals = [total0, total1, total2, total3]
    blocks = SEQ // TABLE_ROWS
    g0, r1, r2 = lax.optimization_barrier((g0, r1, r2))
    tail_chain = Chain([g0, r1, r2], [3 * own, own])
    tables = [table_sums(totals, index, chunks, 0, blocks // 2)]
    index = wait_for(pinned(index, tables[0]), tail_chain)
    tail_chain.go_on()
    tables.append(table_sums(totals, index, chunks, blocks // 2, blocks - blocks // 2))
    sums1 = wait_for(pinned(sums1, tables[1]), tail_chain)
    while tail_chain.done is None:
        tail_chain.go_on()
    qkv_sum, out_sum = tail_chain.done
    up_sum, down_sum = mlp_sum[:width].astype(F32), mlp_sum[width:].astype(F32)

    held, sent = collect(
        ids, sums2, sums1, token_images, tables, [upb13, upb20], [js0, js1, js2]
    )
    held = held + swap(sent, "mp", 1)
    sent = jnp.concatenate([held[24:], held[8:24]], axis=0)
    held = held[:24] + swap(sent, "mp", 2)
    masks = dp_masks()
    for shift in masks[:-1]:
        held = held + swap(held, "dp", shift)
    (
        gamma_mlp_grad, down_bias_grad, gain2_grad, shift2_grad, gamma_attn_grad, out_bias_grad,
        gain1_grad, shift1_grad, token_grad, qb_grad, vb_grad, table_grad, upb_grad,
    ) = emit(held, swap(held, "dp", masks[-1]), own, (own_heads, table_rows), hidden)

    return (
        output.reshape(rows, width),
        patch_grad.reshape(rows, width),
        token_grad,
        gain1_grad,
        shift1_grad,
        qkv_sum.reshape(3, own, width).transpose(2, 0, 1),
        qb_grad,
        vb_grad,
        table_grad.T,
        out_sum,
        out_bias_grad,
        gamma_attn_grad,
        gain2_grad,
        shift2_grad,
        up_sum,
        upb_grad,
        down_sum,
        down_bias_grad,
        gamma_mlp_grad,
    )


def solution(mesh):
    return jax.shard_map(
        local,
        mesh=mesh,
        in_specs=(
            P(("dp", "mp"), None), P("dp"), P(), P(), P("dp", None), P(), P(), P(),
            P(None, None, "mp"), P("mp"), P("mp"), P(None, "mp"), P("mp", None), P(), P(), P(), P(),
            P(None, "mp"), P("mp"), P("mp", None), P(), P(), P(("dp", "mp"), None),
        ),
        out_specs=(
            P(("dp", "mp"), None), P(("dp", "mp"), None), P(), P(), P(), P(None, None, "mp"),
            P("mp"), P("mp"), P(None, "mp"), P("mp", None), P(), P(), P(), P(), P(None, "mp"),
            P("mp"), P("mp", None), P(), P(),
        ),
        check_vma=False,
    )
```

```python
import functools

import jax
import jax.numpy as jnp
from jax import lax
from jax.experimental import pallas as pl
from jax.experimental.pallas import tpu as pltpu
from jax.sharding import PartitionSpec as P

HEAD = 64
SEQ = 200
GROUPS = 8
LANES = 128
BF = jnp.bfloat16
F32 = jnp.float32


def dot_nn(left, right):
    return lax.dot_general(left, right, (((1,), (0,)), ((), ())), preferred_element_type=F32)


def dot_nt(left, right):
    return lax.dot_general(left, right, (((1,), (1,)), ((), ())), preferred_element_type=F32)


def dot_tn(left, right):
    return lax.dot_general(left, right, (((0,), (0,)), ((), ())), preferred_element_type=F32)


def params(mib, steps=1):
    return pltpu.CompilerParams(
        dimension_semantics=("arbitrary",) * steps, vmem_limit_bytes=mib << 20
    )


def cost(micros):
    return pl.CostEstimate(flops=int(micros * 1.1e8), transcendentals=0, bytes_accessed=0)


def whole(shape, at=0):
    zeros = (0,) * (len(shape) - 1)
    return pl.BlockSpec(shape, lambda *_: (at,) + zeros, pipeline_mode=pl.Buffered(1))


def image_spec(width):
    return pl.BlockSpec((1, SEQ, width), lambda i, *_: (i, 0, 0))


def resident(shape):
    zeros = (0,) * len(shape)
    return pl.BlockSpec(shape, lambda *_: zeros)


def placed(operands, keep=()):
    return [
        item
        if any(item is kept for kept in keep)
        else pltpu.with_memory_space_constraint(item, pltpu.HBM)
        for item in operands
    ]


def in_hbm(shape, dtype):
    return pltpu.HBM(tuple(shape), dtype)


def shaped(shape, dtype):
    return jax.ShapeDtypeStruct(shape, dtype)


TILE = 40


def normalise(values):
    mean = jnp.mean(values, axis=-1, keepdims=True)
    centred = values - mean
    spread = jnp.mean(centred * centred, axis=-1, keepdims=True)
    scale = lax.rsqrt(spread + 1e-06)
    return centred * scale, scale


def normalise_back(grad, gain, xhat, scale):
    u = grad * gain
    return (
        u - jnp.mean(u, axis=-1, keepdims=True) - xhat * jnp.mean(u * xhat, axis=-1, keepdims=True)
    ) * scale


def line(ref):
    return ref[...].reshape(1, -1)


def token_line(ids_ref, token_ref):
    tokens = token_ref[...].astype(F32)
    group = lax.broadcasted_iota(jnp.int32, tokens.shape, 0)
    return jnp.sum(jnp.where(group == ids_ref[pl.program_id(0)], tokens, 0.0), axis=0, keepdims=True)


def mixed(patch_ref, sel_ref, token, at):
    sel = sel_ref[0, at : at + TILE, :]
    return patch_ref[0, at : at + TILE, :].astype(F32) * (1.0 - sel) + sel * token, sel


def tiles():
    return range(0, SEQ, TILE)


def fold(values):
    return jnp.sum(values.reshape(values.shape[0] // 8, 8, values.shape[1]), axis=0)


SMALL_ROWS = 16


def prepare_kernel(
    side_ref, qkv_ref, out_ref, down_ref, qb_ref, vb_ref, upb_ref, table_ref,
    small_ref, attn_ref, half_ref, pack_ref,
):
    own = qb_ref.shape[0]
    width = small_ref.shape[1]
    small_ref[...] = jnp.zeros_like(small_ref)
    small_ref[0:1, :own] = line(qb_ref)
    small_ref[0:1, 2 * own : 3 * own] = line(vb_ref)
    small_ref[1:2, : upb_ref.shape[0]] = line(upb_ref)
    small_ref[2 : 2 + table_ref.shape[0], : table_ref.shape[1]] = table_ref[...]
    attn_ref[2 * own :, :] = small_ref[...]
    pack_ref[: 3 * own, :] = qkv_ref[...]
    pack_ref[3 * own :, :] = out_ref[...]

    @pl.when(side_ref[0] == 0)
    def _():
        attn_ref[: 2 * own, :] = qkv_ref[: 2 * own, :]
        half_ref[...] = down_ref[:, : width // 2]

    @pl.when(side_ref[0] == 1)
    def _():
        attn_ref[:own, :] = qkv_ref[2 * own :, :]
        attn_ref[own : 2 * own, :] = out_ref[...]
        half_ref[...] = down_ref[:, width // 2 :]


def prepare(side, qkv, out, down, qb, vb, upb, table):
    width = out.shape[1]
    vmem = pl.BlockSpec(memory_space=pltpu.VMEM)
    return pl.pallas_call(
        prepare_kernel,
        out_shape=[
            shaped((SMALL_ROWS, width), BF),
            shaped((2 * qb.shape[0] + SMALL_ROWS, width), BF),
            shaped((down.shape[0], width // 2), BF),
            shaped((4 * qb.shape[0], width), BF),
        ],
        in_specs=[pl.BlockSpec(memory_space=pltpu.SMEM)] + [vmem] * 7,
        out_specs=[vmem] * 4,
        compiler_params=params(8, 0),
        cost_estimate=cost(2),
        name="prepare",
    )(side, *placed([qkv, out, down, qb, vb, upb, table]))


def bias_kernel(near_ref, far_ref, narrow_ref, out_ref, index_ref):
    own = out_ref.shape[0] // 2
    chunks = near_ref.shape[1] // LANES
    tables = (near_ref[...].astype(F32), far_ref[...].astype(F32))
    index_ref[...] = jnp.zeros_like(index_ref)
    index_ref[:, : narrow_ref.shape[1]] = narrow_ref[...]

    def rows_of(step, _):
        row = pl.multiple_of(step * 8, 8)
        for col in range(0, index_ref.shape[1], LANES):
            index = index_ref[pl.ds(row, 8), col : col + LANES]
            low = index & (LANES - 1)
            high = index >> 7
            for head in range(2 * own):
                table, at = tables[head // own], 2 + head % own
                found = jnp.zeros((8, LANES), F32)
                for chunk in range(chunks):
                    source = jnp.broadcast_to(
                        table[at : at + 1, chunk * LANES : (chunk + 1) * LANES], (8, LANES)
                    )
                    picked = jnp.take_along_axis(source, low, axis=1)
                    found = jnp.where(high == chunk, picked, found)
                out_ref[head, pl.ds(row, 8), col : col + LANES] = found
        return 0

    lax.fori_loop(0, SEQ // 8, rows_of, 0, unroll=5)


def small_spec(small):
    return whole((SMALL_ROWS, small[0].shape[1]), small[1])


def position_bias(small, heads, index):
    return pl.pallas_call(
        bias_kernel,
        out_shape=shaped((heads, SEQ, 2 * LANES), F32),
        grid=(1,),
        in_specs=[small_spec(item) for item in small] + [whole(index.shape)],
        out_specs=resident((heads, SEQ, 2 * LANES)),
        scratch_shapes=[pltpu.VMEM((SEQ, 2 * LANES), jnp.int32)],
        compiler_params=params(6),
        cost_estimate=cost(2),
        name="position_bias",
    )(*placed([item for item, _ in small] + [index]))


TABLE_ROWS = 8


def table_kernel(*refs):
    total_refs, (index_ref, out_ref) = refs[:-2], refs[-2:]

    @pl.when(pl.program_id(0) == 0)
    def _():
        out_ref[...] = jnp.zeros_like(out_ref)

    chunks = out_ref.shape[0] // sum(ref.shape[0] for ref in total_refs)
    spots = lax.broadcasted_iota(jnp.int32, (LANES, SEQ), 0)
    acc = jnp.zeros(out_ref.shape, F32)
    for row in range(TABLE_ROWS):
        index = index_ref[row : row + 1, :]
        hot = (spots == (index & (LANES - 1))).astype(F32).astype(BF)
        high = index >> 7
        total = jnp.concatenate([ref[:, row, :] for ref in total_refs], axis=0)
        parts = [jnp.where(high == chunk, total, 0.0) for chunk in range(chunks)]
        acc = acc + dot_nt(jnp.concatenate(parts, axis=0).astype(BF), hot)
    out_ref[...] += acc


def table_sums(totals, index, chunks, first, steps):
    own = totals[0][0].shape[0]
    heads = own * len(totals)
    return pl.pallas_call(
        table_kernel,
        out_shape=shaped((chunks * heads, LANES), F32),
        grid=(steps,),
        in_specs=[
            pl.BlockSpec((own, TABLE_ROWS, SEQ), lambda i, at=at: (at, first + i, 0))
            for _, at in totals
        ]
        + [pl.BlockSpec((TABLE_ROWS, SEQ), lambda i: (first + i, 0))],
        out_specs=resident((chunks * heads, LANES)),
        compiler_params=params(6),
        cost_estimate=cost(5),
        name="table_sums",
    )(*placed([total for total, _ in totals] + [index]))


def block(values, at):
    return values[:, at * LANES : (at + 1) * LANES]


def turned(values):
    return pltpu.roll(values, HEAD, 1)


def only(keep, values):
    return jnp.where(keep, values, jnp.zeros_like(values))


def lower_lanes():
    return lax.broadcasted_iota(jnp.int32, (SEQ, LANES), 1) < HEAD


def shard_forward(x, weight_ref, small_ref, bias_ref, mask, joint_ref, probs_ref, context_ref, base):
    width = joint_ref.shape[2]
    own = width // 3
    low = lower_lanes()
    high = jnp.logical_not(low)
    column = lax.broadcasted_iota(jnp.int32, (1, width), 1)
    scale = jnp.where(column < own, HEAD**-0.5, 1.0)
    joint = dot_nt(x, weight_ref[...])
    joint_ref[0] = ((joint + small_ref[...].astype(F32)[0:1, :width]) * scale).astype(BF)
    joint = joint_ref[0]
    b1, b2, b3 = block(joint, 1), block(joint, 2), block(joint, 3)
    t0, t1 = turned(block(joint, 0)), turned(b1)
    left = [only(high, b1), only(low, b2), only(high, b2)]
    right = [t0, t0, t1]
    value = [b3, b3, joint[:, 4 * LANES :]]
    heads = range(3)
    scores = [dot_nt(left[i], right[i]) + bias_ref[base + i][:, :SEQ] + mask for i in heads]
    raised = [jnp.exp(item - jnp.max(item, axis=0, keepdims=True)) for item in scores]
    probs = [(item * (1.0 / jnp.sum(item, axis=0, keepdims=True))).astype(BF) for item in raised]
    for i in heads:
        probs_ref[0, base + i] = probs[i]
    found = [dot_tn(probs[i], value[i]) for i in heads]
    context_ref[0, :, :LANES] = jnp.where(low, found[0], found[1]).astype(BF)
    context_ref[0, :, LANES:] = found[2].astype(BF)


def attend_kernel(first, last, parted, *refs):
    refs = list(refs)

    def take(count):
        found = refs[:count]
        del refs[:count]
        return found

    if first or last:
        (ids_ref,) = take(1)
    if parted:
        (side_ref,) = take(1)
    if first or last:
        patch_ref, sel_ref, token_ref, gain_ref, shift_ref = take(5)
    if last:
        obias_ref, gamma_ref = take(2)
    if not first:
        x_ref, part_in_ref = take(2)
    weight_ref, out_ref, small_ref, bias_ref, mask_ref = take(5)
    if first:
        (x_ref,) = take(1)
    joint_ref, probs_ref, context_ref, part_ref = take(4)
    if last:
        middle_ref, normed_ref = take(2)
    if parted:
        p_ref, q_ref = weight_ref, out_ref
        (pack_ref,) = take(1)
        half = p_ref.shape[0] - SMALL_ROWS

        @pl.when(pl.program_id(0) == 0)
        def _():
            for side in range(2):
                @pl.when(side_ref[0] == side)
                def _():
                    pack_ref[side * half : (side + 1) * half, :] = p_ref[:half, :]
                    pack_ref[(1 - side) * half : (2 - side) * half, :] = q_ref[:half, :]

        joint = joint_ref.shape[2]
        weight_ref, out_ref = pack_ref.at[:joint], pack_ref.at[joint:]
    if first:
        token = token_line(ids_ref, token_ref)
        for at in tiles():
            start, _ = mixed(patch_ref, sel_ref, token, at)
            xhat, _ = normalise(start)
            x_ref[0, at : at + TILE, :] = (xhat * line(gain_ref) + line(shift_ref)).astype(BF)
    shard_forward(
        x_ref[0], weight_ref, small_ref, bias_ref, mask_ref[0], joint_ref, probs_ref, context_ref, 0
    )
    part = dot_nn(context_ref[0], out_ref[...])
    part_ref[0] = part if first else part + part_in_ref[0]
    if last:
        token = token_line(ids_ref, token_ref)
        for at in tiles():
            rows = slice(at, at + TILE)
            start, _ = mixed(patch_ref, sel_ref, token, at)
            value = part_ref[0, rows, :] + line(obias_ref)
            middle = start + line(gamma_ref) * value
            xhat, _ = normalise(middle)
            part_ref[0, rows, :] = value
            middle_ref[0, rows, :] = middle
            normed_ref[0, rows, :] = (xhat * line(gain_ref) + line(shift_ref)).astype(BF)


def mix_specs(width, groups):
    return [
        image_spec(width),
        pl.BlockSpec((1, SEQ, 1), lambda i, ids, *_: (ids[i], 0, 0)),
        whole((groups, width)),
    ]


def attend(mix, norm, weight, out, small, bias, turn, mask, x=None, part=None, side=None, after=None):
    ids, patches, sel_table, tokens = mix
    images, _, width = patches.shape
    heads = bias.shape[0] // 2
    own = heads * HEAD
    first, last, parted = x is None, after is not None, side is not None
    prefetch, in_specs, operands = [], [], []
    if first or last:
        prefetch.append(ids)
    if parted:
        prefetch.append(side)
    if first or last:
        in_specs += mix_specs(width, tokens.shape[0]) + [whole((width,))] * 2
        operands += [patches, sel_table, tokens, *norm]
    if last:
        in_specs += [whole((width,))] * 2
        operands += list(after)
    if not first:
        in_specs += [image_spec(width)] * 2
        operands += [x, part]
    if parted:
        in_specs += [whole(weight.shape), whole(out.shape)]
    else:
        in_specs += [whole((3 * own, width)), whole((own, width), out[1])]
        out = out[0]
    in_specs += [small_spec(small)]
    in_specs += [whole((heads,) + bias.shape[1:], turn), image_spec(1)]
    operands += [weight, out, small[0], bias, mask]
    outs = [
        (in_hbm((images, SEQ, 3 * own), BF), image_spec(3 * own)),
        (
            in_hbm((images, heads, SEQ, SEQ), BF),
            pl.BlockSpec((1, heads, SEQ, SEQ), lambda i, *_: (i, 0, 0, 0)),
        ),
        (in_hbm((images, SEQ, own), BF), image_spec(own)),
        (shaped(patches.shape, F32), image_spec(width)),
    ]
    if first:
        outs = [(in_hbm(patches.shape, BF), image_spec(width))] + outs
    if last:
        outs += [
            (shaped(patches.shape, F32), image_spec(width)),
            (shaped(patches.shape, BF), image_spec(width)),
        ]
    if parted:
        outs.append((in_hbm((4 * own, width), BF), resident((4 * own, width))))
    return pl.pallas_call(
        functools.partial(attend_kernel, first, last, parted),
        out_shape=[shape for shape, _ in outs],
        grid_spec=pltpu.PrefetchScalarGridSpec(
            num_scalar_prefetch=len(prefetch),
            grid=(images,),
            in_specs=in_specs,
            out_specs=[spec for _, spec in outs],
        ),
        compiler_params=params(14),
        cost_estimate=cost(9),
        name="attend",
    )(*prefetch, *placed(operands, [part, bias]))


def shards_backward(x, grad, shards, total_ref):
    low = lower_lanes()
    high = jnp.logical_not(low)
    left, right, queries, keys, probs = [], [], [], [], []
    for joint_ref, probs_ref, _, _, out_ref, _, _, _ in shards:
        grad_context = dot_nt(grad, out_ref[...]).astype(BF)
        d0, d1 = grad_context[:, :LANES], grad_context[:, LANES:]
        joint = joint_ref[0]
        b3 = block(joint, 3)
        t0, t1, t2 = turned(block(joint, 0)), turned(block(joint, 1)), turned(block(joint, 2))
        left += [only(low, b3), only(high, b3), joint[:, 4 * LANES :]]
        right += [d0, d0, d1]
        queries += [t0, t0, t1]
        keys += [t1, t2, t2]
        probs += [probs_ref[0, i] for i in range(3)]
    heads = range(len(left))
    grad_probs = [dot_nt(left[i], right[i]) for i in heads]
    grads_v = [dot_nn(probs[i], right[i]) for i in heads]
    grad_scores = []
    for i in heads:
        wide = probs[i].astype(F32)
        centre = jnp.sum(wide * grad_probs[i], axis=0, keepdims=True)
        grad_scores.append((wide * (grad_probs[i] - centre)).astype(BF))
    for i in heads:
        total_ref[i] += grad_scores[i].astype(F32)
    grads_k = [dot_nn(grad_scores[i], queries[i]) for i in heads]
    grads_q = [dot_tn(grad_scores[i], keys[i]) for i in heads]
    scale = HEAD**-0.5
    part = None
    for which, (_, _, context_ref, weight_ref, _, sums_ref, acc_ref, joint_grad_ref) in enumerate(shards):
        gq, gk, gv = (items[3 * which : 3 * which + 3] for items in (grads_q, grads_k, grads_v))
        blocks = [
            jnp.where(low, gq[0], gq[1]) * scale,
            jnp.where(low, gq[2] * scale, gk[0]),
            jnp.where(low, gk[1], gk[2]),
            jnp.where(low, gv[0], gv[1]),
            gv[2],
        ]
        for at, values in enumerate(blocks):
            cols = slice(at * LANES, at * LANES + values.shape[1])
            held = values.astype(BF)
            joint_grad_ref[:, cols] = held
            sums_ref[:, cols] += fold(held.astype(F32))
        width = joint_grad_ref.shape[1]
        joint_grad = joint_grad_ref[...]
        acc_ref[:width, :] += dot_tn(joint_grad, x)
        acc_ref[width:, :] += dot_tn(context_ref[0], grad)
        own = dot_nn(joint_grad, weight_ref[...])
        part = own if part is None else part + own
    return part


def attend_back_kernel(first, last, count, *refs):
    refs = list(refs)

    def take(number):
        found = refs[:number]
        del refs[:number]
        return found

    (ids_ref,) = take(1)
    if last:
        patch_ref, sel_ref, token_ref, gmiddle_ref, gain_ref = take(5)
    if not first:
        (carried_ref,) = take(1)
    x_ref, grad_ref = take(2)
    inputs = [take(5) for _ in range(count)]
    outputs = [take(2) for _ in range(count)]
    (total_ref,) = take(1)
    if last:
        patch_out_ref, norm_ref, token_out_ref = take(3)
    else:
        (carry_out_ref,) = take(1)
    scratch = [take(2) for _ in range(count)]
    step = pl.program_id(0)

    @pl.when(step == 0)
    def _():
        zeroed = [total_ref] + [item[1] for item in outputs] + [item[0] for item in scratch]
        for ref in zeroed + ([norm_ref] if last else []):
            ref[...] = jnp.zeros_like(ref)

    shards = [
        (*ins, out[1], own[0], own[1]) for ins, out, own in zip(inputs, outputs, scratch)
    ]
    part = shards_backward(x_ref[0], grad_ref[0], shards, total_ref)
    if not first:
        part = part + carried_ref[0]
    if last:
        (carry_ref,) = refs
        carry_ref[...] = part
        token = token_line(ids_ref, token_ref)
        token_sum = jnp.zeros((8, part.shape[1]), F32)
        for at in tiles():
            rows = slice(at, at + TILE)
            start, sel = mixed(patch_ref, sel_ref, token, at)
            xhat, scale = normalise(start)
            grad_normed = carry_ref[rows, :]
            norm_ref[0:8, :] += fold(grad_normed * xhat)
            norm_ref[8:16, :] += fold(grad_normed)
            grad_start = gmiddle_ref[0, rows, :] + normalise_back(
                grad_normed, line(gain_ref), xhat, scale
            )
            patch_out_ref[0, rows, :] = grad_start * (1.0 - sel)
            token_sum = token_sum + fold(grad_start * sel)
        token_out_ref[0] = token_sum
    else:
        carry_out_ref[0] = part

    @pl.when(step == pl.num_programs(0) - 1)
    def _():
        for out, own in zip(outputs, scratch):
            out[0][...] = own[0][...].astype(BF)


def attend_back(ids, x, grad, shards, carried, tail):
    images, _, width = x.shape
    joint_width = shards[0][0].shape[2]
    own = joint_width // 3
    heads = own // HEAD
    count = len(shards)
    square = pl.BlockSpec((1, heads, SEQ, SEQ), lambda i, *_: (i, 0, 0, 0))
    first, last = carried is None, tail is not None
    in_specs = [image_spec(width)] * 2
    operands = [x, grad]
    for joint, probs, context, weight, weight_at, out, out_at in shards:
        in_specs += [image_spec(joint_width), square, image_spec(own)]
        in_specs += [whole((joint_width, width), weight_at), whole((own, width), out_at)]
        operands += [joint, probs, context, weight, out]
    if not first:
        in_specs = [image_spec(width)] + in_specs
        operands = [carried] + operands
    out_shape, out_specs, scratch = [], [], []
    for _ in shards:
        out_shape += [in_hbm((joint_width + own, width), BF), in_hbm((8, joint_width), F32)]
        out_specs += [resident((joint_width + own, width)), resident((8, joint_width))]
        scratch += [pltpu.VMEM((joint_width + own, width), F32), pltpu.VMEM((SEQ, joint_width), BF)]
    out_shape.append(in_hbm((count * heads, SEQ, SEQ), F32))
    out_specs.append(resident((count * heads, SEQ, SEQ)))
    if last:
        patches, sel_table, tokens, grad_middle, gain = tail
        in_specs = (
            mix_specs(width, tokens.shape[0]) + [image_spec(width), whole((width,))] + in_specs
        )
        operands = [patches, sel_table, tokens, grad_middle, gain] + operands
        out_shape += [
            shaped(x.shape, F32), shaped((16, width), F32), shaped((images, 8, width), F32)
        ]
        out_specs += [
            image_spec(width),
            resident((16, width)),
            pl.BlockSpec((1, 8, width), lambda i, *_: (i, 0, 0)),
        ]
        scratch.append(pltpu.VMEM((SEQ, width), F32))
    else:
        out_shape.append(in_hbm(x.shape, F32))
        out_specs.append(image_spec(width))
    return pl.pallas_call(
        functools.partial(attend_back_kernel, first, last, count),
        out_shape=out_shape,
        grid_spec=pltpu.PrefetchScalarGridSpec(
            num_scalar_prefetch=1,
            grid=(images,),
            in_specs=in_specs,
            out_specs=out_specs,
            scratch_shapes=scratch,
        ),
        compiler_params=params(14 if count == 1 else 24),
        cost_estimate=cost(13 * count),
        name="attend_back",
    )(ids, *placed(operands))


MLP_MIB = 40


def mlp_kernel(first, lengths, *refs):
    refs = list(refs)

    def take(number):
        found = refs[:number]
        del refs[:number]
        return found

    count = len(lengths)
    (side_ref,) = take(1)
    x_ref, cot_ref, gamma_ref = take(3)
    shards = [take(length) for length in lengths]
    if not first:
        carried = take(2)
    totals = take(2)
    grads = take(count)
    upb_grad_ref, gm_ref, up_ref, down_ref, held_ref, value_ref, grad_ref, in_sem, out_sem, sem = refs
    accs = (value_ref, grad_ref)
    step = pl.program_id(0)

    def moves(sources, targets, sems):
        return [
            pltpu.make_async_copy(source, target, sems.at[at])
            for at, (source, target) in enumerate(zip(sources, targets))
        ]

    def weights(at):
        shard = shards[at]
        if len(shard) == 3:
            targets = [up_ref.at[at], down_ref.at[at]]
        else:
            half = shard[1].shape[1]
            places = [
                pl.ds(pl.multiple_of(place * half, LANES), half)
                for place in (side_ref[0], 1 - side_ref[0])
            ]
            targets = [up_ref.at[at]] + [down_ref.at[at, :, place] for place in places]
        return moves(shard[:-1], targets, in_sem.at[at])

    @pl.when(step == 0)
    def _():
        for at in range(count):
            for move in weights(at):
                move.start()
        if first:
            for ref in accs:
                ref[...] = jnp.zeros_like(ref)
        else:
            for move in moves(carried, accs, sem):
                move.start()
        gm_ref[...] = (line(gamma_ref) * cot_ref[...].astype(F32)).astype(BF)

    for at in range(count):
        @pl.when(step == at)
        def _():
            for move in weights(at):
                move.wait()

    x = x_ref[...]
    gm = gm_ref[...]
    up = up_ref[step]
    down = down_ref[step]
    upb = shards[0][-1][...].astype(F32)[1:2, :]
    for at in range(1, count):
        upb = jnp.where(step == at, shards[at][-1][...].astype(F32)[1:2, :], upb)
    before = dot_nn(x, up) + upb
    share = 0.5 + 0.5 * lax.erf(before * (0.5**0.5))
    density = jnp.exp(before * before * -0.5) * ((2.0 * jnp.pi) ** -0.5)
    hidden = (before * share).astype(BF)
    slope = share + before * density
    grad_before = (dot_nt(gm, down) * slope).astype(BF)
    upb_grad_ref[...] = fold(grad_before.astype(F32))
    held_ref[step, x.shape[1] :, :] = dot_tn(hidden, gm).astype(BF)
    held_ref[step, : x.shape[1], :] = dot_tn(x, grad_before).astype(BF)
    for at in range(count):
        @pl.when(step == at)
        def _():
            pltpu.make_async_copy(held_ref.at[at], grads[at], out_sem.at[at]).start()

    if not first:
        @pl.when(step == 0)
        def _():
            for move in moves(carried, accs, sem):
                move.wait()

    value_ref[...] += dot_nn(hidden, down)
    grad_ref[...] += dot_nt(grad_before, up)

    @pl.when(step == count - 1)
    def _():
        for move in moves(accs, totals, sem):
            move.start()
        for move in moves(accs, totals, sem):
            move.wait()
        for at in range(count):
            pltpu.make_async_copy(held_ref.at[at], grads[at], out_sem.at[at]).wait()


def mlp(x, cot, gamma, shards, carried, side):
    rows, width = x.shape
    hidden = shards[0][0].shape[1]
    first = carried is None
    count = len(shards)
    anywhere = pl.BlockSpec(memory_space=pl.ANY)
    in_specs = [whole((rows, width)), whole((rows, width)), whole((width,))]
    operands = [x, cot, gamma]
    for shard in shards:
        in_specs += [anywhere] * (len(shard) - 1) + [small_spec(shard[-1])]
        operands += list(shard[:-1]) + [shard[-1][0]]
    aliases = {}
    if not first:
        at = len(operands) + 1
        aliases = {at: 0, at + 1: 1}
        in_specs += [anywhere] * 2
        operands += list(carried)
    total = shaped((rows, width), F32)
    grads = [in_hbm((width + hidden, width), BF)]
    grad_specs = [anywhere]
    return pl.pallas_call(
        functools.partial(mlp_kernel, first, [len(shard) for shard in shards]),
        out_shape=[total, total] + grads * count + [shaped((8 * count, hidden), F32)],
        grid_spec=pltpu.PrefetchScalarGridSpec(
            num_scalar_prefetch=1,
            grid=(count,),
            in_specs=in_specs,
            out_specs=[anywhere] * 2
            + grad_specs * count
            + [pl.BlockSpec((8, hidden), lambda i, *_: (i, 0))],
            scratch_shapes=[
                pltpu.VMEM((rows, width), BF),
                pltpu.VMEM((count, width, hidden), BF),
                pltpu.VMEM((count, hidden, width), BF),
                pltpu.VMEM((count, width + hidden, width), BF),
                pltpu.VMEM((rows, width), F32),
                pltpu.VMEM((rows, width), F32),
                pltpu.SemaphoreType.DMA((count, 3)),
                pltpu.SemaphoreType.DMA((count,)),
                pltpu.SemaphoreType.DMA((2,)),
            ],
        ),
        input_output_aliases=aliases,
        compiler_params=params(MLP_MIB),
        cost_estimate=cost(9 * count),
        name="mlp",
    )(side, *placed(operands, [x] + list(carried or [])))


def middle_back_kernel(
    value_ref, grad_ref, middle_ref, attn_ref, cot_ref, dbias_ref, gmlp_ref, gattn_ref, gain_ref,
    out_ref, gmiddle_ref, gattn_out_ref, sums_ref,
):
    @pl.when(pl.program_id(0) == 0)
    def _():
        sums_ref[...] = jnp.zeros_like(sums_ref)

    def add(row, values):
        sums_ref[8 * row : 8 * row + 8, :] += fold(values)

    for at in tiles():
        rows = slice(at, at + TILE)
        value = value_ref[0, rows, :] + line(dbias_ref)
        cot = cot_ref[0, rows, :].astype(F32)
        middle = middle_ref[0, rows, :]
        out_ref[0, rows, :] = (middle + line(gmlp_ref) * value).astype(BF)
        add(0, cot * value)
        add(1, (line(gmlp_ref) * cot).astype(BF).astype(F32))
        xhat, scale = normalise(middle)
        grad = grad_ref[0, rows, :]
        add(2, grad * xhat)
        add(3, grad)
        grad_middle = cot + normalise_back(grad, line(gain_ref), xhat, scale)
        gmiddle_ref[0, rows, :] = grad_middle
        add(4, grad_middle * attn_ref[0, rows, :])
        grad_attn = (line(gattn_ref) * grad_middle).astype(BF)
        gattn_out_ref[0, rows, :] = grad_attn
        add(5, grad_attn.astype(F32))


def middle_back(value, grad, middle, attn, cot, vectors):
    images, _, width = middle.shape
    return pl.pallas_call(
        middle_back_kernel,
        out_shape=(
            in_hbm(middle.shape, BF),
            in_hbm(middle.shape, F32),
            in_hbm(middle.shape, BF),
            shaped((48, width), F32),
        ),
        grid=(images,),
        in_specs=[image_spec(width)] * 5 + [whole((width,))] * 4,
        out_specs=(image_spec(width),) * 3 + (resident((48, width)),),
        compiler_params=params(12),
        cost_estimate=cost(5),
        name="middle_back",
    )(*placed([value, grad, middle, attn, cot, *vectors], [value, grad, middle, attn]))


def swap(values, axis, mask):
    count = lax.axis_size(axis)
    return lax.ppermute(values, axis, [(i, i ^ mask) for i in range(count)])


def dp_masks():
    count = lax.axis_size("dp")
    return [1 << bit for bit in range(count.bit_length() - 1)]


def pinned(value, *others):
    return lax.optimization_barrier((value,) + others)[0]


def plus(left, right):
    return (left.astype(F32) + right.astype(F32)).astype(BF)


ORDERS = ((0, 1), (1, 2))


def axis_bits():
    place = lax.axis_index("dp")
    return jnp.stack([(place >> bit) & 1 for bit in range(len(dp_masks()))]).astype(jnp.int32)


def halves_of(ref, base, size, bit):
    keep = pl.multiple_of(base + bit * size, 16)
    sent = pl.multiple_of(base + (1 - bit) * size, 16)
    return ref[pl.ds(keep, size), :], ref[pl.ds(sent, size), :]


def split_kernel(bits_ref, a_ref, b_ref, c_ref, *refs):
    outs, total_ref = refs[:4], refs[4]
    for at in range(0, total_ref.shape[0], 64):
        rows = slice(at, at + 64)
        total_ref[rows, :] = (
            a_ref[rows, :].astype(F32) + b_ref[rows, :].astype(F32) + c_ref[rows, :].astype(F32)
        ).astype(BF)
    part = total_ref.shape[0] // 2
    for which in range(2):
        keep, sent = halves_of(total_ref, which * part, part // 2, bits_ref[ORDERS[which][0]])
        outs[2 * which][...] = keep
        outs[2 * which + 1][...] = sent


def again_kernel(bits_ref, *refs):
    ins, outs, totals = refs[:4], refs[4:8], refs[8:]
    for which in range(2):
        total_ref = totals[which]
        total_ref[...] = plus(ins[2 * which][...], ins[2 * which + 1][...])
        size = total_ref.shape[0] // 2
        keep, sent = halves_of(total_ref, 0, size, bits_ref[ORDERS[which][1]])
        outs[2 * which][...] = keep
        outs[2 * which + 1][...] = sent


def both_kernel(bits_ref, *refs):
    for which in range(2):
        refs[4 + which][...] = plus(refs[2 * which][...], refs[2 * which + 1][...])


def put(out_ref, base, own, other, bit):
    size = own.shape[0]
    out_ref[pl.ds(pl.multiple_of(base + bit * size, 16), size), :] = own.astype(out_ref.dtype)
    out_ref[pl.ds(pl.multiple_of(base + (1 - bit) * size, 16), size), :] = other.astype(out_ref.dtype)


def grow_kernel(bits_ref, *refs):
    for which in range(2):
        put(refs[4 + which], 0, refs[2 * which][...], refs[2 * which + 1][...], bits_ref[ORDERS[which][1]])


def whole_kernel(bits_ref, *refs):
    ins, (*out_refs, total_ref) = refs[:4], refs[4:]
    part = total_ref.shape[0] // 2
    for which in range(2):
        put(total_ref, which * part, ins[2 * which][...], ins[2 * which + 1][...], bits_ref[ORDERS[which][0]])
    base = 0
    for out_ref in out_refs:
        out_ref[...] = total_ref[base : base + out_ref.shape[0], :].astype(F32)
        base += out_ref.shape[0]


def step_call(kernel, bits, arrays, outs, scratch, name):
    vmem = pl.BlockSpec(memory_space=pltpu.VMEM)
    return pl.pallas_call(
        kernel,
        out_shape=outs,
        in_specs=[pl.BlockSpec(memory_space=pltpu.SMEM)] + [vmem] * len(arrays),
        out_specs=[vmem] * len(outs),
        scratch_shapes=scratch,
        compiler_params=params(12, 0),
        cost_estimate=cost(1),
        name=name,
    )(bits, *arrays)


def dp_chain(pieces, sizes):
    bits = axis_bits()
    masks = dp_masks()
    rows, width = pieces[0].shape
    quarter, eighth = shaped((rows // 4, width), BF), shaped((rows // 8, width), BF)
    rest = [[axis for axis in range(len(masks)) if axis not in order] for order in ORDERS]

    def send(a, b, axes):
        return [swap(array, "dp", masks[axis]) for array, axis in zip((a, b), axes)]

    a, a_sent, b, b_sent = step_call(
        split_kernel, bits, placed(pieces), [quarter] * 4, [pltpu.VMEM((rows, width), BF)], "dp_split"
    )
    a_got, b_got = yield send(a_sent, b_sent, [ORDERS[0][0], ORDERS[1][0]])
    a, a_sent, b, b_sent = step_call(
        again_kernel, bits, [a, a_got, b, b_got], [eighth] * 4,
        [pltpu.VMEM((rows // 4, width), BF)] * 2, "dp_again",
    )
    a_got, b_got = yield send(a_sent, b_sent, [ORDERS[0][1], ORDERS[1][1]])
    a, b = step_call(both_kernel, bits, [a, a_got, b, b_got], [eighth] * 2, [], "dp_both")
    for axes in zip(*rest):
        a_got, b_got = yield send(a, b, axes)
        a, b = step_call(both_kernel, bits, [a, a_got, b, b_got], [eighth] * 2, [], "dp_both")
    a_got, b_got = yield send(a, b, [ORDERS[0][1], ORDERS[1][1]])
    a, b = step_call(grow_kernel, bits, [a, a_got, b, b_got], [quarter] * 2, [], "dp_grow")
    a_got, b_got = yield send(a, b, [ORDERS[0][0], ORDERS[1][0]])
    return step_call(
        whole_kernel, bits, [a, a_got, b, b_got],
        [shaped((size, width), F32) for size in sizes], [pltpu.VMEM((rows, width), BF)], "dp_whole",
    )


class Chain:
    def __init__(self, steps):
        self.steps = steps
        self.done = None
        self.got = next(self.steps)

    def go_on(self):
        try:
            self.got = self.steps.send(self.got)
        except StopIteration as stop:
            self.done, self.got = stop.value, []


def together(*chains):
    flat = list(lax.optimization_barrier(tuple(item for chain in chains for item in chain.got)))
    for chain in chains:
        chain.got, flat = flat[: len(chain.got)], flat[len(chain.got) :]


def small_chain(held, sent, keep, own_rows):
    (got,) = yield [swap(sent, "mp", 1)]
    held = held + got
    sent = jnp.concatenate([held[keep + own_rows :], held[own_rows : keep + own_rows]], axis=0)
    (got,) = yield [swap(sent, "mp", 2)]
    held = held[: keep + own_rows] + got
    masks = dp_masks()
    for shift in masks[:-1]:
        (got,) = yield [swap(held, "dp", shift)]
        held = held + got
    (got,) = yield [swap(held, "dp", masks[-1])]
    return held, got


def collect_kernel(ids_ref, sums2_ref, sums1_ref, tokens_ref, table0_ref, table1_ref, *refs):
    upb_refs, joint_refs, (out_ref, sent_ref) = refs[:2], refs[2:6], refs[6:]
    upb_lines = [upb_refs[1][8:16, :], upb_refs[1][0:8, :], upb_refs[0][8:16, :], upb_refs[0][0:8, :]]
    out_ref[...] = jnp.zeros_like(out_ref)
    sent_ref[...] = jnp.zeros_like(sent_ref)
    table = table0_ref[...] + table1_ref[...]

    def total(values):
        return jnp.sum(values, axis=0, keepdims=True)

    lines = [total(sums2_ref[8 * i : 8 * i + 8, :]) for i in range(6)]
    lines += [total(sums1_ref[8 * i : 8 * i + 8, :]) for i in range(2)]
    images = [total(tokens_ref[i]) for i in range(tokens_ref.shape[0])]
    for group in range(GROUPS):
        found = jnp.zeros_like(images[0])
        for at, values in enumerate(images):
            found = found + jnp.where(ids_ref[at] == group, values, 0.0)
        lines.append(found)
    for at, values in enumerate(lines):
        out_ref[8 + at : 9 + at, :] = values
        sent_ref[8 + at : 9 + at, :] = values
    hidden = upb_refs[0].shape[1]
    for which in range(4):
        ref = out_ref if which % 2 == 0 else sent_ref
        base = 0 if which < 2 else 24
        ref[base : base + 1, :hidden] = total(upb_lines[which])
        joint = total(joint_refs[which][...])
        ref[base + 1 : base + 2, : joint.shape[1]] = joint
        per = table.shape[0] // (out_ref.shape[1] // LANES)
        own = per // 4
        for chunk in range(out_ref.shape[1] // LANES):
            ref[base + 2 : base + 2 + own, chunk * LANES : (chunk + 1) * LANES] = table[
                chunk * per + which * own : chunk * per + (which + 1) * own, :
            ]


def collect(ids, sums2, sums1, tokens, tables, upbs, joints):
    width = sums2.shape[1]
    vmem = pl.BlockSpec(memory_space=pltpu.VMEM)
    return pl.pallas_call(
        collect_kernel,
        out_shape=(shaped((32, width), F32), shaped((32, width), F32)),
        in_specs=[pl.BlockSpec(memory_space=pltpu.SMEM)] + [vmem] * 11,
        out_specs=(vmem, vmem),
        cost_estimate=cost(1),
        name="collect",
    )(ids, *placed([sums2, sums1, tokens, *tables, *upbs, *joints], [sums1, tokens, *tables]))


def emit_kernel(held_ref, got_ref, *outs):
    own = outs[9].shape[0]
    value = held_ref[...] + got_ref[...]
    for at in range(8):
        outs[at][...] = value[8 + at : 9 + at, :].reshape(-1)
    outs[8][...] = value[16:24, :]
    outs[9][...] = value[1:2, :own].reshape(-1)
    outs[10][...] = value[1:2, 2 * own : 3 * own].reshape(-1)
    outs[11][...] = value[2 : 2 + outs[11].shape[0], : outs[11].shape[1]]
    outs[12][...] = value[0:1, : outs[12].shape[0]].reshape(-1)


def emit(held, got, own, table_shape, hidden):
    width = held.shape[1]
    return pl.pallas_call(
        emit_kernel,
        out_shape=[shaped((width,), F32)] * 8
        + [
            shaped((GROUPS, width), F32),
            shaped((own,), F32),
            shaped((own,), F32),
            shaped(table_shape, F32),
            shaped((hidden,), F32),
        ],
        cost_estimate=cost(1),
        name="emit",
    )(held, got)


def local(
    patches, dataset_id, patch_masks, mask_tokens, key_mask, bias_index, norm1_gain, norm1_shift,
    qkv_weight, query_bias, value_bias, bias_table, out_weight, out_bias, gamma_attn, norm2_gain,
    norm2_shift, up_weight, up_bias, down_weight, down_bias, gamma_mlp, cotangent,
):
    rows, width = patches.shape
    images = rows // SEQ
    place = lax.axis_index("mp")
    own = qkv_weight.shape[2]
    own_heads = own // HEAD
    table_rows = bias_table.shape[0]
    chunks = width // LANES
    hidden = up_weight.shape[1]

    ids = lax.dynamic_slice_in_dim(dataset_id, place * images, images, 0)
    keys_here = lax.dynamic_slice_in_dim(key_mask, place * images, images, 0)
    mask = jnp.where(keys_here > 0, 0.0, -1e30).astype(F32)[:, :, None]
    sel_table = patch_masks.astype(F32)[:, :, None]
    images3 = patches.reshape(images, SEQ, width)
    cot3 = cotangent.reshape(images, SEQ, width)
    index = bias_index.T
    mix = (ids, images3, sel_table, mask_tokens)

    parity = lax.axis_index("dp") & 1
    side = parity.reshape(1)
    qkv_own = qkv_weight.transpose(1, 2, 0).reshape(3 * own, width)
    small, attn_half, down_half, pack0 = prepare(
        side, qkv_own, out_weight, down_weight, query_bias, value_bias, up_bias, bias_table.T
    )
    small0, small1 = (small, 0), (swap(small, "mp", 1), 0)
    attn_p2 = swap(attn_half, "mp", 2)
    down_p2 = swap(down_half, "mp", 2)
    pack1 = swap(pack0, "mp", 1)
    bias_near = position_bias([small0, small1], 2 * own_heads, index)
    up2 = swap(pinned(up_weight, bias_near), "mp", 2)
    up1, down1 = swap(up_weight, "mp", 1), swap(down_weight, "mp", 1)

    norm1 = [norm1_gain, norm1_shift]
    x1, j0, probs0, c0, part = attend(
        mix, norm1, qkv_own, (out_weight, 0), small0, bias_near, 0, mask
    )
    part, attn_p2 = lax.optimization_barrier((part, attn_p2))
    attn_q2 = swap(attn_p2, "dp", 1)
    attn_p3 = swap(attn_p2, "mp", 1)
    small2, small3 = (attn_p2, 2 * own // SMALL_ROWS), (attn_p3, 2 * own // SMALL_ROWS)
    j1, probs1, c1, part = attend(mix, norm1, pack1, (pack1, 3), small1, bias_near, 1, mask, x1, part)
    part, attn_q2 = lax.optimization_barrier((part, attn_q2))
    attn_q3 = swap(attn_q2, "mp", 1)
    bias_far = position_bias([small2, small3], 2 * own_heads, index)
    j2, probs2, c2, part, pack2 = attend(
        mix, norm1, attn_p2, attn_q2, small2, bias_far, 0, mask, x1, part, side
    )
    part, down_p2 = lax.optimization_barrier((part, down_p2))
    down_q2 = swap(down_p2, "dp", 1)
    down_p3 = swap(down_p2, "mp", 1)
    j3, probs3, c3, attn_value, middle, normed2, pack3 = attend(
        mix, [norm2_gain, norm2_shift], attn_p3, attn_q3, small3, bias_far, 1, mask, x1, part, side,
        [out_bias, gamma_attn],
    )

    x2 = normed2.reshape(rows, width)
    x2, up2, down_q2 = lax.optimization_barrier((x2, up2, down_q2))
    up3 = swap(up2, "mp", 1)
    down_q3 = swap(down_q2, "mp", 1)
    value, grad2, m3, m2, upb32 = mlp(
        x2, cotangent, gamma_mlp, [(up3, down_p3, down_q3, small3), (up2, down_p2, down_q2, small2)],
        None, side,
    )
    mlp_far = plus(m2, swap(m3, "mp", 1))
    x2, mlp_far = lax.optimization_barrier((x2, mlp_far))
    mr2 = swap(mlp_far, "mp", 2)
    value, grad2, m1, m0, upb10 = mlp(
        x2, cotangent, gamma_mlp, [(up1, down1, small1), (up_weight, down_weight, small0)],
        (value, grad2), side,
    )

    shape3 = (images, SEQ, width)
    output, grad_middle, grad_attn, sums2 = middle_back(
        value.reshape(shape3), grad2.reshape(shape3), middle, attn_value, cot3,
        [down_bias, gamma_mlp, gamma_attn, norm2_gain],
    )

    mr1 = [swap(m1[:width], "mp", 1), swap(m1[width:], "mp", 1)]
    grad_attn, *mr1 = lax.optimization_barrier((grad_attn, *mr1))
    g1, js1, g3, js3, total13, carried = attend_back(
        ids, x1, grad_attn,
        [(j1, probs1, c1, pack1, 0, pack1, 3), (j3, probs3, c3, pack3, 0, pack3, 3)], None, None,
    )
    mlp_sum = [
        (own.astype(F32) + near.astype(F32) + far.astype(F32)).astype(BF)
        for own, near, far in zip((m0[:width], m0[width:]), mr1, (mr2[:width], mr2[width:]))
    ]
    carried, *mlp_sum = lax.optimization_barrier((carried, *mlp_sum))
    up_sum, down_sum = lax.psum(tuple(mlp_sum), "dp")
    r3 = swap(g3, "mp", 1)
    g2, js2, total2, carried = attend_back(
        ids, x1, grad_attn, [(j2, probs2, c2, pack2, 0, pack2, 3)], carried, None
    )
    far = plus(g2, r3)
    carried, far, g1 = lax.optimization_barrier((carried, far, g1))
    r1 = swap(g1, "mp", 1)
    r2 = swap(far, "mp", 2)
    g0, js0, total0, patch_grad, sums1, token_images = attend_back(
        ids, x1, grad_attn, [(j0, probs0, c0, qkv_own, 0, out_weight, 0)], carried,
        (images3, sel_table, mask_tokens, grad_middle, norm1_gain),
    )
    totals = [(total0, 0), (total13, 0), (total2, 0), (total13, 1)]
    blocks = SEQ // TABLE_ROWS
    table0 = table_sums(totals, index, chunks, 0, blocks // 2)
    g0, r1, r2, table0 = lax.optimization_barrier((g0, r1, r2, table0))
    tail = Chain(dp_chain([g0, r1, r2], [3 * own, own]))
    table1 = table_sums(totals, index, chunks, blocks // 2, blocks - blocks // 2)
    held, sent = collect(
        ids, sums2, sums1, token_images, [table0, table1], [upb32, upb10], [js0, js1, js2, js3]
    )
    tail.go_on()
    small = Chain(small_chain(held, sent, 16, 8))
    while tail.done is None or small.done is None:
        going = [chain for chain in (tail, small) if chain.done is None]
        together(*going)
        for chain in going:
            chain.go_on()
    qkv_sum, out_sum = tail.done
    up_sum, down_sum = up_sum.astype(F32), down_sum.astype(F32)
    (
        gamma_mlp_grad, down_bias_grad, gain2_grad, shift2_grad, gamma_attn_grad, out_bias_grad,
        gain1_grad, shift1_grad, token_grad, qb_grad, vb_grad, table_grad, upb_grad,
    ) = emit(*small.done, own, (own_heads, table_rows), hidden)

    return (
        output.reshape(rows, width),
        patch_grad.reshape(rows, width),
        token_grad,
        gain1_grad,
        shift1_grad,
        qkv_sum.reshape(3, own, width).transpose(2, 0, 1),
        qb_grad,
        vb_grad,
        table_grad.T,
        out_sum,
        out_bias_grad,
        gamma_attn_grad,
        gain2_grad,
        shift2_grad,
        up_sum,
        upb_grad,
        down_sum,
        down_bias_grad,
        gamma_mlp_grad,
    )


def solution(mesh):
    return jax.shard_map(
        local,
        mesh=mesh,
        in_specs=(
            P(("dp", "mp"), None), P("dp"), P(), P(), P("dp", None), P(), P(), P(),
            P(None, None, "mp"), P("mp"), P("mp"), P(None, "mp"), P("mp", None), P(), P(), P(), P(),
            P(None, "mp"), P("mp"), P("mp", None), P(), P(), P(("dp", "mp"), None),
        ),
        out_specs=(
            P(("dp", "mp"), None), P(("dp", "mp"), None), P(), P(), P(), P(None, None, "mp"),
            P("mp"), P("mp"), P(None, "mp"), P("mp", None), P(), P(), P(), P(), P(None, "mp"),
            P("mp"), P("mp", None), P(), P(),
        ),
        check_vma=False,
    )
```

```python
import functools

import jax
import jax.numpy as jnp
from jax import lax
from jax.experimental import pallas as pl
from jax.experimental.pallas import tpu as pltpu
from jax.sharding import PartitionSpec as P

HEAD = 64
SEQ = 200
GROUPS = 8
LANES = 128
BF = jnp.bfloat16
F32 = jnp.float32


def dot_nn(left, right):
    return lax.dot_general(left, right, (((1,), (0,)), ((), ())), preferred_element_type=F32)


def dot_nt(left, right):
    return lax.dot_general(left, right, (((1,), (1,)), ((), ())), preferred_element_type=F32)


def dot_tn(left, right):
    return lax.dot_general(left, right, (((0,), (0,)), ((), ())), preferred_element_type=F32)


def params(mib, steps=1):
    return pltpu.CompilerParams(
        dimension_semantics=("arbitrary",) * steps, vmem_limit_bytes=mib << 20
    )


def cost(micros):
    return pl.CostEstimate(flops=int(micros * 1.1e8), transcendentals=0, bytes_accessed=0)


def whole(shape, at=0):
    zeros = (0,) * (len(shape) - 1)
    return pl.BlockSpec(shape, lambda *_: (at,) + zeros, pipeline_mode=pl.Buffered(1))


def image_spec(width):
    return pl.BlockSpec((1, SEQ, width), lambda i, *_: (i, 0, 0))


def resident(shape):
    zeros = (0,) * len(shape)
    return pl.BlockSpec(shape, lambda *_: zeros)


def placed(operands, keep=()):
    return [
        item
        if any(item is kept for kept in keep)
        else pltpu.with_memory_space_constraint(item, pltpu.HBM)
        for item in operands
    ]


def in_hbm(shape, dtype):
    return pltpu.HBM(tuple(shape), dtype)


def shaped(shape, dtype):
    return jax.ShapeDtypeStruct(shape, dtype)


TILE = 40


def normalise(values):
    mean = jnp.mean(values, axis=-1, keepdims=True)
    centred = values - mean
    spread = jnp.mean(centred * centred, axis=-1, keepdims=True)
    scale = lax.rsqrt(spread + 1e-06)
    return centred * scale, scale


def normalise_back(grad, gain, xhat, scale):
    u = grad * gain
    return (
        u - jnp.mean(u, axis=-1, keepdims=True) - xhat * jnp.mean(u * xhat, axis=-1, keepdims=True)
    ) * scale


def line(ref):
    return ref[...].reshape(1, -1)


def token_line(ids_ref, token_ref):
    tokens = token_ref[...].astype(F32)
    group = lax.broadcasted_iota(jnp.int32, tokens.shape, 0)
    return jnp.sum(jnp.where(group == ids_ref[pl.program_id(0)], tokens, 0.0), axis=0, keepdims=True)


def mixed(patch_ref, sel_ref, token, at):
    sel = sel_ref[0, at : at + TILE, :]
    return patch_ref[0, at : at + TILE, :].astype(F32) * (1.0 - sel) + sel * token, sel


def tiles():
    return range(0, SEQ, TILE)


def fold(values):
    return jnp.sum(values.reshape(values.shape[0] // 8, 8, values.shape[1]), axis=0)


SMALL_ROWS = 16


def prepare_kernel(
    side_ref, qkv_ref, out_ref, down_ref, qb_ref, vb_ref, upb_ref, table_ref,
    small_ref, attn_ref, half_ref, pack_ref,
):
    own = qb_ref.shape[0]
    width = small_ref.shape[1]
    small_ref[...] = jnp.zeros_like(small_ref)
    small_ref[0:1, :own] = line(qb_ref)
    small_ref[0:1, 2 * own : 3 * own] = line(vb_ref)
    small_ref[1:2, : upb_ref.shape[0]] = line(upb_ref)
    small_ref[2 : 2 + table_ref.shape[0], : table_ref.shape[1]] = table_ref[...]
    attn_ref[2 * own :, :] = small_ref[...]
    pack_ref[: 3 * own, :] = qkv_ref[...]
    pack_ref[3 * own :, :] = out_ref[...]

    @pl.when(side_ref[0] == 0)
    def _():
        attn_ref[: 2 * own, :] = qkv_ref[: 2 * own, :]
        half_ref[...] = down_ref[:, : width // 2]

    @pl.when(side_ref[0] == 1)
    def _():
        attn_ref[:own, :] = qkv_ref[2 * own :, :]
        attn_ref[own : 2 * own, :] = out_ref[...]
        half_ref[...] = down_ref[:, width // 2 :]


def prepare(side, qkv, out, down, qb, vb, upb, table):
    width = out.shape[1]
    vmem = pl.BlockSpec(memory_space=pltpu.VMEM)
    return pl.pallas_call(
        prepare_kernel,
        out_shape=[
            shaped((SMALL_ROWS, width), BF),
            shaped((2 * qb.shape[0] + SMALL_ROWS, width), BF),
            shaped((down.shape[0], width // 2), BF),
            shaped((4 * qb.shape[0], width), BF),
        ],
        in_specs=[pl.BlockSpec(memory_space=pltpu.SMEM)] + [vmem] * 7,
        out_specs=[vmem] * 4,
        compiler_params=params(8, 0),
        cost_estimate=cost(2),
        name="prepare",
    )(side, *placed([qkv, out, down, qb, vb, upb, table]))


def bias_kernel(near_ref, far_ref, narrow_ref, out_ref, index_ref):
    own = out_ref.shape[0] // 2
    chunks = near_ref.shape[1] // LANES
    tables = (near_ref[...].astype(F32), far_ref[...].astype(F32))
    index_ref[...] = jnp.zeros_like(index_ref)
    index_ref[:, : narrow_ref.shape[1]] = narrow_ref[...]

    def rows_of(step, _):
        row = pl.multiple_of(step * 8, 8)
        for col in range(0, index_ref.shape[1], LANES):
            index = index_ref[pl.ds(row, 8), col : col + LANES]
            low = index & (LANES - 1)
            high = index >> 7
            for head in range(2 * own):
                table, at = tables[head // own], 2 + head % own
                found = jnp.zeros((8, LANES), F32)
                for chunk in range(chunks):
                    source = jnp.broadcast_to(
                        table[at : at + 1, chunk * LANES : (chunk + 1) * LANES], (8, LANES)
                    )
                    picked = jnp.take_along_axis(source, low, axis=1)
                    found = jnp.where(high == chunk, picked, found)
                out_ref[head, pl.ds(row, 8), col : col + LANES] = found
        return 0

    lax.fori_loop(0, SEQ // 8, rows_of, 0, unroll=5)


def small_spec(small):
    return whole((SMALL_ROWS, small[0].shape[1]), small[1])


def position_bias(small, heads, index):
    return pl.pallas_call(
        bias_kernel,
        out_shape=shaped((heads, SEQ, 2 * LANES), F32),
        grid=(1,),
        in_specs=[small_spec(item) for item in small] + [whole(index.shape)],
        out_specs=resident((heads, SEQ, 2 * LANES)),
        scratch_shapes=[pltpu.VMEM((SEQ, 2 * LANES), jnp.int32)],
        compiler_params=params(6),
        cost_estimate=cost(2),
        name="position_bias",
    )(*placed([item for item, _ in small] + [index]))


TABLE_ROWS = 8


def table_kernel(*refs):
    total_refs, (index_ref, out_ref) = refs[:-2], refs[-2:]

    @pl.when(pl.program_id(0) == 0)
    def _():
        out_ref[...] = jnp.zeros_like(out_ref)

    chunks = out_ref.shape[0] // sum(ref.shape[0] for ref in total_refs)
    spots = lax.broadcasted_iota(jnp.int32, (LANES, SEQ), 0)
    acc = jnp.zeros(out_ref.shape, F32)
    for row in range(TABLE_ROWS):
        index = index_ref[row : row + 1, :]
        hot = (spots == (index & (LANES - 1))).astype(F32).astype(BF)
        high = index >> 7
        total = jnp.concatenate([ref[:, row, :] for ref in total_refs], axis=0)
        parts = [jnp.where(high == chunk, total, 0.0) for chunk in range(chunks)]
        acc = acc + dot_nt(jnp.concatenate(parts, axis=0).astype(BF), hot)
    out_ref[...] += acc


def table_sums(totals, index, chunks, first, steps):
    own = totals[0][0].shape[0]
    heads = own * len(totals)
    return pl.pallas_call(
        table_kernel,
        out_shape=shaped((chunks * heads, LANES), F32),
        grid=(steps,),
        in_specs=[
            pl.BlockSpec((own, TABLE_ROWS, SEQ), lambda i, at=at: (at, first + i, 0))
            for _, at in totals
        ]
        + [pl.BlockSpec((TABLE_ROWS, SEQ), lambda i: (first + i, 0))],
        out_specs=resident((chunks * heads, LANES)),
        compiler_params=params(6),
        cost_estimate=cost(5),
        name="table_sums",
    )(*placed([total for total, _ in totals] + [index]))


def block(values, at):
    return values[:, at * LANES : (at + 1) * LANES]


def turned(values):
    return pltpu.roll(values, HEAD, 1)


def only(keep, values):
    return jnp.where(keep, values, jnp.zeros_like(values))


def lower_lanes():
    return lax.broadcasted_iota(jnp.int32, (SEQ, LANES), 1) < HEAD


def shard_forward(x, weight_ref, small_ref, bias_ref, mask, joint_ref, probs_ref, context_ref, base):
    width = joint_ref.shape[2]
    own = width // 3
    low = lower_lanes()
    high = jnp.logical_not(low)
    column = lax.broadcasted_iota(jnp.int32, (1, width), 1)
    scale = jnp.where(column < own, HEAD**-0.5, 1.0)
    joint = dot_nt(x, weight_ref[...])
    joint_ref[0] = ((joint + small_ref[...].astype(F32)[0:1, :width]) * scale).astype(BF)
    joint = joint_ref[0]
    b1, b2, b3 = block(joint, 1), block(joint, 2), block(joint, 3)
    t0, t1 = turned(block(joint, 0)), turned(b1)
    left = [only(high, b1), only(low, b2), only(high, b2)]
    right = [t0, t0, t1]
    value = [b3, b3, joint[:, 4 * LANES :]]
    heads = range(3)
    scores = [dot_nt(left[i], right[i]) + bias_ref[base + i][:, :SEQ] + mask for i in heads]
    raised = [jnp.exp(item - jnp.max(item, axis=0, keepdims=True)) for item in scores]
    probs = [(item * (1.0 / jnp.sum(item, axis=0, keepdims=True))).astype(BF) for item in raised]
    for i in heads:
        probs_ref[0, base + i] = probs[i]
    found = [dot_tn(probs[i], value[i]) for i in heads]
    context_ref[0, :, :LANES] = jnp.where(low, found[0], found[1]).astype(BF)
    context_ref[0, :, LANES:] = found[2].astype(BF)


def attend_kernel(first, last, parted, *refs):
    refs = list(refs)

    def take(count):
        found = refs[:count]
        del refs[:count]
        return found

    if first or last:
        (ids_ref,) = take(1)
    if parted:
        (side_ref,) = take(1)
    if first or last:
        patch_ref, sel_ref, token_ref, gain_ref, shift_ref = take(5)
    if last:
        obias_ref, gamma_ref = take(2)
    if not first:
        x_ref, part_in_ref = take(2)
    weight_ref, out_ref, small_ref, bias_ref, mask_ref = take(5)
    if first:
        (x_ref,) = take(1)
    joint_ref, probs_ref, context_ref, part_ref = take(4)
    if last:
        middle_ref, normed_ref = take(2)
    if parted:
        p_ref, q_ref = weight_ref, out_ref
        (pack_ref,) = take(1)
        half = p_ref.shape[0] - SMALL_ROWS

        @pl.when(pl.program_id(0) == 0)
        def _():
            for side in range(2):
                @pl.when(side_ref[0] == side)
                def _():
                    pack_ref[side * half : (side + 1) * half, :] = p_ref[:half, :]
                    pack_ref[(1 - side) * half : (2 - side) * half, :] = q_ref[:half, :]

        joint = joint_ref.shape[2]
        weight_ref, out_ref = pack_ref.at[:joint], pack_ref.at[joint:]
    if first:
        token = token_line(ids_ref, token_ref)
        for at in tiles():
            start, _ = mixed(patch_ref, sel_ref, token, at)
            xhat, _ = normalise(start)
            x_ref[0, at : at + TILE, :] = (xhat * line(gain_ref) + line(shift_ref)).astype(BF)
    shard_forward(
        x_ref[0], weight_ref, small_ref, bias_ref, mask_ref[0], joint_ref, probs_ref, context_ref, 0
    )
    part = dot_nn(context_ref[0], out_ref[...])
    part_ref[0] = part if first else part + part_in_ref[0]
    if last:
        token = token_line(ids_ref, token_ref)
        for at in tiles():
            rows = slice(at, at + TILE)
            start, _ = mixed(patch_ref, sel_ref, token, at)
            value = part_ref[0, rows, :] + line(obias_ref)
            middle = start + line(gamma_ref) * value
            xhat, _ = normalise(middle)
            part_ref[0, rows, :] = value
            middle_ref[0, rows, :] = middle
            normed_ref[0, rows, :] = (xhat * line(gain_ref) + line(shift_ref)).astype(BF)


def mix_specs(width, groups):
    return [
        image_spec(width),
        pl.BlockSpec((1, SEQ, 1), lambda i, ids, *_: (ids[i], 0, 0)),
        whole((groups, width)),
    ]


def attend(mix, norm, weight, out, small, bias, turn, mask, x=None, part=None, side=None, after=None):
    ids, patches, sel_table, tokens = mix
    images, _, width = patches.shape
    heads = bias.shape[0] // 2
    own = heads * HEAD
    first, last, parted = x is None, after is not None, side is not None
    prefetch, in_specs, operands = [], [], []
    if first or last:
        prefetch.append(ids)
    if parted:
        prefetch.append(side)
    if first or last:
        in_specs += mix_specs(width, tokens.shape[0]) + [whole((width,))] * 2
        operands += [patches, sel_table, tokens, *norm]
    if last:
        in_specs += [whole((width,))] * 2
        operands += list(after)
    if not first:
        in_specs += [image_spec(width)] * 2
        operands += [x, part]
    if parted:
        in_specs += [whole(weight.shape), whole(out.shape)]
    else:
        in_specs += [whole((3 * own, width)), whole((own, width), out[1])]
        out = out[0]
    in_specs += [small_spec(small)]
    in_specs += [whole((heads,) + bias.shape[1:], turn), image_spec(1)]
    operands += [weight, out, small[0], bias, mask]
    outs = [
        (in_hbm((images, SEQ, 3 * own), BF), image_spec(3 * own)),
        (
            in_hbm((images, heads, SEQ, SEQ), BF),
            pl.BlockSpec((1, heads, SEQ, SEQ), lambda i, *_: (i, 0, 0, 0)),
        ),
        (in_hbm((images, SEQ, own), BF), image_spec(own)),
        (shaped(patches.shape, F32), image_spec(width)),
    ]
    if first:
        outs = [(in_hbm(patches.shape, BF), image_spec(width))] + outs
    if last:
        outs += [
            (shaped(patches.shape, F32), image_spec(width)),
            (shaped(patches.shape, BF), image_spec(width)),
        ]
    if parted:
        outs.append((in_hbm((4 * own, width), BF), resident((4 * own, width))))
    return pl.pallas_call(
        functools.partial(attend_kernel, first, last, parted),
        out_shape=[shape for shape, _ in outs],
        grid_spec=pltpu.PrefetchScalarGridSpec(
            num_scalar_prefetch=len(prefetch),
            grid=(images,),
            in_specs=in_specs,
            out_specs=[spec for _, spec in outs],
        ),
        compiler_params=params(14),
        cost_estimate=cost(9),
        name="attend",
    )(*prefetch, *placed(operands, [part, bias]))


def shards_backward(x, grad, shards, total_ref):
    low = lower_lanes()
    high = jnp.logical_not(low)
    left, right, queries, keys, probs = [], [], [], [], []
    for joint_ref, probs_ref, _, _, out_ref, _, _, _ in shards:
        grad_context = dot_nt(grad, out_ref[...]).astype(BF)
        d0, d1 = grad_context[:, :LANES], grad_context[:, LANES:]
        joint = joint_ref[0]
        b3 = block(joint, 3)
        t0, t1, t2 = turned(block(joint, 0)), turned(block(joint, 1)), turned(block(joint, 2))
        left += [only(low, b3), only(high, b3), joint[:, 4 * LANES :]]
        right += [d0, d0, d1]
        queries += [t0, t0, t1]
        keys += [t1, t2, t2]
        probs += [probs_ref[0, i] for i in range(3)]
    heads = range(len(left))
    grad_probs = [dot_nt(left[i], right[i]) for i in heads]
    grads_v = [dot_nn(probs[i], right[i]) for i in heads]
    grad_scores = []
    for i in heads:
        wide = probs[i].astype(F32)
        centre = jnp.sum(wide * grad_probs[i], axis=0, keepdims=True)
        grad_scores.append((wide * (grad_probs[i] - centre)).astype(BF))
    for i in heads:
        total_ref[i] += grad_scores[i].astype(F32)
    grads_k = [dot_nn(grad_scores[i], queries[i]) for i in heads]
    grads_q = [dot_tn(grad_scores[i], keys[i]) for i in heads]
    scale = HEAD**-0.5
    part = None
    for which, (_, _, context_ref, weight_ref, _, sums_ref, acc_ref, joint_grad_ref) in enumerate(shards):
        gq, gk, gv = (items[3 * which : 3 * which + 3] for items in (grads_q, grads_k, grads_v))
        blocks = [
            jnp.where(low, gq[0], gq[1]) * scale,
            jnp.where(low, gq[2] * scale, gk[0]),
            jnp.where(low, gk[1], gk[2]),
            jnp.where(low, gv[0], gv[1]),
            gv[2],
        ]
        for at, values in enumerate(blocks):
            cols = slice(at * LANES, at * LANES + values.shape[1])
            held = values.astype(BF)
            joint_grad_ref[:, cols] = held
            sums_ref[:, cols] += fold(held.astype(F32))
        width = joint_grad_ref.shape[1]
        joint_grad = joint_grad_ref[...]
        acc_ref[:width, :] += dot_tn(joint_grad, x)
        acc_ref[width:, :] += dot_tn(context_ref[0], grad)
        own = dot_nn(joint_grad, weight_ref[...])
        part = own if part is None else part + own
    return part


def attend_back_kernel(first, last, count, *refs):
    refs = list(refs)

    def take(number):
        found = refs[:number]
        del refs[:number]
        return found

    (ids_ref,) = take(1)
    if last:
        patch_ref, sel_ref, token_ref, gmiddle_ref, gain_ref = take(5)
    if not first:
        (carried_ref,) = take(1)
    x_ref, grad_ref = take(2)
    inputs = [take(5) for _ in range(count)]
    outputs = [take(2) for _ in range(count)]
    (total_ref,) = take(1)
    if last:
        patch_out_ref, norm_ref, token_out_ref = take(3)
    else:
        (carry_out_ref,) = take(1)
    scratch = [take(2) for _ in range(count)]
    step = pl.program_id(0)

    @pl.when(step == 0)
    def _():
        zeroed = [total_ref] + [item[1] for item in outputs] + [item[0] for item in scratch]
        for ref in zeroed + ([norm_ref] if last else []):
            ref[...] = jnp.zeros_like(ref)

    shards = [
        (*ins, out[1], own[0], own[1]) for ins, out, own in zip(inputs, outputs, scratch)
    ]
    part = shards_backward(x_ref[0], grad_ref[0], shards, total_ref)
    if not first:
        part = part + carried_ref[0]
    if last:
        (carry_ref,) = refs
        carry_ref[...] = part
        token = token_line(ids_ref, token_ref)
        token_sum = jnp.zeros((8, part.shape[1]), F32)
        for at in tiles():
            rows = slice(at, at + TILE)
            start, sel = mixed(patch_ref, sel_ref, token, at)
            xhat, scale = normalise(start)
            grad_normed = carry_ref[rows, :]
            norm_ref[0:8, :] += fold(grad_normed * xhat)
            norm_ref[8:16, :] += fold(grad_normed)
            grad_start = gmiddle_ref[0, rows, :] + normalise_back(
                grad_normed, line(gain_ref), xhat, scale
            )
            patch_out_ref[0, rows, :] = grad_start * (1.0 - sel)
            token_sum = token_sum + fold(grad_start * sel)
        token_out_ref[0] = token_sum
    else:
        carry_out_ref[0] = part

    @pl.when(step == pl.num_programs(0) - 1)
    def _():
        for out, own in zip(outputs, scratch):
            out[0][...] = own[0][...].astype(BF)


def attend_back(ids, x, grad, shards, carried, tail):
    images, _, width = x.shape
    joint_width = shards[0][0].shape[2]
    own = joint_width // 3
    heads = own // HEAD
    count = len(shards)
    square = pl.BlockSpec((1, heads, SEQ, SEQ), lambda i, *_: (i, 0, 0, 0))
    first, last = carried is None, tail is not None
    in_specs = [image_spec(width)] * 2
    operands = [x, grad]
    for joint, probs, context, weight, weight_at, out, out_at in shards:
        in_specs += [image_spec(joint_width), square, image_spec(own)]
        in_specs += [whole((joint_width, width), weight_at), whole((own, width), out_at)]
        operands += [joint, probs, context, weight, out]
    if not first:
        in_specs = [image_spec(width)] + in_specs
        operands = [carried] + operands
    out_shape, out_specs, scratch = [], [], []
    for _ in shards:
        out_shape += [in_hbm((joint_width + own, width), BF), in_hbm((8, joint_width), F32)]
        out_specs += [resident((joint_width + own, width)), resident((8, joint_width))]
        scratch += [pltpu.VMEM((joint_width + own, width), F32), pltpu.VMEM((SEQ, joint_width), BF)]
    out_shape.append(in_hbm((count * heads, SEQ, SEQ), F32))
    out_specs.append(resident((count * heads, SEQ, SEQ)))
    if last:
        patches, sel_table, tokens, grad_middle, gain = tail
        in_specs = (
            mix_specs(width, tokens.shape[0]) + [image_spec(width), whole((width,))] + in_specs
        )
        operands = [patches, sel_table, tokens, grad_middle, gain] + operands
        out_shape += [
            shaped(x.shape, F32), shaped((16, width), F32), shaped((images, 8, width), F32)
        ]
        out_specs += [
            image_spec(width),
            resident((16, width)),
            pl.BlockSpec((1, 8, width), lambda i, *_: (i, 0, 0)),
        ]
        scratch.append(pltpu.VMEM((SEQ, width), F32))
    else:
        out_shape.append(in_hbm(x.shape, F32))
        out_specs.append(image_spec(width))
    return pl.pallas_call(
        functools.partial(attend_back_kernel, first, last, count),
        out_shape=out_shape,
        grid_spec=pltpu.PrefetchScalarGridSpec(
            num_scalar_prefetch=1,
            grid=(images,),
            in_specs=in_specs,
            out_specs=out_specs,
            scratch_shapes=scratch,
        ),
        compiler_params=params(14 if count == 1 else 24),
        cost_estimate=cost(13 * count),
        name="attend_back",
    )(ids, *placed(operands))


MLP_MIB = 40


def mlp_kernel(first, lengths, *refs):
    refs = list(refs)

    def take(number):
        found = refs[:number]
        del refs[:number]
        return found

    count = len(lengths)
    (side_ref,) = take(1)
    x_ref, cot_ref, gamma_ref = take(3)
    shards = [take(length) for length in lengths]
    if not first:
        carried = take(2)
    totals = take(2)
    grads = take(count)
    upb_grad_ref, gm_ref, up_ref, down_ref, held_ref, value_ref, grad_ref, in_sem, out_sem, sem = refs
    accs = (value_ref, grad_ref)
    step = pl.program_id(0)

    def moves(sources, targets, sems):
        return [
            pltpu.make_async_copy(source, target, sems.at[at])
            for at, (source, target) in enumerate(zip(sources, targets))
        ]

    def weights(at):
        shard = shards[at]
        if len(shard) == 3:
            targets = [up_ref.at[at], down_ref.at[at]]
        else:
            half = shard[1].shape[1]
            places = [
                pl.ds(pl.multiple_of(place * half, LANES), half)
                for place in (side_ref[0], 1 - side_ref[0])
            ]
            targets = [up_ref.at[at]] + [down_ref.at[at, :, place] for place in places]
        return moves(shard[:-1], targets, in_sem.at[at])

    @pl.when(step == 0)
    def _():
        for at in range(count):
            for move in weights(at):
                move.start()
        if first:
            for ref in accs:
                ref[...] = jnp.zeros_like(ref)
        else:
            for move in moves(carried, accs, sem):
                move.start()
        gm_ref[...] = (line(gamma_ref) * cot_ref[...].astype(F32)).astype(BF)

    for at in range(count):
        @pl.when(step == at)
        def _():
            for move in weights(at):
                move.wait()

    x = x_ref[...]
    gm = gm_ref[...]
    up = up_ref[step]
    down = down_ref[step]
    upb = shards[0][-1][...].astype(F32)[1:2, :]
    for at in range(1, count):
        upb = jnp.where(step == at, shards[at][-1][...].astype(F32)[1:2, :], upb)
    before = dot_nn(x, up) + upb
    share = 0.5 + 0.5 * lax.erf(before * (0.5**0.5))
    density = jnp.exp(before * before * -0.5) * ((2.0 * jnp.pi) ** -0.5)
    hidden = (before * share).astype(BF)
    slope = share + before * density
    grad_before = (dot_nt(gm, down) * slope).astype(BF)
    upb_grad_ref[...] = fold(grad_before.astype(F32))
    held_ref[step, x.shape[1] :, :] = dot_tn(hidden, gm).astype(BF)
    held_ref[step, : x.shape[1], :] = dot_tn(x, grad_before).astype(BF)
    for at in range(count):
        @pl.when(step == at)
        def _():
            pltpu.make_async_copy(held_ref.at[at], grads[at], out_sem.at[at]).start()

    if not first:
        @pl.when(step == 0)
        def _():
            for move in moves(carried, accs, sem):
                move.wait()

    value_ref[...] += dot_nn(hidden, down)
    grad_ref[...] += dot_nt(grad_before, up)

    @pl.when(step == count - 1)
    def _():
        for move in moves(accs, totals, sem):
            move.start()
        for move in moves(accs, totals, sem):
            move.wait()
        for at in range(count):
            pltpu.make_async_copy(held_ref.at[at], grads[at], out_sem.at[at]).wait()


def mlp(x, cot, gamma, shards, carried, side):
    rows, width = x.shape
    hidden = shards[0][0].shape[1]
    first = carried is None
    count = len(shards)
    anywhere = pl.BlockSpec(memory_space=pl.ANY)
    in_specs = [whole((rows, width)), whole((rows, width)), whole((width,))]
    operands = [x, cot, gamma]
    for shard in shards:
        in_specs += [anywhere] * (len(shard) - 1) + [small_spec(shard[-1])]
        operands += list(shard[:-1]) + [shard[-1][0]]
    aliases = {}
    if not first:
        at = len(operands) + 1
        aliases = {at: 0, at + 1: 1}
        in_specs += [anywhere] * 2
        operands += list(carried)
    total = shaped((rows, width), F32)
    grads = [in_hbm((width + hidden, width), BF)]
    grad_specs = [anywhere]
    return pl.pallas_call(
        functools.partial(mlp_kernel, first, [len(shard) for shard in shards]),
        out_shape=[total, total] + grads * count + [shaped((8 * count, hidden), F32)],
        grid_spec=pltpu.PrefetchScalarGridSpec(
            num_scalar_prefetch=1,
            grid=(count,),
            in_specs=in_specs,
            out_specs=[anywhere] * 2
            + grad_specs * count
            + [pl.BlockSpec((8, hidden), lambda i, *_: (i, 0))],
            scratch_shapes=[
                pltpu.VMEM((rows, width), BF),
                pltpu.VMEM((count, width, hidden), BF),
                pltpu.VMEM((count, hidden, width), BF),
                pltpu.VMEM((count, width + hidden, width), BF),
                pltpu.VMEM((rows, width), F32),
                pltpu.VMEM((rows, width), F32),
                pltpu.SemaphoreType.DMA((count, 3)),
                pltpu.SemaphoreType.DMA((count,)),
                pltpu.SemaphoreType.DMA((2,)),
            ],
        ),
        input_output_aliases=aliases,
        compiler_params=params(MLP_MIB),
        cost_estimate=cost(9 * count),
        name="mlp",
    )(side, *placed(operands, [x] + list(carried or [])))


def middle_back_kernel(
    value_ref, grad_ref, middle_ref, attn_ref, cot_ref, dbias_ref, gmlp_ref, gattn_ref, gain_ref,
    out_ref, gmiddle_ref, gattn_out_ref, sums_ref,
):
    @pl.when(pl.program_id(0) == 0)
    def _():
        sums_ref[...] = jnp.zeros_like(sums_ref)

    def add(row, values):
        sums_ref[8 * row : 8 * row + 8, :] += fold(values)

    for at in tiles():
        rows = slice(at, at + TILE)
        value = value_ref[0, rows, :] + line(dbias_ref)
        cot = cot_ref[0, rows, :].astype(F32)
        middle = middle_ref[0, rows, :]
        out_ref[0, rows, :] = (middle + line(gmlp_ref) * value).astype(BF)
        add(0, cot * value)
        add(1, (line(gmlp_ref) * cot).astype(BF).astype(F32))
        xhat, scale = normalise(middle)
        grad = grad_ref[0, rows, :]
        add(2, grad * xhat)
        add(3, grad)
        grad_middle = cot + normalise_back(grad, line(gain_ref), xhat, scale)
        gmiddle_ref[0, rows, :] = grad_middle
        add(4, grad_middle * attn_ref[0, rows, :])
        grad_attn = (line(gattn_ref) * grad_middle).astype(BF)
        gattn_out_ref[0, rows, :] = grad_attn
        add(5, grad_attn.astype(F32))


def middle_back(value, grad, middle, attn, cot, vectors):
    images, _, width = middle.shape
    return pl.pallas_call(
        middle_back_kernel,
        out_shape=(
            in_hbm(middle.shape, BF),
            in_hbm(middle.shape, F32),
            in_hbm(middle.shape, BF),
            shaped((48, width), F32),
        ),
        grid=(images,),
        in_specs=[image_spec(width)] * 5 + [whole((width,))] * 4,
        out_specs=(image_spec(width),) * 3 + (resident((48, width)),),
        compiler_params=params(12),
        cost_estimate=cost(5),
        name="middle_back",
    )(*placed([value, grad, middle, attn, cot, *vectors], [value, grad, middle, attn]))


def swap(values, axis, mask):
    count = lax.axis_size(axis)
    return lax.ppermute(values, axis, [(i, i ^ mask) for i in range(count)])


def dp_masks():
    count = lax.axis_size("dp")
    return [1 << bit for bit in range(count.bit_length() - 1)]


def pinned(value, *others):
    return lax.optimization_barrier((value,) + others)[0]


def plus(left, right):
    return (left.astype(F32) + right.astype(F32)).astype(BF)


ORDERS = ((0, 1), (1, 2))


def axis_bits():
    place = lax.axis_index("dp")
    return jnp.stack([(place >> bit) & 1 for bit in range(len(dp_masks()))]).astype(jnp.int32)


def halves_of(ref, base, size, bit):
    keep = pl.multiple_of(base + bit * size, 16)
    sent = pl.multiple_of(base + (1 - bit) * size, 16)
    return ref[pl.ds(keep, size), :], ref[pl.ds(sent, size), :]


def split_kernel(bits_ref, a_ref, b_ref, c_ref, *refs):
    outs, total_ref = refs[:4], refs[4]
    for at in range(0, total_ref.shape[0], 64):
        rows = slice(at, at + 64)
        total_ref[rows, :] = (
            a_ref[rows, :].astype(F32) + b_ref[rows, :].astype(F32) + c_ref[rows, :].astype(F32)
        ).astype(BF)
    part = total_ref.shape[0] // 2
    for which in range(2):
        keep, sent = halves_of(total_ref, which * part, part // 2, bits_ref[ORDERS[which][0]])
        outs[2 * which][...] = keep
        outs[2 * which + 1][...] = sent


def again_kernel(bits_ref, *refs):
    ins, outs, totals = refs[:4], refs[4:8], refs[8:]
    for which in range(2):
        total_ref = totals[which]
        total_ref[...] = plus(ins[2 * which][...], ins[2 * which + 1][...])
        size = total_ref.shape[0] // 2
        keep, sent = halves_of(total_ref, 0, size, bits_ref[ORDERS[which][1]])
        outs[2 * which][...] = keep
        outs[2 * which + 1][...] = sent


def both_kernel(bits_ref, *refs):
    for which in range(2):
        refs[4 + which][...] = plus(refs[2 * which][...], refs[2 * which + 1][...])


def put(out_ref, base, own, other, bit):
    size = own.shape[0]
    out_ref[pl.ds(pl.multiple_of(base + bit * size, 16), size), :] = own.astype(out_ref.dtype)
    out_ref[pl.ds(pl.multiple_of(base + (1 - bit) * size, 16), size), :] = other.astype(out_ref.dtype)


def grow_kernel(bits_ref, *refs):
    for which in range(2):
        put(refs[4 + which], 0, refs[2 * which][...], refs[2 * which + 1][...], bits_ref[ORDERS[which][1]])


def whole_kernel(bits_ref, *refs):
    ins, (*out_refs, total_ref) = refs[:4], refs[4:]
    part = total_ref.shape[0] // 2
    for which in range(2):
        put(total_ref, which * part, ins[2 * which][...], ins[2 * which + 1][...], bits_ref[ORDERS[which][0]])
    base = 0
    for out_ref in out_refs:
        out_ref[...] = total_ref[base : base + out_ref.shape[0], :].astype(F32)
        base += out_ref.shape[0]


def step_call(kernel, bits, arrays, outs, scratch, name):
    vmem = pl.BlockSpec(memory_space=pltpu.VMEM)
    return pl.pallas_call(
        kernel,
        out_shape=outs,
        in_specs=[pl.BlockSpec(memory_space=pltpu.SMEM)] + [vmem] * len(arrays),
        out_specs=[vmem] * len(outs),
        scratch_shapes=scratch,
        compiler_params=params(12, 0),
        cost_estimate=cost(1),
        name=name,
    )(bits, *arrays)


def dp_chain(pieces, sizes):
    bits = axis_bits()
    masks = dp_masks()
    rows, width = pieces[0].shape
    quarter, eighth = shaped((rows // 4, width), BF), shaped((rows // 8, width), BF)
    rest = [[axis for axis in range(len(masks)) if axis not in order] for order in ORDERS]

    def send(a, b, axes):
        return [swap(array, "dp", masks[axis]) for array, axis in zip((a, b), axes)]

    a, a_sent, b, b_sent = step_call(
        split_kernel, bits, placed(pieces), [quarter] * 4, [pltpu.VMEM((rows, width), BF)], "dp_split"
    )
    a_got, b_got = yield send(a_sent, b_sent, [ORDERS[0][0], ORDERS[1][0]])
    a, a_sent, b, b_sent = step_call(
        again_kernel, bits, [a, a_got, b, b_got], [eighth] * 4,
        [pltpu.VMEM((rows // 4, width), BF)] * 2, "dp_again",
    )
    a_got, b_got = yield send(a_sent, b_sent, [ORDERS[0][1], ORDERS[1][1]])
    a, b = step_call(both_kernel, bits, [a, a_got, b, b_got], [eighth] * 2, [], "dp_both")
    for axes in zip(*rest):
        a_got, b_got = yield send(a, b, axes)
        a, b = step_call(both_kernel, bits, [a, a_got, b, b_got], [eighth] * 2, [], "dp_both")
    a_got, b_got = yield send(a, b, [ORDERS[0][1], ORDERS[1][1]])
    a, b = step_call(grow_kernel, bits, [a, a_got, b, b_got], [quarter] * 2, [], "dp_grow")
    a_got, b_got = yield send(a, b, [ORDERS[0][0], ORDERS[1][0]])
    return step_call(
        whole_kernel, bits, [a, a_got, b, b_got],
        [shaped((size, width), F32) for size in sizes], [pltpu.VMEM((rows, width), BF)], "dp_whole",
    )


class Chain:
    def __init__(self, steps):
        self.steps = steps
        self.done = None
        self.got = next(self.steps)

    def go_on(self):
        try:
            self.got = self.steps.send(self.got)
        except StopIteration as stop:
            self.done, self.got = stop.value, []


def together(*chains):
    flat = list(lax.optimization_barrier(tuple(item for chain in chains for item in chain.got)))
    for chain in chains:
        chain.got, flat = flat[: len(chain.got)], flat[len(chain.got) :]


def small_chain(held, sent, keep, own_rows):
    (got,) = yield [swap(sent, "mp", 1)]
    held = held + got
    sent = jnp.concatenate([held[keep + own_rows :], held[own_rows : keep + own_rows]], axis=0)
    (got,) = yield [swap(sent, "mp", 2)]
    held = held[: keep + own_rows] + got
    masks = dp_masks()
    for shift in masks[:-1]:
        (got,) = yield [swap(held, "dp", shift)]
        held = held + got
    (got,) = yield [swap(held, "dp", masks[-1])]
    return held, got


def collect_kernel(ids_ref, sums2_ref, sums1_ref, tokens_ref, table0_ref, table1_ref, *refs):
    upb_refs, joint_refs, (out_ref, sent_ref) = refs[:2], refs[2:6], refs[6:]
    upb_lines = [upb_refs[1][8:16, :], upb_refs[1][0:8, :], upb_refs[0][8:16, :], upb_refs[0][0:8, :]]
    out_ref[...] = jnp.zeros_like(out_ref)
    sent_ref[...] = jnp.zeros_like(sent_ref)
    table = table0_ref[...] + table1_ref[...]

    def total(values):
        return jnp.sum(values, axis=0, keepdims=True)

    lines = [total(sums2_ref[8 * i : 8 * i + 8, :]) for i in range(6)]
    lines += [total(sums1_ref[8 * i : 8 * i + 8, :]) for i in range(2)]
    images = [total(tokens_ref[i]) for i in range(tokens_ref.shape[0])]
    for group in range(GROUPS):
        found = jnp.zeros_like(images[0])
        for at, values in enumerate(images):
            found = found + jnp.where(ids_ref[at] == group, values, 0.0)
        lines.append(found)
    for at, values in enumerate(lines):
        out_ref[8 + at : 9 + at, :] = values
        sent_ref[8 + at : 9 + at, :] = values
    hidden = upb_refs[0].shape[1]
    for which in range(4):
        ref = out_ref if which % 2 == 0 else sent_ref
        base = 0 if which < 2 else 24
        ref[base : base + 1, :hidden] = total(upb_lines[which])
        joint = total(joint_refs[which][...])
        ref[base + 1 : base + 2, : joint.shape[1]] = joint
        per = table.shape[0] // (out_ref.shape[1] // LANES)
        own = per // 4
        for chunk in range(out_ref.shape[1] // LANES):
            ref[base + 2 : base + 2 + own, chunk * LANES : (chunk + 1) * LANES] = table[
                chunk * per + which * own : chunk * per + (which + 1) * own, :
            ]


def collect(ids, sums2, sums1, tokens, tables, upbs, joints):
    width = sums2.shape[1]
    vmem = pl.BlockSpec(memory_space=pltpu.VMEM)
    return pl.pallas_call(
        collect_kernel,
        out_shape=(shaped((32, width), F32), shaped((32, width), F32)),
        in_specs=[pl.BlockSpec(memory_space=pltpu.SMEM)] + [vmem] * 11,
        out_specs=(vmem, vmem),
        cost_estimate=cost(1),
        name="collect",
    )(ids, *placed([sums2, sums1, tokens, *tables, *upbs, *joints], [sums1, tokens, *tables]))


def emit_kernel(held_ref, got_ref, *outs):
    own = outs[9].shape[0]
    value = held_ref[...] + got_ref[...]
    for at in range(8):
        outs[at][...] = value[8 + at : 9 + at, :].reshape(-1)
    outs[8][...] = value[16:24, :]
    outs[9][...] = value[1:2, :own].reshape(-1)
    outs[10][...] = value[1:2, 2 * own : 3 * own].reshape(-1)
    outs[11][...] = value[2 : 2 + outs[11].shape[0], : outs[11].shape[1]]
    outs[12][...] = value[0:1, : outs[12].shape[0]].reshape(-1)


def emit(held, got, own, table_shape, hidden):
    width = held.shape[1]
    return pl.pallas_call(
        emit_kernel,
        out_shape=[shaped((width,), F32)] * 8
        + [
            shaped((GROUPS, width), F32),
            shaped((own,), F32),
            shaped((own,), F32),
            shaped(table_shape, F32),
            shaped((hidden,), F32),
        ],
        cost_estimate=cost(1),
        name="emit",
    )(held, got)


def local(
    patches, dataset_id, patch_masks, mask_tokens, key_mask, bias_index, norm1_gain, norm1_shift,
    qkv_weight, query_bias, value_bias, bias_table, out_weight, out_bias, gamma_attn, norm2_gain,
    norm2_shift, up_weight, up_bias, down_weight, down_bias, gamma_mlp, cotangent,
):
    rows, width = patches.shape
    images = rows // SEQ
    place = lax.axis_index("mp")
    own = qkv_weight.shape[2]
    own_heads = own // HEAD
    table_rows = bias_table.shape[0]
    chunks = width // LANES
    hidden = up_weight.shape[1]

    ids = lax.dynamic_slice_in_dim(dataset_id, place * images, images, 0)
    keys_here = lax.dynamic_slice_in_dim(key_mask, place * images, images, 0)
    mask = jnp.where(keys_here > 0, 0.0, -1e30).astype(F32)[:, :, None]
    sel_table = patch_masks.astype(F32)[:, :, None]
    images3 = patches.reshape(images, SEQ, width)
    cot3 = cotangent.reshape(images, SEQ, width)
    index = bias_index.T
    mix = (ids, images3, sel_table, mask_tokens)

    parity = lax.axis_index("dp") & 1
    side = parity.reshape(1)
    qkv_own = qkv_weight.transpose(1, 2, 0).reshape(3 * own, width)
    small, attn_half, down_half, pack0 = prepare(
        side, qkv_own, out_weight, down_weight, query_bias, value_bias, up_bias, bias_table.T
    )
    small0, small1 = (small, 0), (swap(small, "mp", 1), 0)
    attn_p2 = swap(attn_half, "mp", 2)
    down_p2 = swap(down_half, "mp", 2)
    pack1 = swap(pack0, "mp", 1)
    bias_near = position_bias([small0, small1], 2 * own_heads, index)
    up2 = swap(pinned(up_weight, bias_near), "mp", 2)
    up1, down1 = swap(up_weight, "mp", 1), swap(down_weight, "mp", 1)

    norm1 = [norm1_gain, norm1_shift]
    x1, j0, probs0, c0, part = attend(
        mix, norm1, qkv_own, (out_weight, 0), small0, bias_near, 0, mask
    )
    part, attn_p2 = lax.optimization_barrier((part, attn_p2))
    attn_q2 = swap(attn_p2, "dp", 1)
    attn_p3 = swap(attn_p2, "mp", 1)
    small2, small3 = (attn_p2, 2 * own // SMALL_ROWS), (attn_p3, 2 * own // SMALL_ROWS)
    j1, probs1, c1, part = attend(mix, norm1, pack1, (pack1, 3), small1, bias_near, 1, mask, x1, part)
    part, index = lax.optimization_barrier((part, index))
    bias_far = position_bias([small2, small3], 2 * own_heads, index)
    part, bias_far, attn_q2, down_p2 = lax.optimization_barrier((part, bias_far, attn_q2, down_p2))
    attn_q3 = swap(attn_q2, "mp", 1)
    down_q2 = swap(down_p2, "dp", 1)
    down_p3 = swap(down_p2, "mp", 1)
    j2, probs2, c2, part, pack2 = attend(
        mix, norm1, attn_p2, attn_q2, small2, bias_far, 0, mask, x1, part, side
    )
    j3, probs3, c3, attn_value, middle, normed2, pack3 = attend(
        mix, [norm2_gain, norm2_shift], attn_p3, attn_q3, small3, bias_far, 1, mask, x1, part, side,
        [out_bias, gamma_attn],
    )

    x2 = normed2.reshape(rows, width)
    x2, up2, down_q2 = lax.optimization_barrier((x2, up2, down_q2))
    up3 = swap(up2, "mp", 1)
    down_q3 = swap(down_q2, "mp", 1)
    value, grad2, m3, m2, upb32 = mlp(
        x2, cotangent, gamma_mlp, [(up3, down_p3, down_q3, small3), (up2, down_p2, down_q2, small2)],
        None, side,
    )
    mlp_far = plus(m2, swap(m3, "mp", 1))
    x2, mlp_far = lax.optimization_barrier((x2, mlp_far))
    mr2 = swap(mlp_far, "mp", 2)
    value, grad2, m1, m0, upb10 = mlp(
        x2, cotangent, gamma_mlp, [(up1, down1, small1), (up_weight, down_weight, small0)],
        (value, grad2), side,
    )

    shape3 = (images, SEQ, width)
    output, grad_middle, grad_attn, sums2 = middle_back(
        value.reshape(shape3), grad2.reshape(shape3), middle, attn_value, cot3,
        [down_bias, gamma_mlp, gamma_attn, norm2_gain],
    )

    mr1 = [swap(m1[:width], "mp", 1), swap(m1[width:], "mp", 1)]
    grad_attn, *mr1 = lax.optimization_barrier((grad_attn, *mr1))
    g1, js1, g3, js3, total13, carried = attend_back(
        ids, x1, grad_attn,
        [(j1, probs1, c1, pack1, 0, pack1, 3), (j3, probs3, c3, pack3, 0, pack3, 3)], None, None,
    )
    mlp_sum = [
        (own.astype(F32) + near.astype(F32) + far.astype(F32)).astype(BF)
        for own, near, far in zip((m0[:width], m0[width:]), mr1, (mr2[:width], mr2[width:]))
    ]
    carried, *mlp_sum = lax.optimization_barrier((carried, *mlp_sum))
    up_sum, down_sum = lax.psum(tuple(mlp_sum), "dp")
    r3 = swap(g3, "mp", 1)
    g2, js2, total2, carried = attend_back(
        ids, x1, grad_attn, [(j2, probs2, c2, pack2, 0, pack2, 3)], carried, None
    )
    far = plus(g2, r3)
    carried, far, g1 = lax.optimization_barrier((carried, far, g1))
    r1 = swap(g1, "mp", 1)
    r2 = swap(far, "mp", 2)
    g0, js0, total0, patch_grad, sums1, token_images = attend_back(
        ids, x1, grad_attn, [(j0, probs0, c0, qkv_own, 0, out_weight, 0)], carried,
        (images3, sel_table, mask_tokens, grad_middle, norm1_gain),
    )
    totals = [(total0, 0), (total13, 0), (total2, 0), (total13, 1)]
    blocks = SEQ // TABLE_ROWS
    table0 = table_sums(totals, index, chunks, 0, blocks // 2)
    g0, r1, r2, table0 = lax.optimization_barrier((g0, r1, r2, table0))
    tail = Chain(dp_chain([g0, r1, r2], [3 * own, own]))
    table1 = table_sums(totals, index, chunks, blocks // 2, blocks - blocks // 2)
    held, sent = collect(
        ids, sums2, sums1, token_images, [table0, table1], [upb32, upb10], [js0, js1, js2, js3]
    )
    tail.go_on()
    small = Chain(small_chain(held, sent, 16, 8))
    joint = 0
    while tail.done is None or small.done is None:
        going = [chain for chain in (tail, small) if chain.done is None]
        joint += 1
        if joint == 3:
            going[0].got[0], up_sum, down_sum = lax.optimization_barrier(
                (going[0].got[0], up_sum, down_sum)
            )
        together(*going)
        for chain in going:
            chain.go_on()
    qkv_sum, out_sum = tail.done
    up_sum, down_sum = up_sum.astype(F32), down_sum.astype(F32)
    (
        gamma_mlp_grad, down_bias_grad, gain2_grad, shift2_grad, gamma_attn_grad, out_bias_grad,
        gain1_grad, shift1_grad, token_grad, qb_grad, vb_grad, table_grad, upb_grad,
    ) = emit(*small.done, own, (own_heads, table_rows), hidden)

    return (
        output.reshape(rows, width),
        patch_grad.reshape(rows, width),
        token_grad,
        gain1_grad,
        shift1_grad,
        qkv_sum.reshape(3, own, width).transpose(2, 0, 1),
        qb_grad,
        vb_grad,
        table_grad.T,
        out_sum,
        out_bias_grad,
        gamma_attn_grad,
        gain2_grad,
        shift2_grad,
        up_sum,
        upb_grad,
        down_sum,
        down_bias_grad,
        gamma_mlp_grad,
    )


def solution(mesh):
    return jax.shard_map(
        local,
        mesh=mesh,
        in_specs=(
            P(("dp", "mp"), None), P("dp"), P(), P(), P("dp", None), P(), P(), P(),
            P(None, None, "mp"), P("mp"), P("mp"), P(None, "mp"), P("mp", None), P(), P(), P(), P(),
            P(None, "mp"), P("mp"), P("mp", None), P(), P(), P(("dp", "mp"), None),
        ),
        out_specs=(
            P(("dp", "mp"), None), P(("dp", "mp"), None), P(), P(), P(), P(None, None, "mp"),
            P("mp"), P("mp"), P(None, "mp"), P("mp", None), P(), P(), P(), P(), P(None, "mp"),
            P("mp"), P("mp", None), P(), P(),
        ),
        check_vma=False,
    )
```

```python
import functools

import jax
import jax.numpy as jnp
from jax import lax
from jax.experimental import pallas as pl
from jax.experimental.pallas import tpu as pltpu
from jax.sharding import PartitionSpec as P

HEAD = 64
SEQ = 200
GROUPS = 8
LANES = 128
BF = jnp.bfloat16
F32 = jnp.float32


def dot_nn(left, right):
    return lax.dot_general(left, right, (((1,), (0,)), ((), ())), preferred_element_type=F32)


def dot_nt(left, right):
    return lax.dot_general(left, right, (((1,), (1,)), ((), ())), preferred_element_type=F32)


def dot_tn(left, right):
    return lax.dot_general(left, right, (((0,), (0,)), ((), ())), preferred_element_type=F32)


def params(mib, steps=1):
    return pltpu.CompilerParams(
        dimension_semantics=("arbitrary",) * steps, vmem_limit_bytes=mib << 20
    )


def cost(micros):
    return pl.CostEstimate(flops=int(micros * 1.1e8), transcendentals=0, bytes_accessed=0)


def whole(shape, at=0):
    zeros = (0,) * (len(shape) - 1)
    return pl.BlockSpec(shape, lambda *_: (at,) + zeros, pipeline_mode=pl.Buffered(1))


def image_spec(width):
    return pl.BlockSpec((1, SEQ, width), lambda i, *_: (i, 0, 0))


def resident(shape):
    zeros = (0,) * len(shape)
    return pl.BlockSpec(shape, lambda *_: zeros)


def placed(operands, keep=()):
    return [
        item
        if any(item is kept for kept in keep)
        else pltpu.with_memory_space_constraint(item, pltpu.HBM)
        for item in operands
    ]


def in_hbm(shape, dtype):
    return pltpu.HBM(tuple(shape), dtype)


def shaped(shape, dtype):
    return jax.ShapeDtypeStruct(shape, dtype)


TILE = 40


def normalise(values):
    mean = jnp.mean(values, axis=-1, keepdims=True)
    centred = values - mean
    spread = jnp.mean(centred * centred, axis=-1, keepdims=True)
    scale = lax.rsqrt(spread + 1e-06)
    return centred * scale, scale


def normalise_back(grad, gain, xhat, scale):
    u = grad * gain
    return (
        u - jnp.mean(u, axis=-1, keepdims=True) - xhat * jnp.mean(u * xhat, axis=-1, keepdims=True)
    ) * scale


def line(ref):
    return ref[...].reshape(1, -1)


def token_line(ids_ref, token_ref):
    tokens = token_ref[...].astype(F32)
    group = lax.broadcasted_iota(jnp.int32, tokens.shape, 0)
    return jnp.sum(jnp.where(group == ids_ref[pl.program_id(0)], tokens, 0.0), axis=0, keepdims=True)


def mixed(patch_ref, sel_ref, token, at):
    sel = sel_ref[0, at : at + TILE, :]
    return patch_ref[0, at : at + TILE, :].astype(F32) * (1.0 - sel) + sel * token, sel


def tiles():
    return range(0, SEQ, TILE)


def fold(values):
    return jnp.sum(values.reshape(values.shape[0] // 8, 8, values.shape[1]), axis=0)


SMALL_ROWS = 16


def prepare_kernel(
    side_ref, qkv_ref, out_ref, down_ref, qb_ref, vb_ref, upb_ref, table_ref,
    small_ref, attn_ref, half_ref, pack_ref,
):
    own = qb_ref.shape[0]
    width = small_ref.shape[1]
    small_ref[...] = jnp.zeros_like(small_ref)
    small_ref[0:1, :own] = line(qb_ref)
    small_ref[0:1, 2 * own : 3 * own] = line(vb_ref)
    small_ref[1:2, : upb_ref.shape[0]] = line(upb_ref)
    small_ref[2 : 2 + table_ref.shape[0], : table_ref.shape[1]] = table_ref[...]
    attn_ref[2 * own :, :] = small_ref[...]
    pack_ref[: 3 * own, :] = qkv_ref[...]
    pack_ref[3 * own :, :] = out_ref[...]

    @pl.when(side_ref[0] == 0)
    def _():
        attn_ref[: 2 * own, :] = qkv_ref[: 2 * own, :]
        half_ref[...] = down_ref[:, : width // 2]

    @pl.when(side_ref[0] == 1)
    def _():
        attn_ref[:own, :] = qkv_ref[2 * own :, :]
        attn_ref[own : 2 * own, :] = out_ref[...]
        half_ref[...] = down_ref[:, width // 2 :]


def prepare(side, qkv, out, down, qb, vb, upb, table):
    width = out.shape[1]
    vmem = pl.BlockSpec(memory_space=pltpu.VMEM)
    return pl.pallas_call(
        prepare_kernel,
        out_shape=[
            shaped((SMALL_ROWS, width), BF),
            shaped((2 * qb.shape[0] + SMALL_ROWS, width), BF),
            shaped((down.shape[0], width // 2), BF),
            shaped((4 * qb.shape[0], width), BF),
        ],
        in_specs=[pl.BlockSpec(memory_space=pltpu.SMEM)] + [vmem] * 7,
        out_specs=[vmem] * 4,
        compiler_params=params(8, 0),
        cost_estimate=cost(2),
        name="prepare",
    )(side, *placed([qkv, out, down, qb, vb, upb, table]))


def bias_kernel(near_ref, far_ref, narrow_ref, out_ref, index_ref):
    own = out_ref.shape[0] // 2
    chunks = near_ref.shape[1] // LANES
    tables = (near_ref[...].astype(F32), far_ref[...].astype(F32))
    index_ref[...] = jnp.zeros_like(index_ref)
    index_ref[:, : narrow_ref.shape[1]] = narrow_ref[...]

    def rows_of(step, _):
        row = pl.multiple_of(step * 8, 8)
        for col in range(0, index_ref.shape[1], LANES):
            index = index_ref[pl.ds(row, 8), col : col + LANES]
            low = index & (LANES - 1)
            high = index >> 7
            for head in range(2 * own):
                table, at = tables[head // own], 2 + head % own
                found = jnp.zeros((8, LANES), F32)
                for chunk in range(chunks):
                    source = jnp.broadcast_to(
                        table[at : at + 1, chunk * LANES : (chunk + 1) * LANES], (8, LANES)
                    )
                    picked = jnp.take_along_axis(source, low, axis=1)
                    found = jnp.where(high == chunk, picked, found)
                out_ref[head, pl.ds(row, 8), col : col + LANES] = found
        return 0

    lax.fori_loop(0, SEQ // 8, rows_of, 0, unroll=5)


def small_spec(small):
    return whole((SMALL_ROWS, small[0].shape[1]), small[1])


def position_bias(small, heads, index):
    return pl.pallas_call(
        bias_kernel,
        out_shape=shaped((heads, SEQ, 2 * LANES), F32),
        grid=(1,),
        in_specs=[small_spec(item) for item in small] + [whole(index.shape)],
        out_specs=resident((heads, SEQ, 2 * LANES)),
        scratch_shapes=[pltpu.VMEM((SEQ, 2 * LANES), jnp.int32)],
        compiler_params=params(6),
        cost_estimate=cost(2),
        name="position_bias",
    )(*placed([item for item, _ in small] + [index]))


TABLE_ROWS = 8


def table_kernel(*refs):
    total_refs, (index_ref, out_ref) = refs[:-2], refs[-2:]

    @pl.when(pl.program_id(0) == 0)
    def _():
        out_ref[...] = jnp.zeros_like(out_ref)

    chunks = out_ref.shape[0] // sum(ref.shape[0] for ref in total_refs)
    spots = lax.broadcasted_iota(jnp.int32, (LANES, SEQ), 0)
    acc = jnp.zeros(out_ref.shape, F32)
    for row in range(TABLE_ROWS):
        index = index_ref[row : row + 1, :]
        hot = (spots == (index & (LANES - 1))).astype(F32).astype(BF)
        high = index >> 7
        total = jnp.concatenate([ref[:, row, :] for ref in total_refs], axis=0)
        parts = [jnp.where(high == chunk, total, 0.0) for chunk in range(chunks)]
        acc = acc + dot_nt(jnp.concatenate(parts, axis=0).astype(BF), hot)
    out_ref[...] += acc


def table_sums(totals, index, chunks, first, steps):
    own = totals[0][0].shape[0]
    heads = own * len(totals)
    return pl.pallas_call(
        table_kernel,
        out_shape=shaped((chunks * heads, LANES), F32),
        grid=(steps,),
        in_specs=[
            pl.BlockSpec((own, TABLE_ROWS, SEQ), lambda i, at=at: (at, first + i, 0))
            for _, at in totals
        ]
        + [pl.BlockSpec((TABLE_ROWS, SEQ), lambda i: (first + i, 0))],
        out_specs=resident((chunks * heads, LANES)),
        compiler_params=params(6),
        cost_estimate=cost(5),
        name="table_sums",
    )(*placed([total for total, _ in totals] + [index]))


def block(values, at):
    return values[:, at * LANES : (at + 1) * LANES]


def turned(values):
    return pltpu.roll(values, HEAD, 1)


def only(keep, values):
    return jnp.where(keep, values, jnp.zeros_like(values))


def lower_lanes():
    return lax.broadcasted_iota(jnp.int32, (SEQ, LANES), 1) < HEAD


def shard_forward(x, weight_ref, small_ref, bias_ref, mask, joint_ref, probs_ref, context_ref, base):
    width = joint_ref.shape[2]
    own = width // 3
    low = lower_lanes()
    high = jnp.logical_not(low)
    column = lax.broadcasted_iota(jnp.int32, (1, width), 1)
    scale = jnp.where(column < own, HEAD**-0.5, 1.0)
    joint = dot_nt(x, weight_ref[...])
    joint_ref[0] = ((joint + small_ref[...].astype(F32)[0:1, :width]) * scale).astype(BF)
    joint = joint_ref[0]
    b1, b2, b3 = block(joint, 1), block(joint, 2), block(joint, 3)
    t0, t1 = turned(block(joint, 0)), turned(b1)
    left = [only(high, b1), only(low, b2), only(high, b2)]
    right = [t0, t0, t1]
    value = [b3, b3, joint[:, 4 * LANES :]]
    heads = range(3)
    scores = [dot_nt(left[i], right[i]) + bias_ref[base + i][:, :SEQ] + mask for i in heads]
    raised = [jnp.exp(item - jnp.max(item, axis=0, keepdims=True)) for item in scores]
    probs = [(item * (1.0 / jnp.sum(item, axis=0, keepdims=True))).astype(BF) for item in raised]
    for i in heads:
        probs_ref[0, base + i] = probs[i]
    found = [dot_tn(probs[i], value[i]) for i in heads]
    context_ref[0, :, :LANES] = jnp.where(low, found[0], found[1]).astype(BF)
    context_ref[0, :, LANES:] = found[2].astype(BF)


def attend_kernel(first, last, parted, *refs):
    refs = list(refs)

    def take(count):
        found = refs[:count]
        del refs[:count]
        return found

    if first or last:
        (ids_ref,) = take(1)
    if parted:
        (side_ref,) = take(1)
    if first or last:
        patch_ref, sel_ref, token_ref, gain_ref, shift_ref = take(5)
    if last:
        obias_ref, gamma_ref = take(2)
    if not first:
        x_ref, part_in_ref = take(2)
    weight_ref, out_ref, small_ref, bias_ref, mask_ref = take(5)
    if first:
        (x_ref,) = take(1)
    joint_ref, probs_ref, context_ref, part_ref = take(4)
    if last:
        middle_ref, normed_ref = take(2)
    if parted:
        p_ref, q_ref = weight_ref, out_ref
        (pack_ref,) = take(1)
        half = p_ref.shape[0] - SMALL_ROWS

        @pl.when(pl.program_id(0) == 0)
        def _():
            for side in range(2):
                @pl.when(side_ref[0] == side)
                def _():
                    pack_ref[side * half : (side + 1) * half, :] = p_ref[:half, :]
                    pack_ref[(1 - side) * half : (2 - side) * half, :] = q_ref[:half, :]

        joint = joint_ref.shape[2]
        weight_ref, out_ref = pack_ref.at[:joint], pack_ref.at[joint:]
    if first:
        token = token_line(ids_ref, token_ref)
        for at in tiles():
            start, _ = mixed(patch_ref, sel_ref, token, at)
            xhat, _ = normalise(start)
            x_ref[0, at : at + TILE, :] = (xhat * line(gain_ref) + line(shift_ref)).astype(BF)
    shard_forward(
        x_ref[0], weight_ref, small_ref, bias_ref, mask_ref[0], joint_ref, probs_ref, context_ref, 0
    )
    part = dot_nn(context_ref[0], out_ref[...])
    part_ref[0] = part if first else part + part_in_ref[0]
    if last:
        token = token_line(ids_ref, token_ref)
        for at in tiles():
            rows = slice(at, at + TILE)
            start, _ = mixed(patch_ref, sel_ref, token, at)
            value = part_ref[0, rows, :] + line(obias_ref)
            middle = start + line(gamma_ref) * value
            xhat, _ = normalise(middle)
            part_ref[0, rows, :] = value
            middle_ref[0, rows, :] = middle
            normed_ref[0, rows, :] = (xhat * line(gain_ref) + line(shift_ref)).astype(BF)


def mix_specs(width, groups):
    return [
        image_spec(width),
        pl.BlockSpec((1, SEQ, 1), lambda i, ids, *_: (ids[i], 0, 0)),
        whole((groups, width)),
    ]


def attend(mix, norm, weight, out, small, bias, turn, mask, x=None, part=None, side=None, after=None):
    ids, patches, sel_table, tokens = mix
    images, _, width = patches.shape
    heads = bias.shape[0] // 2
    own = heads * HEAD
    first, last, parted = x is None, after is not None, side is not None
    prefetch, in_specs, operands = [], [], []
    if first or last:
        prefetch.append(ids)
    if parted:
        prefetch.append(side)
    if first or last:
        in_specs += mix_specs(width, tokens.shape[0]) + [whole((width,))] * 2
        operands += [patches, sel_table, tokens, *norm]
    if last:
        in_specs += [whole((width,))] * 2
        operands += list(after)
    if not first:
        in_specs += [image_spec(width)] * 2
        operands += [x, part]
    if parted:
        in_specs += [whole(weight.shape), whole(out.shape)]
    else:
        in_specs += [whole((3 * own, width)), whole((own, width), out[1])]
        out = out[0]
    in_specs += [small_spec(small)]
    in_specs += [whole((heads,) + bias.shape[1:], turn), image_spec(1)]
    operands += [weight, out, small[0], bias, mask]
    outs = [
        (in_hbm((images, SEQ, 3 * own), BF), image_spec(3 * own)),
        (
            in_hbm((images, heads, SEQ, SEQ), BF),
            pl.BlockSpec((1, heads, SEQ, SEQ), lambda i, *_: (i, 0, 0, 0)),
        ),
        (in_hbm((images, SEQ, own), BF), image_spec(own)),
        (shaped(patches.shape, F32), image_spec(width)),
    ]
    if first:
        outs = [(in_hbm(patches.shape, BF), image_spec(width))] + outs
    if last:
        outs += [
            (shaped(patches.shape, F32), image_spec(width)),
            (shaped(patches.shape, BF), image_spec(width)),
        ]
    if parted:
        outs.append((in_hbm((4 * own, width), BF), resident((4 * own, width))))
    return pl.pallas_call(
        functools.partial(attend_kernel, first, last, parted),
        out_shape=[shape for shape, _ in outs],
        grid_spec=pltpu.PrefetchScalarGridSpec(
            num_scalar_prefetch=len(prefetch),
            grid=(images,),
            in_specs=in_specs,
            out_specs=[spec for _, spec in outs],
        ),
        compiler_params=params(14),
        cost_estimate=cost(9),
        name="attend",
    )(*prefetch, *placed(operands, [part, bias]))


def shards_backward(x, grad, shards, total_ref):
    low = lower_lanes()
    high = jnp.logical_not(low)
    left, right, queries, keys, probs = [], [], [], [], []
    for joint_ref, probs_ref, _, _, out_ref, _, _, _ in shards:
        grad_context = dot_nt(grad, out_ref[...]).astype(BF)
        d0, d1 = grad_context[:, :LANES], grad_context[:, LANES:]
        joint = joint_ref[0]
        b3 = block(joint, 3)
        t0, t1, t2 = turned(block(joint, 0)), turned(block(joint, 1)), turned(block(joint, 2))
        left += [only(low, b3), only(high, b3), joint[:, 4 * LANES :]]
        right += [d0, d0, d1]
        queries += [t0, t0, t1]
        keys += [t1, t2, t2]
        probs += [probs_ref[0, i] for i in range(3)]
    heads = range(len(left))
    grad_probs = [dot_nt(left[i], right[i]) for i in heads]
    grads_v = [dot_nn(probs[i], right[i]) for i in heads]
    grad_scores = []
    for i in heads:
        wide = probs[i].astype(F32)
        centre = jnp.sum(wide * grad_probs[i], axis=0, keepdims=True)
        grad_scores.append((wide * (grad_probs[i] - centre)).astype(BF))
    for i in heads:
        total_ref[i] += grad_scores[i].astype(F32)
    grads_k = [dot_nn(grad_scores[i], queries[i]) for i in heads]
    grads_q = [dot_tn(grad_scores[i], keys[i]) for i in heads]
    scale = HEAD**-0.5
    part = None
    for which, (_, _, context_ref, weight_ref, _, sums_ref, acc_ref, joint_grad_ref) in enumerate(shards):
        gq, gk, gv = (items[3 * which : 3 * which + 3] for items in (grads_q, grads_k, grads_v))
        blocks = [
            jnp.where(low, gq[0], gq[1]) * scale,
            jnp.where(low, gq[2] * scale, gk[0]),
            jnp.where(low, gk[1], gk[2]),
            jnp.where(low, gv[0], gv[1]),
            gv[2],
        ]
        for at, values in enumerate(blocks):
            cols = slice(at * LANES, at * LANES + values.shape[1])
            held = values.astype(BF)
            joint_grad_ref[:, cols] = held
            sums_ref[:, cols] += fold(held.astype(F32))
        width = joint_grad_ref.shape[1]
        joint_grad = joint_grad_ref[...]
        acc_ref[:width, :] += dot_tn(joint_grad, x)
        acc_ref[width:, :] += dot_tn(context_ref[0], grad)
        own = dot_nn(joint_grad, weight_ref[...])
        part = own if part is None else part + own
    return part


def attend_back_kernel(first, last, count, *refs):
    refs = list(refs)

    def take(number):
        found = refs[:number]
        del refs[:number]
        return found

    (ids_ref,) = take(1)
    if last:
        patch_ref, sel_ref, token_ref, gmiddle_ref, gain_ref = take(5)
    if not first:
        (carried_ref,) = take(1)
    x_ref, grad_ref = take(2)
    inputs = [take(5) for _ in range(count)]
    outputs = [take(2) for _ in range(count)]
    (total_ref,) = take(1)
    if last:
        patch_out_ref, norm_ref, token_out_ref = take(3)
    else:
        (carry_out_ref,) = take(1)
    scratch = [take(2) for _ in range(count)]
    step = pl.program_id(0)

    @pl.when(step == 0)
    def _():
        zeroed = [total_ref] + [item[1] for item in outputs] + [item[0] for item in scratch]
        for ref in zeroed + ([norm_ref] if last else []):
            ref[...] = jnp.zeros_like(ref)

    shards = [
        (*ins, out[1], own[0], own[1]) for ins, out, own in zip(inputs, outputs, scratch)
    ]
    part = shards_backward(x_ref[0], grad_ref[0], shards, total_ref)
    if not first:
        part = part + carried_ref[0]
    if last:
        (carry_ref,) = refs
        carry_ref[...] = part
        token = token_line(ids_ref, token_ref)
        token_sum = jnp.zeros((8, part.shape[1]), F32)
        for at in tiles():
            rows = slice(at, at + TILE)
            start, sel = mixed(patch_ref, sel_ref, token, at)
            xhat, scale = normalise(start)
            grad_normed = carry_ref[rows, :]
            norm_ref[0:8, :] += fold(grad_normed * xhat)
            norm_ref[8:16, :] += fold(grad_normed)
            grad_start = gmiddle_ref[0, rows, :] + normalise_back(
                grad_normed, line(gain_ref), xhat, scale
            )
            patch_out_ref[0, rows, :] = grad_start * (1.0 - sel)
            token_sum = token_sum + fold(grad_start * sel)
        token_out_ref[0] = token_sum
    else:
        carry_out_ref[0] = part

    @pl.when(step == pl.num_programs(0) - 1)
    def _():
        for out, own in zip(outputs, scratch):
            out[0][...] = own[0][...].astype(BF)


def attend_back(ids, x, grad, shards, carried, tail):
    images, _, width = x.shape
    joint_width = shards[0][0].shape[2]
    own = joint_width // 3
    heads = own // HEAD
    count = len(shards)
    square = pl.BlockSpec((1, heads, SEQ, SEQ), lambda i, *_: (i, 0, 0, 0))
    first, last = carried is None, tail is not None
    in_specs = [image_spec(width)] * 2
    operands = [x, grad]
    for joint, probs, context, weight, weight_at, out, out_at in shards:
        in_specs += [image_spec(joint_width), square, image_spec(own)]
        in_specs += [whole((joint_width, width), weight_at), whole((own, width), out_at)]
        operands += [joint, probs, context, weight, out]
    if not first:
        in_specs = [image_spec(width)] + in_specs
        operands = [carried] + operands
    out_shape, out_specs, scratch = [], [], []
    for _ in shards:
        out_shape += [in_hbm((joint_width + own, width), BF), in_hbm((8, joint_width), F32)]
        out_specs += [resident((joint_width + own, width)), resident((8, joint_width))]
        scratch += [pltpu.VMEM((joint_width + own, width), F32), pltpu.VMEM((SEQ, joint_width), BF)]
    out_shape.append(in_hbm((count * heads, SEQ, SEQ), F32))
    out_specs.append(resident((count * heads, SEQ, SEQ)))
    if last:
        patches, sel_table, tokens, grad_middle, gain = tail
        in_specs = (
            mix_specs(width, tokens.shape[0]) + [image_spec(width), whole((width,))] + in_specs
        )
        operands = [patches, sel_table, tokens, grad_middle, gain] + operands
        out_shape += [
            shaped(x.shape, F32), shaped((16, width), F32), shaped((images, 8, width), F32)
        ]
        out_specs += [
            image_spec(width),
            resident((16, width)),
            pl.BlockSpec((1, 8, width), lambda i, *_: (i, 0, 0)),
        ]
        scratch.append(pltpu.VMEM((SEQ, width), F32))
    else:
        out_shape.append(in_hbm(x.shape, F32))
        out_specs.append(image_spec(width))
    return pl.pallas_call(
        functools.partial(attend_back_kernel, first, last, count),
        out_shape=out_shape,
        grid_spec=pltpu.PrefetchScalarGridSpec(
            num_scalar_prefetch=1,
            grid=(images,),
            in_specs=in_specs,
            out_specs=out_specs,
            scratch_shapes=scratch,
        ),
        compiler_params=params(14 if count == 1 else 24),
        cost_estimate=cost(13 * count),
        name="attend_back",
    )(ids, *placed(operands))


MLP_MIB = 40


def mlp_kernel(first, lengths, *refs):
    refs = list(refs)

    def take(number):
        found = refs[:number]
        del refs[:number]
        return found

    count = len(lengths)
    (side_ref,) = take(1)
    x_ref, cot_ref, gamma_ref = take(3)
    shards = [take(length) for length in lengths]
    if not first:
        carried = take(2)
    totals = take(2)
    grads = take(count)
    upb_grad_ref, gm_ref, up_ref, down_ref, held_ref, value_ref, grad_ref, in_sem, out_sem, sem = refs
    accs = (value_ref, grad_ref)
    step = pl.program_id(0)

    def moves(sources, targets, sems):
        return [
            pltpu.make_async_copy(source, target, sems.at[at])
            for at, (source, target) in enumerate(zip(sources, targets))
        ]

    def weights(at):
        shard = shards[at]
        if len(shard) == 3:
            targets = [up_ref.at[at], down_ref.at[at]]
        else:
            half = shard[1].shape[1]
            places = [
                pl.ds(pl.multiple_of(place * half, LANES), half)
                for place in (side_ref[0], 1 - side_ref[0])
            ]
            targets = [up_ref.at[at]] + [down_ref.at[at, :, place] for place in places]
        return moves(shard[:-1], targets, in_sem.at[at])

    @pl.when(step == 0)
    def _():
        for at in range(count):
            for move in weights(at):
                move.start()
        if first:
            for ref in accs:
                ref[...] = jnp.zeros_like(ref)
        else:
            for move in moves(carried, accs, sem):
                move.start()
        gm_ref[...] = (line(gamma_ref) * cot_ref[...].astype(F32)).astype(BF)

    for at in range(count):
        @pl.when(step == at)
        def _():
            for move in weights(at):
                move.wait()

    x = x_ref[...]
    gm = gm_ref[...]
    up = up_ref[step]
    down = down_ref[step]
    upb = shards[0][-1][...].astype(F32)[1:2, :]
    for at in range(1, count):
        upb = jnp.where(step == at, shards[at][-1][...].astype(F32)[1:2, :], upb)
    before = dot_nn(x, up) + upb
    share = 0.5 + 0.5 * lax.erf(before * (0.5**0.5))
    density = jnp.exp(before * before * -0.5) * ((2.0 * jnp.pi) ** -0.5)
    hidden = (before * share).astype(BF)
    slope = share + before * density
    grad_before = (dot_nt(gm, down) * slope).astype(BF)
    upb_grad_ref[...] = fold(grad_before.astype(F32))
    held_ref[step, x.shape[1] :, :] = dot_tn(hidden, gm).astype(BF)
    held_ref[step, : x.shape[1], :] = dot_tn(x, grad_before).astype(BF)
    for at in range(count):
        @pl.when(step == at)
        def _():
            pltpu.make_async_copy(held_ref.at[at], grads[at], out_sem.at[at]).start()

    if not first:
        @pl.when(step == 0)
        def _():
            for move in moves(carried, accs, sem):
                move.wait()

    value_ref[...] += dot_nn(hidden, down)
    grad_ref[...] += dot_nt(grad_before, up)

    @pl.when(step == count - 1)
    def _():
        for move in moves(accs, totals, sem):
            move.start()
        for move in moves(accs, totals, sem):
            move.wait()
        for at in range(count):
            pltpu.make_async_copy(held_ref.at[at], grads[at], out_sem.at[at]).wait()


def mlp(x, cot, gamma, shards, carried, side):
    rows, width = x.shape
    hidden = shards[0][0].shape[1]
    first = carried is None
    count = len(shards)
    anywhere = pl.BlockSpec(memory_space=pl.ANY)
    in_specs = [whole((rows, width)), whole((rows, width)), whole((width,))]
    operands = [x, cot, gamma]
    for shard in shards:
        in_specs += [anywhere] * (len(shard) - 1) + [small_spec(shard[-1])]
        operands += list(shard[:-1]) + [shard[-1][0]]
    aliases = {}
    if not first:
        at = len(operands) + 1
        aliases = {at: 0, at + 1: 1}
        in_specs += [anywhere] * 2
        operands += list(carried)
    total = shaped((rows, width), F32)
    grads = [in_hbm((width + hidden, width), BF)]
    grad_specs = [anywhere]
    return pl.pallas_call(
        functools.partial(mlp_kernel, first, [len(shard) for shard in shards]),
        out_shape=[total, total] + grads * count + [shaped((8 * count, hidden), F32)],
        grid_spec=pltpu.PrefetchScalarGridSpec(
            num_scalar_prefetch=1,
            grid=(count,),
            in_specs=in_specs,
            out_specs=[anywhere] * 2
            + grad_specs * count
            + [pl.BlockSpec((8, hidden), lambda i, *_: (i, 0))],
            scratch_shapes=[
                pltpu.VMEM((rows, width), BF),
                pltpu.VMEM((count, width, hidden), BF),
                pltpu.VMEM((count, hidden, width), BF),
                pltpu.VMEM((count, width + hidden, width), BF),
                pltpu.VMEM((rows, width), F32),
                pltpu.VMEM((rows, width), F32),
                pltpu.SemaphoreType.DMA((count, 3)),
                pltpu.SemaphoreType.DMA((count,)),
                pltpu.SemaphoreType.DMA((2,)),
            ],
        ),
        input_output_aliases=aliases,
        compiler_params=params(MLP_MIB),
        cost_estimate=cost(9 * count),
        name="mlp",
    )(side, *placed(operands, [x] + list(carried or [])))


def middle_back_kernel(
    value_ref, grad_ref, middle_ref, attn_ref, cot_ref, dbias_ref, gmlp_ref, gattn_ref, gain_ref,
    out_ref, gmiddle_ref, gattn_out_ref, sums_ref,
):
    @pl.when(pl.program_id(0) == 0)
    def _():
        sums_ref[...] = jnp.zeros_like(sums_ref)

    def add(row, values):
        sums_ref[8 * row : 8 * row + 8, :] += fold(values)

    for at in tiles():
        rows = slice(at, at + TILE)
        value = value_ref[0, rows, :] + line(dbias_ref)
        cot = cot_ref[0, rows, :].astype(F32)
        middle = middle_ref[0, rows, :]
        out_ref[0, rows, :] = (middle + line(gmlp_ref) * value).astype(BF)
        add(0, cot * value)
        add(1, (line(gmlp_ref) * cot).astype(BF).astype(F32))
        xhat, scale = normalise(middle)
        grad = grad_ref[0, rows, :]
        add(2, grad * xhat)
        add(3, grad)
        grad_middle = cot + normalise_back(grad, line(gain_ref), xhat, scale)
        gmiddle_ref[0, rows, :] = grad_middle
        add(4, grad_middle * attn_ref[0, rows, :])
        grad_attn = (line(gattn_ref) * grad_middle).astype(BF)
        gattn_out_ref[0, rows, :] = grad_attn
        add(5, grad_attn.astype(F32))


def middle_back(value, grad, middle, attn, cot, vectors):
    images, _, width = middle.shape
    return pl.pallas_call(
        middle_back_kernel,
        out_shape=(
            in_hbm(middle.shape, BF),
            in_hbm(middle.shape, F32),
            in_hbm(middle.shape, BF),
            shaped((48, width), F32),
        ),
        grid=(images,),
        in_specs=[image_spec(width)] * 5 + [whole((width,))] * 4,
        out_specs=(image_spec(width),) * 3 + (resident((48, width)),),
        compiler_params=params(12),
        cost_estimate=cost(5),
        name="middle_back",
    )(*placed([value, grad, middle, attn, cot, *vectors], [value, grad, middle, attn]))


def swap(values, axis, mask):
    count = lax.axis_size(axis)
    return lax.ppermute(values, axis, [(i, i ^ mask) for i in range(count)])


def dp_masks():
    count = lax.axis_size("dp")
    return [1 << bit for bit in range(count.bit_length() - 1)]


def pinned(value, *others):
    return lax.optimization_barrier((value,) + others)[0]


def plus(left, right):
    return (left.astype(F32) + right.astype(F32)).astype(BF)


ORDERS = ((0, 1), (1, 2))


def axis_bits():
    place = lax.axis_index("dp")
    return jnp.stack([(place >> bit) & 1 for bit in range(len(dp_masks()))]).astype(jnp.int32)


def halves_of(ref, base, size, bit):
    keep = pl.multiple_of(base + bit * size, 16)
    sent = pl.multiple_of(base + (1 - bit) * size, 16)
    return ref[pl.ds(keep, size), :], ref[pl.ds(sent, size), :]


def split_kernel(bits_ref, a_ref, b_ref, c_ref, *refs):
    outs, total_ref = refs[:4], refs[4]
    for at in range(0, total_ref.shape[0], 64):
        rows = slice(at, at + 64)
        total_ref[rows, :] = (
            a_ref[rows, :].astype(F32) + b_ref[rows, :].astype(F32) + c_ref[rows, :].astype(F32)
        ).astype(BF)
    part = total_ref.shape[0] // 2
    for which in range(2):
        keep, sent = halves_of(total_ref, which * part, part // 2, bits_ref[ORDERS[which][0]])
        outs[2 * which][...] = keep
        outs[2 * which + 1][...] = sent


def again_kernel(bits_ref, *refs):
    ins, outs, totals = refs[:4], refs[4:8], refs[8:]
    for which in range(2):
        total_ref = totals[which]
        total_ref[...] = plus(ins[2 * which][...], ins[2 * which + 1][...])
        size = total_ref.shape[0] // 2
        keep, sent = halves_of(total_ref, 0, size, bits_ref[ORDERS[which][1]])
        outs[2 * which][...] = keep
        outs[2 * which + 1][...] = sent


def both_kernel(bits_ref, *refs):
    for which in range(2):
        refs[4 + which][...] = plus(refs[2 * which][...], refs[2 * which + 1][...])


def put(out_ref, base, own, other, bit):
    size = own.shape[0]
    out_ref[pl.ds(pl.multiple_of(base + bit * size, 16), size), :] = own.astype(out_ref.dtype)
    out_ref[pl.ds(pl.multiple_of(base + (1 - bit) * size, 16), size), :] = other.astype(out_ref.dtype)


def grow_kernel(bits_ref, *refs):
    for which in range(2):
        put(refs[4 + which], 0, refs[2 * which][...], refs[2 * which + 1][...], bits_ref[ORDERS[which][1]])


def whole_kernel(bits_ref, *refs):
    ins, (*out_refs, total_ref) = refs[:4], refs[4:]
    part = total_ref.shape[0] // 2
    for which in range(2):
        put(total_ref, which * part, ins[2 * which][...], ins[2 * which + 1][...], bits_ref[ORDERS[which][0]])
    base = 0
    for out_ref in out_refs:
        out_ref[...] = total_ref[base : base + out_ref.shape[0], :].astype(F32)
        base += out_ref.shape[0]


def step_call(kernel, bits, arrays, outs, scratch, name):
    vmem = pl.BlockSpec(memory_space=pltpu.VMEM)
    return pl.pallas_call(
        kernel,
        out_shape=outs,
        in_specs=[pl.BlockSpec(memory_space=pltpu.SMEM)] + [vmem] * len(arrays),
        out_specs=[vmem] * len(outs),
        scratch_shapes=scratch,
        compiler_params=params(12, 0),
        cost_estimate=cost(1),
        name=name,
    )(bits, *arrays)


def dp_chain(pieces, sizes):
    bits = axis_bits()
    masks = dp_masks()
    rows, width = pieces[0].shape
    quarter, eighth = shaped((rows // 4, width), BF), shaped((rows // 8, width), BF)
    rest = [[axis for axis in range(len(masks)) if axis not in order] for order in ORDERS]

    def send(a, b, axes):
        return [swap(array, "dp", masks[axis]) for array, axis in zip((a, b), axes)]

    a, a_sent, b, b_sent = step_call(
        split_kernel, bits, placed(pieces), [quarter] * 4, [pltpu.VMEM((rows, width), BF)], "dp_split"
    )
    a_got, b_got = yield send(a_sent, b_sent, [ORDERS[0][0], ORDERS[1][0]])
    a, a_sent, b, b_sent = step_call(
        again_kernel, bits, [a, a_got, b, b_got], [eighth] * 4,
        [pltpu.VMEM((rows // 4, width), BF)] * 2, "dp_again",
    )
    a_got, b_got = yield send(a_sent, b_sent, [ORDERS[0][1], ORDERS[1][1]])
    a, b = step_call(both_kernel, bits, [a, a_got, b, b_got], [eighth] * 2, [], "dp_both")
    for axes in zip(*rest):
        a_got, b_got = yield send(a, b, axes)
        a, b = step_call(both_kernel, bits, [a, a_got, b, b_got], [eighth] * 2, [], "dp_both")
    a_got, b_got = yield send(a, b, [ORDERS[0][1], ORDERS[1][1]])
    a, b = step_call(grow_kernel, bits, [a, a_got, b, b_got], [quarter] * 2, [], "dp_grow")
    a_got, b_got = yield send(a, b, [ORDERS[0][0], ORDERS[1][0]])
    return step_call(
        whole_kernel, bits, [a, a_got, b, b_got],
        [shaped((size, width), F32) for size in sizes], [pltpu.VMEM((rows, width), BF)], "dp_whole",
    )


class Chain:
    def __init__(self, steps):
        self.steps = steps
        self.done = None
        self.got = next(self.steps)

    def go_on(self):
        try:
            self.got = self.steps.send(self.got)
        except StopIteration as stop:
            self.done, self.got = stop.value, []


def together(*chains):
    flat = list(lax.optimization_barrier(tuple(item for chain in chains for item in chain.got)))
    for chain in chains:
        chain.got, flat = flat[: len(chain.got)], flat[len(chain.got) :]


def small_chain(held, sent, keep, own_rows):
    (got,) = yield [swap(sent, "mp", 1)]
    held = held + got
    sent = jnp.concatenate([held[keep + own_rows :], held[own_rows : keep + own_rows]], axis=0)
    (got,) = yield [swap(sent, "mp", 2)]
    held = held[: keep + own_rows] + got
    masks = dp_masks()
    for shift in masks[:-1]:
        (got,) = yield [swap(held, "dp", shift)]
        held = held + got
    (got,) = yield [swap(held, "dp", masks[-1])]
    return held, got


def collect_kernel(ids_ref, sums2_ref, sums1_ref, tokens_ref, table_ref, *refs):
    upb_refs, joint_refs, (out_ref, sent_ref) = refs[:2], refs[2:6], refs[6:]
    upb_lines = [upb_refs[1][8:16, :], upb_refs[1][0:8, :], upb_refs[0][8:16, :], upb_refs[0][0:8, :]]
    out_ref[...] = jnp.zeros_like(out_ref)
    sent_ref[...] = jnp.zeros_like(sent_ref)
    table = table_ref[...]

    def total(values):
        return jnp.sum(values, axis=0, keepdims=True)

    lines = [total(sums2_ref[8 * i : 8 * i + 8, :]) for i in range(6)]
    lines += [total(sums1_ref[8 * i : 8 * i + 8, :]) for i in range(2)]
    images = [total(tokens_ref[i]) for i in range(tokens_ref.shape[0])]
    for group in range(GROUPS):
        found = jnp.zeros_like(images[0])
        for at, values in enumerate(images):
            found = found + jnp.where(ids_ref[at] == group, values, 0.0)
        lines.append(found)
    for at, values in enumerate(lines):
        out_ref[8 + at : 9 + at, :] = values
        sent_ref[8 + at : 9 + at, :] = values
    hidden = upb_refs[0].shape[1]
    for which in range(4):
        ref = out_ref if which % 2 == 0 else sent_ref
        base = 0 if which < 2 else 24
        ref[base : base + 1, :hidden] = total(upb_lines[which])
        joint = total(joint_refs[which][...])
        ref[base + 1 : base + 2, : joint.shape[1]] = joint
        per = table.shape[0] // (out_ref.shape[1] // LANES)
        own = per // 4
        for chunk in range(out_ref.shape[1] // LANES):
            ref[base + 2 : base + 2 + own, chunk * LANES : (chunk + 1) * LANES] = table[
                chunk * per + which * own : chunk * per + (which + 1) * own, :
            ]


def collect(ids, sums2, sums1, tokens, tables, upbs, joints):
    width = sums2.shape[1]
    vmem = pl.BlockSpec(memory_space=pltpu.VMEM)
    return pl.pallas_call(
        collect_kernel,
        out_shape=(shaped((32, width), F32), shaped((32, width), F32)),
        in_specs=[pl.BlockSpec(memory_space=pltpu.SMEM)] + [vmem] * 10,
        out_specs=(vmem, vmem),
        cost_estimate=cost(1),
        name="collect",
    )(ids, *placed([sums2, sums1, tokens, *tables, *upbs, *joints], [sums1, tokens, *tables]))


def emit_kernel(held_ref, got_ref, *outs):
    own = outs[9].shape[0]
    value = held_ref[...] + got_ref[...]
    for at in range(8):
        outs[at][...] = value[8 + at : 9 + at, :].reshape(-1)
    outs[8][...] = value[16:24, :]
    outs[9][...] = value[1:2, :own].reshape(-1)
    outs[10][...] = value[1:2, 2 * own : 3 * own].reshape(-1)
    outs[11][...] = value[2 : 2 + outs[11].shape[0], : outs[11].shape[1]]
    outs[12][...] = value[0:1, : outs[12].shape[0]].reshape(-1)


def emit(held, got, own, table_shape, hidden):
    width = held.shape[1]
    return pl.pallas_call(
        emit_kernel,
        out_shape=[shaped((width,), F32)] * 8
        + [
            shaped((GROUPS, width), F32),
            shaped((own,), F32),
            shaped((own,), F32),
            shaped(table_shape, F32),
            shaped((hidden,), F32),
        ],
        cost_estimate=cost(1),
        name="emit",
    )(held, got)


def local(
    patches, dataset_id, patch_masks, mask_tokens, key_mask, bias_index, norm1_gain, norm1_shift,
    qkv_weight, query_bias, value_bias, bias_table, out_weight, out_bias, gamma_attn, norm2_gain,
    norm2_shift, up_weight, up_bias, down_weight, down_bias, gamma_mlp, cotangent,
):
    rows, width = patches.shape
    images = rows // SEQ
    place = lax.axis_index("mp")
    own = qkv_weight.shape[2]
    own_heads = own // HEAD
    table_rows = bias_table.shape[0]
    chunks = width // LANES
    hidden = up_weight.shape[1]

    ids = lax.dynamic_slice_in_dim(dataset_id, place * images, images, 0)
    keys_here = lax.dynamic_slice_in_dim(key_mask, place * images, images, 0)
    mask = jnp.where(keys_here > 0, 0.0, -1e30).astype(F32)[:, :, None]
    sel_table = patch_masks.astype(F32)[:, :, None]
    images3 = patches.reshape(images, SEQ, width)
    cot3 = cotangent.reshape(images, SEQ, width)
    index = bias_index.T
    mix = (ids, images3, sel_table, mask_tokens)

    parity = lax.axis_index("dp") & 1
    side = parity.reshape(1)
    qkv_own = qkv_weight.transpose(1, 2, 0).reshape(3 * own, width)
    small, attn_half, down_half, pack0 = prepare(
        side, qkv_own, out_weight, down_weight, query_bias, value_bias, up_bias, bias_table.T
    )
    small0, small1 = (small, 0), (swap(small, "mp", 1), 0)
    attn_p2 = swap(attn_half, "mp", 2)
    down_p2 = swap(down_half, "mp", 2)
    pack1 = swap(pack0, "mp", 1)
    bias_near = position_bias([small0, small1], 2 * own_heads, index)
    up2 = swap(pinned(up_weight, bias_near), "mp", 2)
    up1, down1 = swap(up_weight, "mp", 1), swap(down_weight, "mp", 1)

    norm1 = [norm1_gain, norm1_shift]
    x1, j0, probs0, c0, part = attend(
        mix, norm1, qkv_own, (out_weight, 0), small0, bias_near, 0, mask
    )
    part, attn_p2 = lax.optimization_barrier((part, attn_p2))
    attn_q2 = swap(attn_p2, "dp", 1)
    attn_p3 = swap(attn_p2, "mp", 1)
    small2, small3 = (attn_p2, 2 * own // SMALL_ROWS), (attn_p3, 2 * own // SMALL_ROWS)
    j1, probs1, c1, part = attend(mix, norm1, pack1, (pack1, 3), small1, bias_near, 1, mask, x1, part)
    part, index = lax.optimization_barrier((part, index))
    bias_far = position_bias([small2, small3], 2 * own_heads, index)
    part, bias_far, attn_q2, down_p2 = lax.optimization_barrier((part, bias_far, attn_q2, down_p2))
    attn_q3 = swap(attn_q2, "mp", 1)
    down_q2 = swap(down_p2, "dp", 1)
    down_p3 = swap(down_p2, "mp", 1)
    j2, probs2, c2, part, pack2 = attend(
        mix, norm1, attn_p2, attn_q2, small2, bias_far, 0, mask, x1, part, side
    )
    j3, probs3, c3, attn_value, middle, normed2, pack3 = attend(
        mix, [norm2_gain, norm2_shift], attn_p3, attn_q3, small3, bias_far, 1, mask, x1, part, side,
        [out_bias, gamma_attn],
    )

    x2 = normed2.reshape(rows, width)
    x2, up2, down_q2 = lax.optimization_barrier((x2, up2, down_q2))
    up3 = swap(up2, "mp", 1)
    down_q3 = swap(down_q2, "mp", 1)
    value, grad2, m3, m2, upb32 = mlp(
        x2, cotangent, gamma_mlp, [(up3, down_p3, down_q3, small3), (up2, down_p2, down_q2, small2)],
        None, side,
    )
    mlp_far = plus(m2, swap(m3, "mp", 1))
    x2, mlp_far = lax.optimization_barrier((x2, mlp_far))
    mr2 = swap(mlp_far, "mp", 2)
    value, grad2, m1, m0, upb10 = mlp(
        x2, cotangent, gamma_mlp, [(up1, down1, small1), (up_weight, down_weight, small0)],
        (value, grad2), side,
    )

    shape3 = (images, SEQ, width)
    output, grad_middle, grad_attn, sums2 = middle_back(
        value.reshape(shape3), grad2.reshape(shape3), middle, attn_value, cot3,
        [down_bias, gamma_mlp, gamma_attn, norm2_gain],
    )

    mr1 = [swap(m1[:width], "mp", 1), swap(m1[width:], "mp", 1)]
    grad_attn, *mr1 = lax.optimization_barrier((grad_attn, *mr1))
    g1, js1, g3, js3, total13, carried = attend_back(
        ids, x1, grad_attn,
        [(j1, probs1, c1, pack1, 0, pack1, 3), (j3, probs3, c3, pack3, 0, pack3, 3)], None, None,
    )
    mlp_sum = [
        (own.astype(F32) + near.astype(F32) + far.astype(F32)).astype(BF)
        for own, near, far in zip((m0[:width], m0[width:]), mr1, (mr2[:width], mr2[width:]))
    ]
    carried, *mlp_sum = lax.optimization_barrier((carried, *mlp_sum))
    up_sum, down_sum = lax.psum(tuple(mlp_sum), "dp")
    r3 = swap(g3, "mp", 1)
    g2, js2, total2, carried = attend_back(
        ids, x1, grad_attn, [(j2, probs2, c2, pack2, 0, pack2, 3)], carried, None
    )
    far = plus(g2, r3)
    carried, far, g1 = lax.optimization_barrier((carried, far, g1))
    r1 = swap(g1, "mp", 1)
    r2 = swap(far, "mp", 2)
    g0, js0, total0, patch_grad, sums1, token_images = attend_back(
        ids, x1, grad_attn, [(j0, probs0, c0, qkv_own, 0, out_weight, 0)], carried,
        (images3, sel_table, mask_tokens, grad_middle, norm1_gain),
    )
    totals = [(total0, 0), (total13, 0), (total2, 0), (total13, 1)]
    blocks = SEQ // TABLE_ROWS
    table = table_sums(totals, index, chunks, 0, blocks)
    held, sent = collect(
        ids, sums2, sums1, token_images, [table], [upb32, upb10], [js0, js1, js2, js3]
    )
    g0, r1, r2, sent = lax.optimization_barrier((g0, r1, r2, sent))
    tail = Chain(dp_chain([g0, r1, r2], [3 * own, own]))
    small = Chain(small_chain(held, sent, 16, 8))
    joint = 0
    while tail.done is None or small.done is None:
        going = [chain for chain in (tail, small) if chain.done is None]
        joint += 1
        if joint == 4:
            going[0].got[0], up_sum, down_sum = lax.optimization_barrier(
                (going[0].got[0], up_sum, down_sum)
            )
        together(*going)
        for chain in going:
            chain.go_on()
    qkv_sum, out_sum = tail.done
    up_sum, down_sum = up_sum.astype(F32), down_sum.astype(F32)
    (
        gamma_mlp_grad, down_bias_grad, gain2_grad, shift2_grad, gamma_attn_grad, out_bias_grad,
        gain1_grad, shift1_grad, token_grad, qb_grad, vb_grad, table_grad, upb_grad,
    ) = emit(*small.done, own, (own_heads, table_rows), hidden)

    return (
        output.reshape(rows, width),
        patch_grad.reshape(rows, width),
        token_grad,
        gain1_grad,
        shift1_grad,
        qkv_sum.reshape(3, own, width).transpose(2, 0, 1),
        qb_grad,
        vb_grad,
        table_grad.T,
        out_sum,
        out_bias_grad,
        gamma_attn_grad,
        gain2_grad,
        shift2_grad,
        up_sum,
        upb_grad,
        down_sum,
        down_bias_grad,
        gamma_mlp_grad,
    )


def solution(mesh):
    return jax.shard_map(
        local,
        mesh=mesh,
        in_specs=(
            P(("dp", "mp"), None), P("dp"), P(), P(), P("dp", None), P(), P(), P(),
            P(None, None, "mp"), P("mp"), P("mp"), P(None, "mp"), P("mp", None), P(), P(), P(), P(),
            P(None, "mp"), P("mp"), P("mp", None), P(), P(), P(("dp", "mp"), None),
        ),
        out_specs=(
            P(("dp", "mp"), None), P(("dp", "mp"), None), P(), P(), P(), P(None, None, "mp"),
            P("mp"), P("mp"), P(None, "mp"), P("mp", None), P(), P(), P(), P(), P(None, "mp"),
            P("mp"), P("mp", None), P(), P(),
        ),
        check_vma=False,
    )
```

```python
import functools

import jax
import jax.numpy as jnp
from jax import lax
from jax.experimental import pallas as pl
from jax.experimental.pallas import tpu as pltpu
from jax.sharding import PartitionSpec as P

HEAD = 64
SEQ = 200
GROUPS = 8
LANES = 128
BF = jnp.bfloat16
F32 = jnp.float32


def dot_nn(left, right):
    return lax.dot_general(left, right, (((1,), (0,)), ((), ())), preferred_element_type=F32)


def dot_nt(left, right):
    return lax.dot_general(left, right, (((1,), (1,)), ((), ())), preferred_element_type=F32)


def dot_tn(left, right):
    return lax.dot_general(left, right, (((0,), (0,)), ((), ())), preferred_element_type=F32)


def params(mib, steps=1):
    return pltpu.CompilerParams(
        dimension_semantics=("arbitrary",) * steps, vmem_limit_bytes=mib << 20
    )


def cost(micros):
    return pl.CostEstimate(flops=int(micros * 1.1e8), transcendentals=0, bytes_accessed=0)


def whole(shape, at=0):
    zeros = (0,) * (len(shape) - 1)
    return pl.BlockSpec(shape, lambda *_: (at,) + zeros, pipeline_mode=pl.Buffered(1))


def image_spec(width):
    return pl.BlockSpec((1, SEQ, width), lambda i, *_: (i, 0, 0))


def resident(shape):
    zeros = (0,) * len(shape)
    return pl.BlockSpec(shape, lambda *_: zeros)


def placed(operands, keep=()):
    return [
        item
        if any(item is kept for kept in keep)
        else pltpu.with_memory_space_constraint(item, pltpu.HBM)
        for item in operands
    ]


def in_hbm(shape, dtype):
    return pltpu.HBM(tuple(shape), dtype)


def shaped(shape, dtype):
    return jax.ShapeDtypeStruct(shape, dtype)


TILE = 40


def normalise(values):
    mean = jnp.mean(values, axis=-1, keepdims=True)
    centred = values - mean
    spread = jnp.mean(centred * centred, axis=-1, keepdims=True)
    scale = lax.rsqrt(spread + 1e-06)
    return centred * scale, scale


def normalise_back(grad, gain, xhat, scale):
    u = grad * gain
    return (
        u - jnp.mean(u, axis=-1, keepdims=True) - xhat * jnp.mean(u * xhat, axis=-1, keepdims=True)
    ) * scale


def line(ref):
    return ref[...].reshape(1, -1)


def token_line(ids_ref, token_ref):
    tokens = token_ref[...].astype(F32)
    group = lax.broadcasted_iota(jnp.int32, tokens.shape, 0)
    return jnp.sum(jnp.where(group == ids_ref[pl.program_id(0)], tokens, 0.0), axis=0, keepdims=True)


def mixed(patch_ref, sel_ref, token, at):
    sel = sel_ref[0, at : at + TILE, :]
    return patch_ref[0, at : at + TILE, :].astype(F32) * (1.0 - sel) + sel * token, sel


def tiles():
    return range(0, SEQ, TILE)


def fold(values):
    return jnp.sum(values.reshape(values.shape[0] // 8, 8, values.shape[1]), axis=0)


SMALL_ROWS = 16


def prepare_kernel(
    side_ref, qkv_ref, out_ref, down_ref, qb_ref, vb_ref, upb_ref, table_ref,
    small_ref, attn_ref, half_ref, pack_ref,
):
    own = qb_ref.shape[0]
    width = small_ref.shape[1]
    small_ref[...] = jnp.zeros_like(small_ref)
    small_ref[0:1, :own] = line(qb_ref)
    small_ref[0:1, 2 * own : 3 * own] = line(vb_ref)
    small_ref[1:2, : upb_ref.shape[0]] = line(upb_ref)
    small_ref[2 : 2 + table_ref.shape[0], : table_ref.shape[1]] = table_ref[...]
    attn_ref[2 * own :, :] = small_ref[...]
    pack_ref[: 3 * own, :] = qkv_ref[...]
    pack_ref[3 * own :, :] = out_ref[...]

    @pl.when(side_ref[0] == 0)
    def _():
        attn_ref[: 2 * own, :] = qkv_ref[: 2 * own, :]
        half_ref[...] = down_ref[:, : width // 2]

    @pl.when(side_ref[0] == 1)
    def _():
        attn_ref[:own, :] = qkv_ref[2 * own :, :]
        attn_ref[own : 2 * own, :] = out_ref[...]
        half_ref[...] = down_ref[:, width // 2 :]


def prepare(side, qkv, out, down, qb, vb, upb, table):
    width = out.shape[1]
    vmem = pl.BlockSpec(memory_space=pltpu.VMEM)
    return pl.pallas_call(
        prepare_kernel,
        out_shape=[
            shaped((SMALL_ROWS, width), BF),
            shaped((2 * qb.shape[0] + SMALL_ROWS, width), BF),
            shaped((down.shape[0], width // 2), BF),
            shaped((4 * qb.shape[0], width), BF),
        ],
        in_specs=[pl.BlockSpec(memory_space=pltpu.SMEM)] + [vmem] * 7,
        out_specs=[vmem] * 4,
        compiler_params=params(8, 0),
        cost_estimate=cost(2),
        name="prepare",
    )(side, *placed([qkv, out, down, qb, vb, upb, table]))


def bias_kernel(near_ref, far_ref, narrow_ref, out_ref, index_ref):
    own = out_ref.shape[0] // 2
    chunks = near_ref.shape[1] // LANES
    tables = (near_ref[...].astype(F32), far_ref[...].astype(F32))
    index_ref[...] = jnp.zeros_like(index_ref)
    index_ref[:, : narrow_ref.shape[1]] = narrow_ref[...]

    def rows_of(step, _):
        row = pl.multiple_of(step * 8, 8)
        for col in range(0, index_ref.shape[1], LANES):
            index = index_ref[pl.ds(row, 8), col : col + LANES]
            low = index & (LANES - 1)
            high = index >> 7
            for head in range(2 * own):
                table, at = tables[head // own], 2 + head % own
                found = jnp.zeros((8, LANES), F32)
                for chunk in range(chunks):
                    source = jnp.broadcast_to(
                        table[at : at + 1, chunk * LANES : (chunk + 1) * LANES], (8, LANES)
                    )
                    picked = jnp.take_along_axis(source, low, axis=1)
                    found = jnp.where(high == chunk, picked, found)
                out_ref[head, pl.ds(row, 8), col : col + LANES] = found
        return 0

    lax.fori_loop(0, SEQ // 8, rows_of, 0, unroll=25)


def small_spec(small):
    return whole((SMALL_ROWS, small[0].shape[1]), small[1])


def position_bias(small, heads, index):
    return pl.pallas_call(
        bias_kernel,
        out_shape=shaped((heads, SEQ, 2 * LANES), F32),
        grid=(1,),
        in_specs=[small_spec(item) for item in small] + [whole(index.shape)],
        out_specs=resident((heads, SEQ, 2 * LANES)),
        scratch_shapes=[pltpu.VMEM((SEQ, 2 * LANES), jnp.int32)],
        compiler_params=params(6),
        cost_estimate=cost(2),
        name="position_bias",
    )(*placed([item for item, _ in small] + [index]))


TABLE_ROWS = 8


def table_kernel(*refs):
    total_refs, (index_ref, out_ref) = refs[:-2], refs[-2:]

    @pl.when(pl.program_id(0) == 0)
    def _():
        out_ref[...] = jnp.zeros_like(out_ref)

    chunks = out_ref.shape[0] // sum(ref.shape[0] for ref in total_refs)
    spots = lax.broadcasted_iota(jnp.int32, (LANES, SEQ), 0)
    acc = jnp.zeros(out_ref.shape, F32)
    for row in range(TABLE_ROWS):
        index = index_ref[row : row + 1, :]
        hot = (spots == (index & (LANES - 1))).astype(F32).astype(BF)
        high = index >> 7
        total = jnp.concatenate([ref[:, row, :] for ref in total_refs], axis=0)
        parts = [jnp.where(high == chunk, total, 0.0) for chunk in range(chunks)]
        acc = acc + dot_nt(jnp.concatenate(parts, axis=0).astype(BF), hot)
    out_ref[...] += acc


def table_sums(totals, index, chunks, first, steps):
    own = totals[0][0].shape[0]
    heads = own * len(totals)
    return pl.pallas_call(
        table_kernel,
        out_shape=shaped((chunks * heads, LANES), F32),
        grid=(steps,),
        in_specs=[
            pl.BlockSpec((own, TABLE_ROWS, SEQ), lambda i, at=at: (at, first + i, 0))
            for _, at in totals
        ]
        + [pl.BlockSpec((TABLE_ROWS, SEQ), lambda i: (first + i, 0))],
        out_specs=resident((chunks * heads, LANES)),
        compiler_params=params(6),
        cost_estimate=cost(5),
        name="table_sums",
    )(*placed([total for total, _ in totals] + [index]))


def block(values, at):
    return values[:, at * LANES : (at + 1) * LANES]


def turned(values):
    return pltpu.roll(values, HEAD, 1)


def only(keep, values):
    return jnp.where(keep, values, jnp.zeros_like(values))


def lower_lanes():
    return lax.broadcasted_iota(jnp.int32, (SEQ, LANES), 1) < HEAD


def shard_forward(x, weight_ref, small_ref, bias_ref, mask, joint_ref, probs_ref, context_ref, base):
    width = joint_ref.shape[2]
    own = width // 3
    low = lower_lanes()
    high = jnp.logical_not(low)
    column = lax.broadcasted_iota(jnp.int32, (1, width), 1)
    scale = jnp.where(column < own, HEAD**-0.5, 1.0)
    joint = dot_nt(x, weight_ref[...])
    joint_ref[0] = ((joint + small_ref[...].astype(F32)[0:1, :width]) * scale).astype(BF)
    joint = joint_ref[0]
    b1, b2, b3 = block(joint, 1), block(joint, 2), block(joint, 3)
    t0, t1 = turned(block(joint, 0)), turned(b1)
    left = [only(high, b1), only(low, b2), only(high, b2)]
    right = [t0, t0, t1]
    value = [b3, b3, joint[:, 4 * LANES :]]
    heads = range(3)
    scores = [dot_nt(left[i], right[i]) + bias_ref[base + i][:, :SEQ] + mask for i in heads]
    raised = [jnp.exp(item - jnp.max(item, axis=0, keepdims=True)) for item in scores]
    probs = [(item * (1.0 / jnp.sum(item, axis=0, keepdims=True))).astype(BF) for item in raised]
    for i in heads:
        probs_ref[0, base + i] = probs[i]
    found = [dot_tn(probs[i], value[i]) for i in heads]
    context_ref[0, :, :LANES] = jnp.where(low, found[0], found[1]).astype(BF)
    context_ref[0, :, LANES:] = found[2].astype(BF)


def attend_kernel(first, last, parted, *refs):
    refs = list(refs)

    def take(count):
        found = refs[:count]
        del refs[:count]
        return found

    if first or last:
        (ids_ref,) = take(1)
    if parted:
        (side_ref,) = take(1)
    if first or last:
        patch_ref, sel_ref, token_ref, gain_ref, shift_ref = take(5)
    if last:
        obias_ref, gamma_ref = take(2)
    if not first:
        x_ref, part_in_ref = take(2)
    weight_ref, out_ref, small_ref, bias_ref, mask_ref = take(5)
    if first:
        (x_ref,) = take(1)
    joint_ref, probs_ref, context_ref, part_ref = take(4)
    if last:
        middle_ref, normed_ref = take(2)
    if parted:
        p_ref, q_ref = weight_ref, out_ref
        (pack_ref,) = take(1)
        half = p_ref.shape[0] - SMALL_ROWS

        @pl.when(pl.program_id(0) == 0)
        def _():
            for side in range(2):
                @pl.when(side_ref[0] == side)
                def _():
                    pack_ref[side * half : (side + 1) * half, :] = p_ref[:half, :]
                    pack_ref[(1 - side) * half : (2 - side) * half, :] = q_ref[:half, :]

        joint = joint_ref.shape[2]
        weight_ref, out_ref = pack_ref.at[:joint], pack_ref.at[joint:]
    if first:
        token = token_line(ids_ref, token_ref)
        for at in tiles():
            start, _ = mixed(patch_ref, sel_ref, token, at)
            xhat, _ = normalise(start)
            x_ref[0, at : at + TILE, :] = (xhat * line(gain_ref) + line(shift_ref)).astype(BF)
    shard_forward(
        x_ref[0], weight_ref, small_ref, bias_ref, mask_ref[0], joint_ref, probs_ref, context_ref, 0
    )
    part = dot_nn(context_ref[0], out_ref[...])
    part_ref[0] = part if first else part + part_in_ref[0]
    if last:
        token = token_line(ids_ref, token_ref)
        for at in tiles():
            rows = slice(at, at + TILE)
            start, _ = mixed(patch_ref, sel_ref, token, at)
            value = part_ref[0, rows, :] + line(obias_ref)
            middle = start + line(gamma_ref) * value
            xhat, _ = normalise(middle)
            part_ref[0, rows, :] = value
            middle_ref[0, rows, :] = middle
            normed_ref[0, rows, :] = (xhat * line(gain_ref) + line(shift_ref)).astype(BF)


def mix_specs(width, groups):
    return [
        image_spec(width),
        pl.BlockSpec((1, SEQ, 1), lambda i, ids, *_: (ids[i], 0, 0)),
        whole((groups, width)),
    ]


def attend(mix, norm, weight, out, small, bias, turn, mask, x=None, part=None, side=None, after=None):
    ids, patches, sel_table, tokens = mix
    images, _, width = patches.shape
    heads = bias.shape[0] // 2
    own = heads * HEAD
    first, last, parted = x is None, after is not None, side is not None
    prefetch, in_specs, operands = [], [], []
    if first or last:
        prefetch.append(ids)
    if parted:
        prefetch.append(side)
    if first or last:
        in_specs += mix_specs(width, tokens.shape[0]) + [whole((width,))] * 2
        operands += [patches, sel_table, tokens, *norm]
    if last:
        in_specs += [whole((width,))] * 2
        operands += list(after)
    if not first:
        in_specs += [image_spec(width)] * 2
        operands += [x, part]
    if parted:
        in_specs += [whole(weight.shape), whole(out.shape)]
    else:
        in_specs += [whole((3 * own, width)), whole((own, width), out[1])]
        out = out[0]
    in_specs += [small_spec(small)]
    in_specs += [whole((heads,) + bias.shape[1:], turn), image_spec(1)]
    operands += [weight, out, small[0], bias, mask]
    outs = [
        (in_hbm((images, SEQ, 3 * own), BF), image_spec(3 * own)),
        (
            in_hbm((images, heads, SEQ, SEQ), BF),
            pl.BlockSpec((1, heads, SEQ, SEQ), lambda i, *_: (i, 0, 0, 0)),
        ),
        (in_hbm((images, SEQ, own), BF), image_spec(own)),
        (shaped(patches.shape, F32), image_spec(width)),
    ]
    if first:
        outs = [(in_hbm(patches.shape, BF), image_spec(width))] + outs
    if last:
        outs += [
            (shaped(patches.shape, F32), image_spec(width)),
            (shaped(patches.shape, BF), image_spec(width)),
        ]
    if parted:
        outs.append((in_hbm((4 * own, width), BF), resident((4 * own, width))))
    return pl.pallas_call(
        functools.partial(attend_kernel, first, last, parted),
        out_shape=[shape for shape, _ in outs],
        grid_spec=pltpu.PrefetchScalarGridSpec(
            num_scalar_prefetch=len(prefetch),
            grid=(images,),
            in_specs=in_specs,
            out_specs=[spec for _, spec in outs],
        ),
        compiler_params=params(14),
        cost_estimate=cost(9),
        name="attend",
    )(*prefetch, *placed(operands, [part, bias]))


def shards_backward(x, grad, shards, total_ref):
    low = lower_lanes()
    high = jnp.logical_not(low)
    left, right, queries, keys, probs = [], [], [], [], []
    for joint_ref, probs_ref, _, _, out_ref, _, _, _ in shards:
        grad_context = dot_nt(grad, out_ref[...]).astype(BF)
        d0, d1 = grad_context[:, :LANES], grad_context[:, LANES:]
        joint = joint_ref[0]
        b3 = block(joint, 3)
        t0, t1, t2 = turned(block(joint, 0)), turned(block(joint, 1)), turned(block(joint, 2))
        left += [only(low, b3), only(high, b3), joint[:, 4 * LANES :]]
        right += [d0, d0, d1]
        queries += [t0, t0, t1]
        keys += [t1, t2, t2]
        probs += [probs_ref[0, i] for i in range(3)]
    heads = range(len(left))
    grad_probs = [dot_nt(left[i], right[i]) for i in heads]
    grads_v = [dot_nn(probs[i], right[i]) for i in heads]
    grad_scores = []
    for i in heads:
        wide = probs[i].astype(F32)
        centre = jnp.sum(wide * grad_probs[i], axis=0, keepdims=True)
        grad_scores.append((wide * (grad_probs[i] - centre)).astype(BF))
    for i in heads:
        total_ref[i] += grad_scores[i].astype(F32)
    grads_k = [dot_nn(grad_scores[i], queries[i]) for i in heads]
    grads_q = [dot_tn(grad_scores[i], keys[i]) for i in heads]
    scale = HEAD**-0.5
    part = None
    for which, (_, _, context_ref, weight_ref, _, sums_ref, acc_ref, joint_grad_ref) in enumerate(shards):
        gq, gk, gv = (items[3 * which : 3 * which + 3] for items in (grads_q, grads_k, grads_v))
        blocks = [
            jnp.where(low, gq[0], gq[1]) * scale,
            jnp.where(low, gq[2] * scale, gk[0]),
            jnp.where(low, gk[1], gk[2]),
            jnp.where(low, gv[0], gv[1]),
            gv[2],
        ]
        for at, values in enumerate(blocks):
            cols = slice(at * LANES, at * LANES + values.shape[1])
            held = values.astype(BF)
            joint_grad_ref[:, cols] = held
            sums_ref[:, cols] += fold(held.astype(F32))
        width = joint_grad_ref.shape[1]
        joint_grad = joint_grad_ref[...]
        acc_ref[:width, :] += dot_tn(joint_grad, x)
        acc_ref[width:, :] += dot_tn(context_ref[0], grad)
        own = dot_nn(joint_grad, weight_ref[...])
        part = own if part is None else part + own
    return part


def attend_back_kernel(first, last, count, *refs):
    refs = list(refs)

    def take(number):
        found = refs[:number]
        del refs[:number]
        return found

    (ids_ref,) = take(1)
    if last:
        patch_ref, sel_ref, token_ref, gmiddle_ref, gain_ref = take(5)
    if not first:
        (carried_ref,) = take(1)
    x_ref, grad_ref = take(2)
    inputs = [take(5) for _ in range(count)]
    outputs = [take(2) for _ in range(count)]
    (total_ref,) = take(1)
    if last:
        patch_out_ref, norm_ref, token_out_ref = take(3)
    else:
        (carry_out_ref,) = take(1)
    scratch = [take(2) for _ in range(count)]
    step = pl.program_id(0)

    @pl.when(step == 0)
    def _():
        zeroed = [total_ref] + [item[1] for item in outputs] + [item[0] for item in scratch]
        for ref in zeroed + ([norm_ref] if last else []):
            ref[...] = jnp.zeros_like(ref)

    shards = [
        (*ins, out[1], own[0], own[1]) for ins, out, own in zip(inputs, outputs, scratch)
    ]
    part = shards_backward(x_ref[0], grad_ref[0], shards, total_ref)
    if not first:
        part = part + carried_ref[0]
    if last:
        (carry_ref,) = refs
        carry_ref[...] = part
        token = token_line(ids_ref, token_ref)
        token_sum = jnp.zeros((8, part.shape[1]), F32)
        for at in tiles():
            rows = slice(at, at + TILE)
            start, sel = mixed(patch_ref, sel_ref, token, at)
            xhat, scale = normalise(start)
            grad_normed = carry_ref[rows, :]
            norm_ref[0:8, :] += fold(grad_normed * xhat)
            norm_ref[8:16, :] += fold(grad_normed)
            grad_start = gmiddle_ref[0, rows, :] + normalise_back(
                grad_normed, line(gain_ref), xhat, scale
            )
            patch_out_ref[0, rows, :] = grad_start * (1.0 - sel)
            token_sum = token_sum + fold(grad_start * sel)
        token_out_ref[0] = token_sum
    else:
        carry_out_ref[0] = part

    @pl.when(step == pl.num_programs(0) - 1)
    def _():
        for out, own in zip(outputs, scratch):
            out[0][...] = own[0][...].astype(BF)


def attend_back(ids, x, grad, shards, carried, tail):
    images, _, width = x.shape
    joint_width = shards[0][0].shape[2]
    own = joint_width // 3
    heads = own // HEAD
    count = len(shards)
    square = pl.BlockSpec((1, heads, SEQ, SEQ), lambda i, *_: (i, 0, 0, 0))
    first, last = carried is None, tail is not None
    in_specs = [image_spec(width)] * 2
    operands = [x, grad]
    for joint, probs, context, weight, weight_at, out, out_at in shards:
        in_specs += [image_spec(joint_width), square, image_spec(own)]
        in_specs += [whole((joint_width, width), weight_at), whole((own, width), out_at)]
        operands += [joint, probs, context, weight, out]
    if not first:
        in_specs = [image_spec(width)] + in_specs
        operands = [carried] + operands
    out_shape, out_specs, scratch = [], [], []
    for _ in shards:
        out_shape += [in_hbm((joint_width + own, width), BF), in_hbm((8, joint_width), F32)]
        out_specs += [resident((joint_width + own, width)), resident((8, joint_width))]
        scratch += [pltpu.VMEM((joint_width + own, width), F32), pltpu.VMEM((SEQ, joint_width), BF)]
    out_shape.append(in_hbm((count * heads, SEQ, SEQ), F32))
    out_specs.append(resident((count * heads, SEQ, SEQ)))
    if last:
        patches, sel_table, tokens, grad_middle, gain = tail
        in_specs = (
            mix_specs(width, tokens.shape[0]) + [image_spec(width), whole((width,))] + in_specs
        )
        operands = [patches, sel_table, tokens, grad_middle, gain] + operands
        out_shape += [
            shaped(x.shape, F32), shaped((16, width), F32), shaped((images, 8, width), F32)
        ]
        out_specs += [
            image_spec(width),
            resident((16, width)),
            pl.BlockSpec((1, 8, width), lambda i, *_: (i, 0, 0)),
        ]
        scratch.append(pltpu.VMEM((SEQ, width), F32))
    else:
        out_shape.append(in_hbm(x.shape, F32))
        out_specs.append(image_spec(width))
    return pl.pallas_call(
        functools.partial(attend_back_kernel, first, last, count),
        out_shape=out_shape,
        grid_spec=pltpu.PrefetchScalarGridSpec(
            num_scalar_prefetch=1,
            grid=(images,),
            in_specs=in_specs,
            out_specs=out_specs,
            scratch_shapes=scratch,
        ),
        compiler_params=params(14 if count == 1 else 24),
        cost_estimate=cost(13 * count),
        name="attend_back",
    )(ids, *placed(operands))


MLP_MIB = 40


def mlp_kernel(first, lengths, *refs):
    refs = list(refs)

    def take(number):
        found = refs[:number]
        del refs[:number]
        return found

    count = len(lengths)
    (side_ref,) = take(1)
    x_ref, cot_ref, gamma_ref = take(3)
    shards = [take(length) for length in lengths]
    if not first:
        carried = take(2)
    totals = take(2)
    grads = take(count)
    upb_grad_ref, gm_ref, up_ref, down_ref, held_ref, value_ref, grad_ref, in_sem, out_sem, sem = refs
    accs = (value_ref, grad_ref)
    step = pl.program_id(0)

    def moves(sources, targets, sems):
        return [
            pltpu.make_async_copy(source, target, sems.at[at])
            for at, (source, target) in enumerate(zip(sources, targets))
        ]

    def weights(at):
        shard = shards[at]
        if len(shard) == 3:
            targets = [up_ref.at[at], down_ref.at[at]]
        else:
            half = shard[1].shape[1]
            places = [
                pl.ds(pl.multiple_of(place * half, LANES), half)
                for place in (side_ref[0], 1 - side_ref[0])
            ]
            targets = [up_ref.at[at]] + [down_ref.at[at, :, place] for place in places]
        return moves(shard[:-1], targets, in_sem.at[at])

    @pl.when(step == 0)
    def _():
        for at in range(count):
            for move in weights(at):
                move.start()
        if first:
            for ref in accs:
                ref[...] = jnp.zeros_like(ref)
        else:
            for move in moves(carried, accs, sem):
                move.start()
        gm_ref[...] = (line(gamma_ref) * cot_ref[...].astype(F32)).astype(BF)

    for at in range(count):
        @pl.when(step == at)
        def _():
            for move in weights(at):
                move.wait()

    x = x_ref[...]
    gm = gm_ref[...]
    up = up_ref[step]
    down = down_ref[step]
    upb = shards[0][-1][...].astype(F32)[1:2, :]
    for at in range(1, count):
        upb = jnp.where(step == at, shards[at][-1][...].astype(F32)[1:2, :], upb)
    before = dot_nn(x, up) + upb
    share = 0.5 + 0.5 * lax.erf(before * (0.5**0.5))
    density = jnp.exp(before * before * -0.5) * ((2.0 * jnp.pi) ** -0.5)
    hidden = (before * share).astype(BF)
    slope = share + before * density
    grad_before = (dot_nt(gm, down) * slope).astype(BF)
    upb_grad_ref[...] = fold(grad_before.astype(F32))
    held_ref[step, x.shape[1] :, :] = dot_tn(hidden, gm).astype(BF)
    held_ref[step, : x.shape[1], :] = dot_tn(x, grad_before).astype(BF)
    for at in range(count):
        @pl.when(step == at)
        def _():
            pltpu.make_async_copy(held_ref.at[at], grads[at], out_sem.at[at]).start()

    if not first:
        @pl.when(step == 0)
        def _():
            for move in moves(carried, accs, sem):
                move.wait()

    value_ref[...] += dot_nn(hidden, down)
    grad_ref[...] += dot_nt(grad_before, up)

    @pl.when(step == count - 1)
    def _():
        for move in moves(accs, totals, sem):
            move.start()
        for move in moves(accs, totals, sem):
            move.wait()
        for at in range(count):
            pltpu.make_async_copy(held_ref.at[at], grads[at], out_sem.at[at]).wait()


def mlp(x, cot, gamma, shards, carried, side):
    rows, width = x.shape
    hidden = shards[0][0].shape[1]
    first = carried is None
    count = len(shards)
    anywhere = pl.BlockSpec(memory_space=pl.ANY)
    in_specs = [whole((rows, width)), whole((rows, width)), whole((width,))]
    operands = [x, cot, gamma]
    for shard in shards:
        in_specs += [anywhere] * (len(shard) - 1) + [small_spec(shard[-1])]
        operands += list(shard[:-1]) + [shard[-1][0]]
    aliases = {}
    if not first:
        at = len(operands) + 1
        aliases = {at: 0, at + 1: 1}
        in_specs += [anywhere] * 2
        operands += list(carried)
    total = shaped((rows, width), F32)
    grads = [in_hbm((width + hidden, width), BF)]
    grad_specs = [anywhere]
    return pl.pallas_call(
        functools.partial(mlp_kernel, first, [len(shard) for shard in shards]),
        out_shape=[total, total] + grads * count + [shaped((8 * count, hidden), F32)],
        grid_spec=pltpu.PrefetchScalarGridSpec(
            num_scalar_prefetch=1,
            grid=(count,),
            in_specs=in_specs,
            out_specs=[anywhere] * 2
            + grad_specs * count
            + [pl.BlockSpec((8, hidden), lambda i, *_: (i, 0))],
            scratch_shapes=[
                pltpu.VMEM((rows, width), BF),
                pltpu.VMEM((count, width, hidden), BF),
                pltpu.VMEM((count, hidden, width), BF),
                pltpu.VMEM((count, width + hidden, width), BF),
                pltpu.VMEM((rows, width), F32),
                pltpu.VMEM((rows, width), F32),
                pltpu.SemaphoreType.DMA((count, 3)),
                pltpu.SemaphoreType.DMA((count,)),
                pltpu.SemaphoreType.DMA((2,)),
            ],
        ),
        input_output_aliases=aliases,
        compiler_params=params(MLP_MIB),
        cost_estimate=cost(9 * count),
        name="mlp",
    )(side, *placed(operands, [x, cot] + list(carried or [])))


def middle_back_kernel(
    value_ref, grad_ref, middle_ref, attn_ref, cot_ref, dbias_ref, gmlp_ref, gattn_ref, gain_ref,
    out_ref, gmiddle_ref, gattn_out_ref, sums_ref,
):
    @pl.when(pl.program_id(0) == 0)
    def _():
        sums_ref[...] = jnp.zeros_like(sums_ref)

    def add(row, values):
        sums_ref[8 * row : 8 * row + 8, :] += fold(values)

    for at in tiles():
        rows = slice(at, at + TILE)
        value = value_ref[0, rows, :] + line(dbias_ref)
        cot = cot_ref[0, rows, :].astype(F32)
        middle = middle_ref[0, rows, :]
        out_ref[0, rows, :] = (middle + line(gmlp_ref) * value).astype(BF)
        add(0, cot * value)
        add(1, (line(gmlp_ref) * cot).astype(BF).astype(F32))
        xhat, scale = normalise(middle)
        grad = grad_ref[0, rows, :]
        add(2, grad * xhat)
        add(3, grad)
        grad_middle = cot + normalise_back(grad, line(gain_ref), xhat, scale)
        gmiddle_ref[0, rows, :] = grad_middle
        add(4, grad_middle * attn_ref[0, rows, :])
        grad_attn = (line(gattn_ref) * grad_middle).astype(BF)
        gattn_out_ref[0, rows, :] = grad_attn
        add(5, grad_attn.astype(F32))


def middle_back(value, grad, middle, attn, cot, vectors):
    images, _, width = middle.shape
    return pl.pallas_call(
        middle_back_kernel,
        out_shape=(
            in_hbm(middle.shape, BF),
            in_hbm(middle.shape, F32),
            in_hbm(middle.shape, BF),
            shaped((48, width), F32),
        ),
        grid=(images,),
        in_specs=[image_spec(width)] * 5 + [whole((width,))] * 4,
        out_specs=(image_spec(width),) * 3 + (resident((48, width)),),
        compiler_params=params(12),
        cost_estimate=cost(5),
        name="middle_back",
    )(*placed([value, grad, middle, attn, cot, *vectors], [value, grad, middle, attn]))


def swap(values, axis, mask):
    count = lax.axis_size(axis)
    return lax.ppermute(values, axis, [(i, i ^ mask) for i in range(count)])


def dp_masks():
    count = lax.axis_size("dp")
    return [1 << bit for bit in range(count.bit_length() - 1)]


def pinned(value, *others):
    return lax.optimization_barrier((value,) + others)[0]


def plus(left, right):
    return (left.astype(F32) + right.astype(F32)).astype(BF)


ORDERS = ((0, 1), (1, 2))


def axis_bits():
    place = lax.axis_index("dp")
    return jnp.stack([(place >> bit) & 1 for bit in range(len(dp_masks()))]).astype(jnp.int32)


def halves_of(ref, base, size, bit):
    keep = pl.multiple_of(base + bit * size, 16)
    sent = pl.multiple_of(base + (1 - bit) * size, 16)
    return ref[pl.ds(keep, size), :], ref[pl.ds(sent, size), :]


def split_kernel(bits_ref, a_ref, b_ref, c_ref, *refs):
    outs, total_ref = refs[:4], refs[4]
    for at in range(0, total_ref.shape[0], 64):
        rows = slice(at, at + 64)
        total_ref[rows, :] = (
            a_ref[rows, :].astype(F32) + b_ref[rows, :].astype(F32) + c_ref[rows, :].astype(F32)
        ).astype(BF)
    part = total_ref.shape[0] // 2
    for which in range(2):
        keep, sent = halves_of(total_ref, which * part, part // 2, bits_ref[ORDERS[which][0]])
        outs[2 * which][...] = keep
        outs[2 * which + 1][...] = sent


def again_kernel(bits_ref, *refs):
    ins, outs, totals = refs[:4], refs[4:8], refs[8:]
    for which in range(2):
        total_ref = totals[which]
        total_ref[...] = plus(ins[2 * which][...], ins[2 * which + 1][...])
        size = total_ref.shape[0] // 2
        keep, sent = halves_of(total_ref, 0, size, bits_ref[ORDERS[which][1]])
        outs[2 * which][...] = keep
        outs[2 * which + 1][...] = sent


def both_kernel(bits_ref, *refs):
    for which in range(2):
        refs[4 + which][...] = plus(refs[2 * which][...], refs[2 * which + 1][...])


def put(out_ref, base, own, other, bit):
    size = own.shape[0]
    out_ref[pl.ds(pl.multiple_of(base + bit * size, 16), size), :] = own.astype(out_ref.dtype)
    out_ref[pl.ds(pl.multiple_of(base + (1 - bit) * size, 16), size), :] = other.astype(out_ref.dtype)


def grow_kernel(bits_ref, *refs):
    for which in range(2):
        put(refs[4 + which], 0, refs[2 * which][...], refs[2 * which + 1][...], bits_ref[ORDERS[which][1]])


def whole_kernel(bits_ref, *refs):
    ins, (*out_refs, total_ref) = refs[:4], refs[4:]
    part = total_ref.shape[0] // 2
    for which in range(2):
        put(total_ref, which * part, ins[2 * which][...], ins[2 * which + 1][...], bits_ref[ORDERS[which][0]])
    base = 0
    for out_ref in out_refs:
        out_ref[...] = total_ref[base : base + out_ref.shape[0], :].astype(F32)
        base += out_ref.shape[0]


def step_call(kernel, bits, arrays, outs, scratch, name):
    vmem = pl.BlockSpec(memory_space=pltpu.VMEM)
    return pl.pallas_call(
        kernel,
        out_shape=outs,
        in_specs=[pl.BlockSpec(memory_space=pltpu.SMEM)] + [vmem] * len(arrays),
        out_specs=[vmem] * len(outs),
        scratch_shapes=scratch,
        compiler_params=params(12, 0),
        cost_estimate=cost(1),
        name=name,
    )(bits, *arrays)


def dp_chain(pieces, sizes):
    bits = axis_bits()
    masks = dp_masks()
    rows, width = pieces[0].shape
    quarter, eighth = shaped((rows // 4, width), BF), shaped((rows // 8, width), BF)
    rest = [[axis for axis in range(len(masks)) if axis not in order] for order in ORDERS]

    def send(a, b, axes):
        return [swap(array, "dp", masks[axis]) for array, axis in zip((a, b), axes)]

    a, a_sent, b, b_sent = step_call(
        split_kernel, bits, placed(pieces), [quarter] * 4, [pltpu.VMEM((rows, width), BF)], "dp_split"
    )
    a_got, b_got = yield send(a_sent, b_sent, [ORDERS[0][0], ORDERS[1][0]])
    a, a_sent, b, b_sent = step_call(
        again_kernel, bits, [a, a_got, b, b_got], [eighth] * 4,
        [pltpu.VMEM((rows // 4, width), BF)] * 2, "dp_again",
    )
    a_got, b_got = yield send(a_sent, b_sent, [ORDERS[0][1], ORDERS[1][1]])
    a, b = step_call(both_kernel, bits, [a, a_got, b, b_got], [eighth] * 2, [], "dp_both")
    for axes in zip(*rest):
        a_got, b_got = yield send(a, b, axes)
        a, b = step_call(both_kernel, bits, [a, a_got, b, b_got], [eighth] * 2, [], "dp_both")
    a_got, b_got = yield send(a, b, [ORDERS[0][1], ORDERS[1][1]])
    a, b = step_call(grow_kernel, bits, [a, a_got, b, b_got], [quarter] * 2, [], "dp_grow")
    a_got, b_got = yield send(a, b, [ORDERS[0][0], ORDERS[1][0]])
    return step_call(
        whole_kernel, bits, [a, a_got, b, b_got],
        [shaped((size, width), F32) for size in sizes], [pltpu.VMEM((rows, width), BF)], "dp_whole",
    )


class Chain:
    def __init__(self, steps):
        self.steps = steps
        self.done = None
        self.got = next(self.steps)

    def go_on(self):
        try:
            self.got = self.steps.send(self.got)
        except StopIteration as stop:
            self.done, self.got = stop.value, []


def together(*chains):
    flat = list(lax.optimization_barrier(tuple(item for chain in chains for item in chain.got)))
    for chain in chains:
        chain.got, flat = flat[: len(chain.got)], flat[len(chain.got) :]


def small_chain(held, sent, keep, own_rows):
    (got,) = yield [swap(sent, "mp", 1)]
    held = held + got
    sent = jnp.concatenate([held[keep + own_rows :], held[own_rows : keep + own_rows]], axis=0)
    (got,) = yield [swap(sent, "mp", 2)]
    held = held[: keep + own_rows] + got
    masks = dp_masks()
    for shift in masks[:-1]:
        (got,) = yield [swap(held, "dp", shift)]
        held = held + got
    (got,) = yield [swap(held, "dp", masks[-1])]
    return held, got


def collect_kernel(ids_ref, sums2_ref, sums1_ref, tokens_ref, table_ref, *refs):
    upb_refs, joint_refs, (out_ref, sent_ref) = refs[:2], refs[2:6], refs[6:]
    upb_lines = [upb_refs[1][8:16, :], upb_refs[1][0:8, :], upb_refs[0][8:16, :], upb_refs[0][0:8, :]]
    out_ref[...] = jnp.zeros_like(out_ref)
    sent_ref[...] = jnp.zeros_like(sent_ref)
    table = table_ref[...]

    def total(values):
        return jnp.sum(values, axis=0, keepdims=True)

    lines = [total(sums2_ref[8 * i : 8 * i + 8, :]) for i in range(6)]
    lines += [total(sums1_ref[8 * i : 8 * i + 8, :]) for i in range(2)]
    images = [total(tokens_ref[i]) for i in range(tokens_ref.shape[0])]
    for group in range(GROUPS):
        found = jnp.zeros_like(images[0])
        for at, values in enumerate(images):
            found = found + jnp.where(ids_ref[at] == group, values, 0.0)
        lines.append(found)
    for at, values in enumerate(lines):
        out_ref[8 + at : 9 + at, :] = values
        sent_ref[8 + at : 9 + at, :] = values
    hidden = upb_refs[0].shape[1]
    for which in range(4):
        ref = out_ref if which % 2 == 0 else sent_ref
        base = 0 if which < 2 else 24
        ref[base : base + 1, :hidden] = total(upb_lines[which])
        joint = total(joint_refs[which][...])
        ref[base + 1 : base + 2, : joint.shape[1]] = joint
        per = table.shape[0] // (out_ref.shape[1] // LANES)
        own = per // 4
        for chunk in range(out_ref.shape[1] // LANES):
            ref[base + 2 : base + 2 + own, chunk * LANES : (chunk + 1) * LANES] = table[
                chunk * per + which * own : chunk * per + (which + 1) * own, :
            ]


def collect(ids, sums2, sums1, tokens, tables, upbs, joints):
    width = sums2.shape[1]
    vmem = pl.BlockSpec(memory_space=pltpu.VMEM)
    return pl.pallas_call(
        collect_kernel,
        out_shape=(shaped((32, width), F32), shaped((32, width), F32)),
        in_specs=[pl.BlockSpec(memory_space=pltpu.SMEM)] + [vmem] * 10,
        out_specs=(vmem, vmem),
        cost_estimate=cost(1),
        name="collect",
    )(ids, *placed([sums2, sums1, tokens, *tables, *upbs, *joints], [sums1, tokens, *tables]))


def emit_kernel(held_ref, got_ref, *outs):
    own = outs[9].shape[0]
    value = held_ref[...] + got_ref[...]
    for at in range(8):
        outs[at][...] = value[8 + at : 9 + at, :].reshape(-1)
    outs[8][...] = value[16:24, :]
    outs[9][...] = value[1:2, :own].reshape(-1)
    outs[10][...] = value[1:2, 2 * own : 3 * own].reshape(-1)
    outs[11][...] = value[2 : 2 + outs[11].shape[0], : outs[11].shape[1]]
    outs[12][...] = value[0:1, : outs[12].shape[0]].reshape(-1)


def emit(held, got, own, table_shape, hidden):
    width = held.shape[1]
    return pl.pallas_call(
        emit_kernel,
        out_shape=[shaped((width,), F32)] * 8
        + [
            shaped((GROUPS, width), F32),
            shaped((own,), F32),
            shaped((own,), F32),
            shaped(table_shape, F32),
            shaped((hidden,), F32),
        ],
        cost_estimate=cost(1),
        name="emit",
    )(held, got)


def local(
    patches, dataset_id, patch_masks, mask_tokens, key_mask, bias_index, norm1_gain, norm1_shift,
    qkv_weight, query_bias, value_bias, bias_table, out_weight, out_bias, gamma_attn, norm2_gain,
    norm2_shift, up_weight, up_bias, down_weight, down_bias, gamma_mlp, cotangent,
):
    rows, width = patches.shape
    images = rows // SEQ
    place = lax.axis_index("mp")
    own = qkv_weight.shape[2]
    own_heads = own // HEAD
    table_rows = bias_table.shape[0]
    chunks = width // LANES
    hidden = up_weight.shape[1]

    ids = lax.dynamic_slice_in_dim(dataset_id, place * images, images, 0)
    keys_here = lax.dynamic_slice_in_dim(key_mask, place * images, images, 0)
    mask = jnp.where(keys_here > 0, 0.0, -1e30).astype(F32)[:, :, None]
    sel_table = patch_masks.astype(F32)[:, :, None]
    images3 = patches.reshape(images, SEQ, width)
    cot3 = cotangent.reshape(images, SEQ, width)
    index = bias_index.T
    mix = (ids, images3, sel_table, mask_tokens)

    parity = lax.axis_index("dp") & 1
    side = parity.reshape(1)
    qkv_own = qkv_weight.transpose(1, 2, 0).reshape(3 * own, width)
    small, attn_half, down_half, pack0 = prepare(
        side, qkv_own, out_weight, down_weight, query_bias, value_bias, up_bias, bias_table.T
    )
    small0, small1 = (small, 0), (swap(small, "mp", 1), 0)
    attn_p2 = swap(attn_half, "mp", 2)
    down_p2 = swap(down_half, "mp", 2)
    pack1 = swap(pack0, "mp", 1)
    bias_near = position_bias([small0, small1], 2 * own_heads, index)
    up2 = swap(pinned(up_weight, bias_near), "mp", 2)
    up1, down1 = swap(up_weight, "mp", 1), swap(down_weight, "mp", 1)

    norm1 = [norm1_gain, norm1_shift]
    x1, j0, probs0, c0, part = attend(
        mix, norm1, qkv_own, (out_weight, 0), small0, bias_near, 0, mask
    )
    part, attn_p2 = lax.optimization_barrier((part, attn_p2))
    attn_q2 = swap(attn_p2, "dp", 1)
    attn_p3 = swap(attn_p2, "mp", 1)
    small2, small3 = (attn_p2, 2 * own // SMALL_ROWS), (attn_p3, 2 * own // SMALL_ROWS)
    j1, probs1, c1, part = attend(mix, norm1, pack1, (pack1, 3), small1, bias_near, 1, mask, x1, part)
    part, index = lax.optimization_barrier((part, index))
    bias_far = position_bias([small2, small3], 2 * own_heads, index)
    part, bias_far, attn_q2, down_p2 = lax.optimization_barrier((part, bias_far, attn_q2, down_p2))
    attn_q3 = swap(attn_q2, "mp", 1)
    down_q2 = swap(down_p2, "dp", 1)
    down_p3 = swap(down_p2, "mp", 1)
    j2, probs2, c2, part, pack2 = attend(
        mix, norm1, attn_p2, attn_q2, small2, bias_far, 0, mask, x1, part, side
    )
    j3, probs3, c3, attn_value, middle, normed2, pack3 = attend(
        mix, [norm2_gain, norm2_shift], attn_p3, attn_q3, small3, bias_far, 1, mask, x1, part, side,
        [out_bias, gamma_attn],
    )

    x2 = normed2.reshape(rows, width)
    x2, up2, down_q2 = lax.optimization_barrier((x2, up2, down_q2))
    up3 = swap(up2, "mp", 1)
    down_q3 = swap(down_q2, "mp", 1)
    value, grad2, m3, m2, upb32 = mlp(
        x2, cotangent, gamma_mlp, [(up3, down_p3, down_q3, small3), (up2, down_p2, down_q2, small2)],
        None, side,
    )
    mlp_far = plus(m2, swap(m3, "mp", 1))
    x2, mlp_far = lax.optimization_barrier((x2, mlp_far))
    mr2 = swap(mlp_far, "mp", 2)
    value, grad2, m1, m0, upb10 = mlp(
        x2, cotangent, gamma_mlp, [(up1, down1, small1), (up_weight, down_weight, small0)],
        (value, grad2), side,
    )

    shape3 = (images, SEQ, width)
    output, grad_middle, grad_attn, sums2 = middle_back(
        value.reshape(shape3), grad2.reshape(shape3), middle, attn_value, cot3,
        [down_bias, gamma_mlp, gamma_attn, norm2_gain],
    )

    mr1 = [swap(m1[:width], "mp", 1), swap(m1[width:], "mp", 1)]
    grad_attn, *mr1 = lax.optimization_barrier((grad_attn, *mr1))
    g1, js1, g3, js3, total13, carried = attend_back(
        ids, x1, grad_attn,
        [(j1, probs1, c1, pack1, 0, pack1, 3), (j3, probs3, c3, pack3, 0, pack3, 3)], None, None,
    )
    mlp_sum = [
        (own.astype(F32) + near.astype(F32) + far.astype(F32)).astype(BF)
        for own, near, far in zip((m0[:width], m0[width:]), mr1, (mr2[:width], mr2[width:]))
    ]
    carried, *mlp_sum = lax.optimization_barrier((carried, *mlp_sum))
    up_sum, down_sum = lax.psum(tuple(mlp_sum), "dp")
    r3 = swap(g3, "mp", 1)
    g2, js2, total2, carried = attend_back(
        ids, x1, grad_attn, [(j2, probs2, c2, pack2, 0, pack2, 3)], carried, None
    )
    far = plus(g2, r3)
    carried, far, g1 = lax.optimization_barrier((carried, far, g1))
    r1 = swap(g1, "mp", 1)
    r2 = swap(far, "mp", 2)
    g0, js0, total0, patch_grad, sums1, token_images = attend_back(
        ids, x1, grad_attn, [(j0, probs0, c0, qkv_own, 0, out_weight, 0)], carried,
        (images3, sel_table, mask_tokens, grad_middle, norm1_gain),
    )
    totals = [(total0, 0), (total13, 0), (total2, 0), (total13, 1)]
    blocks = SEQ // TABLE_ROWS
    table = table_sums(totals, index, chunks, 0, blocks)
    held, sent = collect(
        ids, sums2, sums1, token_images, [table], [upb32, upb10], [js0, js1, js2, js3]
    )
    g0, r1, r2, sent = lax.optimization_barrier((g0, r1, r2, sent))
    tail = Chain(dp_chain([g0, r1, r2], [3 * own, own]))
    small = Chain(small_chain(held, sent, 16, 8))
    joint = 0
    while tail.done is None or small.done is None:
        going = [chain for chain in (tail, small) if chain.done is None]
        joint += 1
        if joint == 4:
            going[0].got[0], up_sum, down_sum = lax.optimization_barrier(
                (going[0].got[0], up_sum, down_sum)
            )
        together(*going)
        for chain in going:
            chain.go_on()
    qkv_sum, out_sum = tail.done
    up_sum, down_sum = up_sum.astype(F32), down_sum.astype(F32)
    (
        gamma_mlp_grad, down_bias_grad, gain2_grad, shift2_grad, gamma_attn_grad, out_bias_grad,
        gain1_grad, shift1_grad, token_grad, qb_grad, vb_grad, table_grad, upb_grad,
    ) = emit(*small.done, own, (own_heads, table_rows), hidden)

    return (
        output.reshape(rows, width),
        patch_grad.reshape(rows, width),
        token_grad,
        gain1_grad,
        shift1_grad,
        qkv_sum.reshape(3, own, width).transpose(2, 0, 1),
        qb_grad,
        vb_grad,
        table_grad.T,
        out_sum,
        out_bias_grad,
        gamma_attn_grad,
        gain2_grad,
        shift2_grad,
        up_sum,
        upb_grad,
        down_sum,
        down_bias_grad,
        gamma_mlp_grad,
    )


def solution(mesh):
    return jax.shard_map(
        local,
        mesh=mesh,
        in_specs=(
            P(("dp", "mp"), None), P("dp"), P(), P(), P("dp", None), P(), P(), P(),
            P(None, None, "mp"), P("mp"), P("mp"), P(None, "mp"), P("mp", None), P(), P(), P(), P(),
            P(None, "mp"), P("mp"), P("mp", None), P(), P(), P(("dp", "mp"), None),
        ),
        out_specs=(
            P(("dp", "mp"), None), P(("dp", "mp"), None), P(), P(), P(), P(None, None, "mp"),
            P("mp"), P("mp"), P(None, "mp"), P("mp", None), P(), P(), P(), P(), P(None, "mp"),
            P("mp"), P("mp", None), P(), P(),
        ),
        check_vma=False,
    )
```
